128 devices in a mesh: ka: 32 (over y, z, core), ga: 4 (over x).
Axes of the slice: x: 4, y: 4, z: 4, core: 2. Of those that a mesh axis runs over, the one named last changes fastest.
Arguments:
- x_dens: bfloat16 [128, 64, 1500], P('ka', None, 'ga'), may hold values from -6 to 6
- y_dens: bfloat16 [128, 64, 1500], P('ka', None, 'ga'), may hold values from -0.15625 to 0.15625
- p_dens: bfloat16 [128, 64, 1500], P('ka', None, 'ga'), may hold values from -1 to 1
- coulomb: float32 [1500], P('ga'), may hold values from 0.1 to 2
- screened: bfloat16 [64, 1500, 1500], P('ka', 'ga'), may hold values from -0.15625 to 0.15625
- pairs: int32 [512, 3], P('ka'), may hold values from 0 to 127, as said below
- q_slot: int32 [64], replicated, may hold values from 0 to 63, as said below
Outputs:
- blocks: float32 [512, 4096], P('ka')
- mirrored: float32 [128, 4096], P('ka')
The draws below stay inside these ranges and needn't reach their ends.
Inputs may be any that keep to these rules, and one draw needn't show every extreme that they name: `pairs`: column 0 of the rows held by index d of ka lies in d * 4 to (d + 1) * 4 - 1; column 1 is any k-point; column 2 is a momentum transfer below 64. Among one index's 16 rows at most 2 have a second k-point held by one same index, and this is reached; at most 2 have q_slot[q] // 2 equal to one same value, and this is reached. `q_slot`: A permutation of the slots; slot s of screened is held by index s // 2 of ka.
All inputs are finite; a program needn't handle non-finite values.
Results may differ from the reference program's by a relative error of at most 0.0014.
Values may be sent and summed in bfloat16 or wider, within the bound.
No kernel may reach another device: no remote copies, remote signals or barrier semaphores. Data moves between devices by JAX's collectives and lax.ppermute only.
A program may use at most 192 MiB of HBM per device.

```python
import math
import jax
import jax.numpy as jnp
from jax import lax

NT = 64
NG = 1500
K_DEV = 4
PAIR_DEV = 16
QS = 2
CAPQ = 2
CAPK = 2
K_ALL = 128
NQ = 64
PAIRS = 512
N_KA = 32


def shared_slots(key):
    return jax.random.permutation(jax.random.fold_in(key, 7), NQ).astype(jnp.int32)


def draw_q_slot(key, part):
    return shared_slots(key)


def draw_pairs(key, part):
    slot_of = shared_slots(key)
    inverse = jnp.zeros((NQ,), jnp.int32).at[slot_of].set(jnp.arange(NQ, dtype=jnp.int32))
    popular = jax.random.permutation(jax.random.fold_in(key, 9), N_KA) < max(1, N_KA // 8)

    def one_block(index):
        block_key = jax.random.fold_in(key, 100 + index)
        keys = jax.random.split(block_key, 7)
        firsts = index * K_DEV + jax.random.randint(keys[0], (PAIR_DEV,), 0, K_DEV)
        k_owners = jax.random.permutation(keys[1], N_KA)[jnp.arange(PAIR_DEV) // CAPK]
        k_owners = k_owners[jax.random.permutation(keys[2], PAIR_DEV)]
        seconds = k_owners * K_DEV + jax.random.randint(keys[3], (PAIR_DEV,), 0, K_DEV)
        scores = jax.random.randint(keys[4], (N_KA,), 0, 1000) + 800 * popular.astype(jnp.int32)
        scores = scores * N_KA + jnp.arange(N_KA, dtype=jnp.int32)
        ranking = jnp.argsort(-scores, stable=True).astype(jnp.int32)
        q_owners = ranking[jnp.arange(PAIR_DEV) // CAPQ]
        q_owners = q_owners[jax.random.permutation(keys[5], PAIR_DEV)]
        slots = q_owners * QS + jax.random.randint(keys[6], (PAIR_DEV,), 0, QS)
        transfers = inverse[slots]
        return jnp.stack([firsts, seconds, transfers], axis=1).astype(jnp.int32)
    return jax.vmap(one_block)(jnp.arange(N_KA, dtype=jnp.int32)).reshape(PAIRS, 3)


def block_levels(stream_key, dims, cuts, smallest, largest):
    level = 1.0
    for dim, shards_of in cuts:
        draws = jax.random.uniform(jax.random.fold_in(jax.random.fold_in(stream_key, 6), dim), (shards_of,), jnp.float32, smallest / len(cuts), largest / len(cuts))
        level = level * jnp.repeat(jnp.exp(draws), dims[dim] // shards_of).reshape((-1,) + (1,) * (len(dims) - 1 - dim))
    return level


def gaussian(own_key, shape, scale, reach, pieces=(), held_as=jnp.bfloat16):
    entries = jax.random.normal(own_key, shape, jnp.float32) * scale
    if len(pieces) > 0:
        entries = block_levels(own_key, shape, pieces, -0.22, 0.18) * entries
    return jnp.clip(entries, min=-reach, max=reach).astype(held_as)


def setup_inputs(seed: int = 0) -> dict:
    arg_keys = jax.random.split(jax.random.key(seed), 8)
    x_dens = gaussian(arg_keys[0], (K_ALL, NT, NG), 1.0, 6.0, ((0, 32), (2, 4)))
    y_dens = gaussian(arg_keys[1], (K_ALL, NT, NG), NG ** -0.5, 0.15625, ((0, 32), (2, 4)))
    p_dens = gaussian(arg_keys[2], (K_ALL, NT, NG), 0.16, 1.0, ((0, 32), (2, 4)))
    coulomb = jnp.clip(jnp.exp(math.log(2.0) - 2.9957323 * jax.random.uniform(arg_keys[3], (NG,), jnp.float32) ** block_levels(arg_keys[3], (NG,), ((0, 4),), -0.2, 0.2)), 0.1, 2.0)
    screened = gaussian(arg_keys[4], (NQ, NG, NG), NG ** -0.5, 0.15625, ((0, 32), (1, 4)))
    pairs = draw_pairs(jax.random.fold_in(arg_keys[7], 71), 0)
    q_slot = draw_q_slot(jax.random.fold_in(arg_keys[7], 71), 0)
    return {"x_dens": x_dens, "y_dens": y_dens, "p_dens": p_dens, "coulomb": coulomb, "screened": screened, "pairs": pairs, "q_slot": q_slot}


def reference(x_dens, y_dens, p_dens, coulomb, screened, pairs, q_slot):
    def one_pair(entry):
        k_index = entry[0]
        partner = entry[1]
        q_index = entry[2]
        w_matrix = screened[q_slot[q_index]]
        half_rows = jnp.dot(x_dens[k_index], w_matrix, preferred_element_type=jnp.float32).astype(jnp.bfloat16)
        direct = jnp.dot(half_rows, y_dens[partner].T, preferred_element_type=jnp.float32)
        weighted = p_dens[k_index].astype(jnp.float32) * coulomb[None, :]
        exchange_term = jnp.dot(weighted, p_dens[partner].astype(jnp.float32).T, precision=lax.Precision.HIGHEST)
        return 2.0 * exchange_term - direct

    kernel_blocks = lax.map(one_pair, pairs)
    flipped = jnp.transpose(kernel_blocks, (0, 2, 1)).reshape(PAIRS, NT * NT)
    mirrored = jax.ops.segment_sum(flipped, pairs[:, 1].astype(jnp.int32), num_segments=K_DEV * N_KA)
    return kernel_blocks.reshape(PAIRS, NT * NT), mirrored
```

```python
import jax
import jax.numpy as jnp
from jax import lax
from jax.experimental import pallas as pl
from jax.experimental.pallas import tpu as pltpu
from jax.sharding import PartitionSpec as P

CAP = 2
QW = 384
CH = 8
F32 = jnp.float32
BF16 = jnp.bfloat16
NT_DIMS = (((1,), (1,)), ((), ()))


def rank_in_group(owners):
    n = owners.shape[-1]
    same = owners[..., :, None] == owners[..., None, :]
    before = jnp.arange(n)[:, None] > jnp.arange(n)[None, :]
    return jnp.sum(jnp.logical_and(same, before).astype(jnp.int32), axis=-1)


def widen(v):
    return jnp.pad(v, ((0, 0),) * (v.ndim - 1) + ((0, QW - v.shape[-1]),))


def flat_tiles(tmp, rows):
    even = tmp[pl.ds(0, rows // 2, stride=2), :]
    odd = tmp[pl.ds(1, rows // 2, stride=2), :]
    return jnp.concatenate([even, odd], axis=1)


def block_kernel(tab, own, big, wk, pk, cw, out, xs, ys, p2, whl, tmp, where_, sx, sy, sp):
    nslot = tab.shape[1]
    npair = own.shape[1]
    nk = pk.shape[0]
    nt = pk.shape[1]

    def p_copy(j):
        return pltpu.make_async_copy(big.at[own[1, j], :, pl.ds(4 * QW, QW)], p2.at[j], sp.at[j])

    def x_copy(k, pos):
        return pltpu.make_async_copy(big.at[k, :, pl.ds(0, 2 * QW)], xs.at[pos], sx.at[pos])

    def y_copy(k, pos):
        return pltpu.make_async_copy(big.at[k, :, pl.ds(2 * QW, 2 * QW)], ys.at[pos], sy.at[pos])

    for j in range(npair):
        p_copy(j).start()

    def clear(i, carry):
        where_[i] = nslot
        return carry

    lax.fori_loop(0, where_.shape[0], clear, 0)

    def count(t, n):
        return n + jnp.where((tab[0, t] == 1) & (tab[3, t] == 0), 1, 0)

    n_first = lax.fori_loop(0, nslot, count, 0)
    chunks_first = (n_first + CH - 1) // CH

    def place(t, carry):
        c0, c1 = carry
        first = tab[3, t] == 0
        used = tab[0, t] == 1
        pos = jnp.where(first, c0, chunks_first * CH + c1)

        @pl.when(used)
        def _():
            where_[pos] = t
            x_copy(tab[1, t], pos).start()
            y_copy(tab[2, t], pos).start()

        add = jnp.where(used, 1, 0)
        return c0 + jnp.where(first, add, 0), c1 + jnp.where(first, 0, add)

    _, n_second = lax.fori_loop(0, nslot, place, (0, 0))
    chunks = chunks_first + (n_second + CH - 1) // CH

    out[...] = jnp.zeros_like(out)
    for k in range(nk):
        w = pk[k].astype(F32) * cw[...]
        hi = w.astype(BF16)
        lo = (w - hi.astype(F32)).astype(BF16)
        whl[k, :nt, :] = hi
        whl[k, nt:, :] = lo
    for first in range(0, npair, CH):
        for i in range(CH):
            j = first + i
            p_copy(j).wait()
            e = lax.dot_general(whl[own[0, j]], p2[j], NT_DIMS, preferred_element_type=F32)
            tmp[i * nt : (i + 1) * nt, :] = 2.0 * (e[:nt] + e[nt:])
        z = flat_tiles(tmp, CH * nt)
        for i in range(CH):
            for q in range(4):
                row = i * (nt // 2) + q * 8
                out[q, nslot + first + i] = z[row : row + 8]

    def chunk(c, carry):
        for i in range(CH):
            pos = c * CH + i
            t = where_[pos]

            @pl.when(t < nslot)
            def _():
                x_copy(0, pos).wait()
                y_copy(0, pos).wait()

        slot = jnp.where(c < chunks_first, 0, 1)
        x = xs[pl.ds(c * CH, CH)].reshape(CH * nt, 2 * QW)
        u = jnp.dot(x, wk[slot], preferred_element_type=F32)
        hi = u.astype(BF16)
        lo = (u - hi.astype(F32)).astype(BF16)
        for i in range(CH):
            r = slice(i * nt, (i + 1) * nt)
            both = jnp.concatenate([hi[r], lo[r]], axis=0)
            d = lax.dot_general(both, ys[c * CH + i], NT_DIMS, preferred_element_type=F32)
            tmp[r, :] = d[:nt] + d[nt:]
        z = flat_tiles(tmp, CH * nt)
        for i in range(CH):
            t = where_[c * CH + i]

            @pl.when(t < nslot)
            def _():
                for q in range(4):
                    row = i * (nt // 2) + q * 8
                    out[q, t] = z[row : row + 8]

        return carry

    lax.fori_loop(0, chunks, chunk, 0)


def combine_kernel(own, e, d, blocks, send):
    send[...] = jnp.zeros_like(send)
    for j in range(e.shape[0]):
        v = e[j] - d[own[2, j]]
        blocks[j] = v
        send[own[3, j]] = v


def mirror_kernel(tab, got, b, out):
    n = b.shape[0]
    out[:n] = b[...]
    out[n:] = jnp.zeros((out.shape[0] - n, *out.shape[1:]), F32)
    for t in range(got.shape[0]):

        @pl.when(tab[4, t] == 1)
        def _():
            k = n + tab[5, t]
            out[k] = out[k] + got[t]


def in_vmem(count):
    return [pl.BlockSpec(memory_space=pltpu.VMEM)] * count


SMEM = pl.BlockSpec(memory_space=pltpu.SMEM)


def per_device(x, y, p, coulomb, w, pairs, q_slot):
    n_ka = lax.axis_size("ka")
    me = lax.axis_index("ka")
    a = lax.axis_index("ga")
    nk, nt, gl = x.shape
    qs = w.shape[0]
    npair = pairs.shape[0]
    nslot = n_ka * CAP

    with jax.named_scope("pack"):
        x_far = lax.ppermute(x, "ga", [(0, 1), (1, 0), (2, 3), (3, 2)])
        y_far = lax.ppermute(y, "ga", [(0, 3), (3, 0), (1, 2), (2, 1)])
        payload = jnp.concatenate([widen(v) for v in (x, x_far, y, y_far, p)], axis=2)
    with jax.named_scope("spread"):
        big = lax.all_gather(payload, "ka", axis=0, tiled=True)

    with jax.named_scope("weights"):
        cols = jnp.stack([w[:, :, i * gl : (i + 1) * gl] for i in range(4)])
        cols = jnp.pad(cols, ((0, 0), (0, 0), (0, QW - gl), (0, QW - gl)))

        def columns_of(b):
            return jnp.concatenate(
                [
                    lax.dynamic_index_in_dim(cols, b, 0, keepdims=False),
                    lax.dynamic_index_in_dim(cols, 3 - b, 0, keepdims=False),
                ],
                axis=2,
            )

        near = columns_of(a)
        far = lax.ppermute(
            columns_of(jnp.bitwise_xor(a, 1)), "ga", [(0, 1), (1, 0), (2, 3), (3, 2)]
        )
        wk = jnp.concatenate([near, far], axis=1)

    with jax.named_scope("tables"):
        every = lax.all_gather(pairs, "ka", axis=0, tiled=True).reshape(n_ka, npair, 3)

        def routes(rows):
            slot = jnp.sum(
                jnp.where(
                    rows[..., 2, None] == jnp.arange(q_slot.shape[0]), q_slot, 0
                ),
                axis=-1,
            )
            q_owner = slot // qs
            k_owner = rows[..., 1] // nk
            return slot % qs, q_owner, rank_in_group(q_owner), k_owner, rank_in_group(k_owner)

        local, q_owner, q_rank, k_owner, k_rank = routes(every)
        ranks = jnp.arange(CAP)
        hot_q = (q_owner == me)[..., None] & (q_rank[..., None] == ranks)
        hot_k = (k_owner == me)[..., None] & (k_rank[..., None] == ranks)

        def pick(hot, v):
            return jnp.sum(jnp.where(hot, v[..., None], 0), axis=1).reshape(nslot)

        ones = jnp.ones_like(local)
        tab = jnp.stack(
            [
                pick(hot_q, ones),
                pick(hot_q, every[..., 0]),
                pick(hot_q, every[..., 1]),
                pick(hot_q, local),
                pick(hot_k, ones),
                pick(hot_k, every[..., 1] - me * nk),
            ]
        )
        _, o1, r1, o2, r2 = routes(pairs)
        own = jnp.stack([pairs[:, 0] - me * nk, pairs[:, 1], o1 * CAP + r1, o2 * CAP + r2])

    cw = jnp.pad(coulomb[None], ((0, 0), (0, QW - gl)))
    npos = nslot + qs * CH
    part = pl.pallas_call(
        block_kernel,
        out_shape=jax.ShapeDtypeStruct((4, nslot + npair, 8, 128), F32),
        in_specs=[SMEM, SMEM, pl.BlockSpec(memory_space=pl.ANY), *in_vmem(3)],
        out_specs=pl.BlockSpec(memory_space=pltpu.VMEM),
        scratch_shapes=[
            pltpu.VMEM((npos, nt, 2 * QW), BF16),
            pltpu.VMEM((npos, nt, 2 * QW), BF16),
            pltpu.VMEM((npair, nt, QW), BF16),
            pltpu.VMEM((nk, 2 * nt, QW), BF16),
            pltpu.VMEM((CH * nt, nt), F32),
            pltpu.SMEM((npos,), jnp.int32),
            pltpu.SemaphoreType.DMA((npos,)),
            pltpu.SemaphoreType.DMA((npos,)),
            pltpu.SemaphoreType.DMA((npair,)),
        ],
        compiler_params=pltpu.CompilerParams(vmem_limit_bytes=48 * 1024 * 1024),
        name="pair_blocks",
    )(tab, own, big, wk, widen(p), cw)

    with jax.named_scope("sum_quarters"):
        quarter = jnp.sum(lax.all_to_all(part, "ga", 0, 0, tiled=True), axis=0)
    with jax.named_scope("to_pairs"):
        direct = lax.all_to_all(quarter[:nslot], "ka", 0, 0, tiled=True)
    blocks, send = pl.pallas_call(
        combine_kernel,
        out_shape=(
            jax.ShapeDtypeStruct((npair, 8, 128), F32),
            jax.ShapeDtypeStruct((nslot, 8, 128), F32),
        ),
        in_specs=[SMEM, *in_vmem(2)],
        out_specs=tuple(in_vmem(2)),
        name="combine",
    )(own, quarter[nslot:], direct)
    with jax.named_scope("to_seconds"):
        got = lax.all_to_all(send, "ka", 0, 0, tiled=True)
    both = pl.pallas_call(
        mirror_kernel,
        out_shape=jax.ShapeDtypeStruct((npair + nk, 8, 128), F32),
        in_specs=[SMEM, *in_vmem(2)],
        out_specs=pl.BlockSpec(memory_space=pltpu.VMEM),
        name="mirror",
    )(tab, got, blocks)
    with jax.named_scope("copies"):
        whole = lax.all_gather(both, "ga", axis=0)
        whole = jnp.transpose(whole, (1, 0, 2, 3)).reshape(npair + nk, nt, nt)
        mirrored = jnp.transpose(whole[npair:], (0, 2, 1)).reshape(nk, nt * nt)
    return whole[:npair].reshape(npair, nt * nt), mirrored


def solution(mesh):
    in_specs = (
        P("ka", None, "ga"),
        P("ka", None, "ga"),
        P("ka", None, "ga"),
        P("ga"),
        P("ka", "ga", None),
        P("ka", None),
        P(),
    )
    out_specs = (P("ka", None), P("ka", None))
    return jax.shard_map(
        per_device, mesh=mesh, in_specs=in_specs, out_specs=out_specs, check_vma=False
    )
```

```python
import jax
import jax.numpy as jnp
from jax import lax
from jax.experimental import pallas as pl
from jax.experimental.pallas import tpu as pltpu
from jax.sharding import PartitionSpec as P

CAP = 2
QW = 384
CH = 8
F32 = jnp.float32
BF16 = jnp.bfloat16
NT_DIMS = (((1,), (1,)), ((), ()))


def rank_in_group(owners):
    n = owners.shape[-1]
    same = owners[..., :, None] == owners[..., None, :]
    before = jnp.arange(n)[:, None] > jnp.arange(n)[None, :]
    return jnp.sum(jnp.logical_and(same, before).astype(jnp.int32), axis=-1)


def widen(v):
    return jnp.pad(v, ((0, 0),) * (v.ndim - 1) + ((0, QW - v.shape[-1]),))


def flat_tiles(tmp, rows):
    even = tmp[pl.ds(0, rows // 2, stride=2), :]
    odd = tmp[pl.ds(1, rows // 2, stride=2), :]
    return jnp.concatenate([even, odd], axis=1)


def direct_kernel(tab, big, wk, out, xs, ys, tmp, where_, sx, sy):
    nslot = tab.shape[1]
    nt = xs.shape[1]
    wide = xs.shape[2]

    def x_copy(k, pos):
        return pltpu.make_async_copy(big.at[k, :, pl.ds(0, wide)], xs.at[pos], sx.at[pos])

    def y_copy(k, pos):
        return pltpu.make_async_copy(big.at[k, :, pl.ds(wide, wide)], ys.at[pos], sy.at[pos])

    def clear(i, carry):
        where_[i] = nslot
        return carry

    lax.fori_loop(0, where_.shape[0], clear, 0)

    def count(t, n):
        return n + jnp.where((tab[0, t] == 1) & (tab[3, t] == 0), 1, 0)

    n_first = lax.fori_loop(0, nslot, count, 0)
    chunks_first = (n_first + CH - 1) // CH

    def place(t, carry):
        c0, c1 = carry
        first = tab[3, t] == 0
        used = tab[0, t] == 1
        pos = jnp.where(first, c0, chunks_first * CH + c1)

        @pl.when(used)
        def _():
            where_[pos] = t
            x_copy(tab[1, t], pos).start()
            y_copy(tab[2, t], pos).start()

        add = jnp.where(used, 1, 0)
        return c0 + jnp.where(first, add, 0), c1 + jnp.where(first, 0, add)

    _, n_second = lax.fori_loop(0, nslot, place, (0, 0))
    chunks = chunks_first + (n_second + CH - 1) // CH
    out[...] = jnp.zeros_like(out)

    def chunk(c, carry):
        for i in range(CH):
            pos = c * CH + i
            t = where_[pos]

            @pl.when(t < nslot)
            def _():
                x_copy(0, pos).wait()
                y_copy(0, pos).wait()

        slot = jnp.where(c < chunks_first, 0, 1)
        x = xs[pl.ds(c * CH, CH)].reshape(CH * nt, wide)
        u = jnp.dot(x, wk[slot], preferred_element_type=F32)
        hi = u.astype(BF16)
        lo = (u - hi.astype(F32)).astype(BF16)
        for i in range(CH):
            r = slice(i * nt, (i + 1) * nt)
            both = jnp.concatenate([hi[r], lo[r]], axis=0)
            d = lax.dot_general(ys[c * CH + i], both, NT_DIMS, preferred_element_type=F32)
            tmp[r, :] = d[:, :nt] + d[:, nt:]
        z = flat_tiles(tmp, CH * nt)
        for i in range(CH):
            t = where_[c * CH + i]

            @pl.when(t < nslot)
            def _():
                for q in range(4):
                    row = i * (nt // 2) + q * 8
                    out[q, t] = z[row : row + 8]

        return carry

    lax.fori_loop(0, chunks, chunk, 0)


def route_kernel(tab, parts, send):
    nk = send.shape[1] - CAP
    send[:, CAP:] = jnp.zeros((send.shape[0], nk, *send.shape[2:]), F32)
    for t in range(tab.shape[1]):
        v = (parts[0, t] + parts[1, t]) + (parts[2, t] + parts[3, t])
        send[t // CAP, t % CAP] = v
        owner = tab[2, t] // nk
        row = CAP + tab[2, t] % nk
        send[owner, row] = send[owner, row] + v


def exchange_kernel(tab, own, big, mine, whi, wlo, cw, out, p1, p2, tot, prod, flat, s1, s2):
    nslot = tab.shape[1]
    npair = own.shape[1]
    nk = tot.shape[0]
    rows = p2.shape[1]
    nt = mine.shape[0] // nk
    wide = p2.shape[2]

    def second(j):
        return pltpu.make_async_copy(big.at[own[1, j]], p2.at[j], s2.at[j])

    def first(t):
        return pltpu.make_async_copy(big.at[tab[6, t]], p1.at[t], s1.at[t])

    for j in range(npair):
        second(j).start()

    def begin(t, carry):
        @pl.when(tab[4, t] == 1)
        def _():
            first(t).start()

        return carry

    lax.fori_loop(0, nslot, begin, 0)
    tot[...] = jnp.zeros_like(tot)
    for j in range(npair):
        second(j).wait()
    b = p2[...].reshape(npair * rows, wide)
    e = lax.dot_general(b, whi[...], NT_DIMS, preferred_element_type=F32)
    e = e + lax.dot_general(b, wlo[...], NT_DIMS, preferred_element_type=F32)
    e = e + e
    for k in range(nk):
        prod[k] = e[:, k * nt : (k + 1) * nt]
    for j in range(npair):
        r = pl.ds(j * rows, rows)
        flat[r, :] = prod[own[0, j], r, :]

    def gather(t, carry):
        @pl.when(tab[4, t] == 1)
        def _():
            first(t).wait()
            k = tab[5, t]
            tot[k] = tot[k] + p1[t].astype(F32)

        return carry

    lax.fori_loop(0, nslot, gather, 0)
    w = tot[...].reshape(nk * rows, wide) * cw[...]
    hi = w.astype(BF16)
    lo = (w - hi.astype(F32)).astype(BF16)
    m = lax.dot_general(
        jnp.concatenate([hi, lo], axis=0), mine[...], NT_DIMS, preferred_element_type=F32
    )
    m = m[: nk * rows] + m[nk * rows :]
    m = m + m
    for k in range(nk):
        flat[pl.ds((npair + k) * rows, rows), :] = m[
            k * rows : (k + 1) * rows, k * nt : (k + 1) * nt
        ]
    z = flat_tiles(flat, (npair + nk) * rows)
    for j in range(npair + nk):
        out[j] = z[8 * j : 8 * j + 8]


def combine_kernel(own, e, got, out):
    nk = got.shape[1] - CAP
    npair = own.shape[1]
    for j in range(npair):
        out[j] = e[j] - got[own[2, j], own[3, j]]
    for k in range(nk):
        out[npair + k] = e[npair + k]
        out[npair + nk + k] = -jnp.sum(got[:, CAP + k], axis=0)


def in_vmem(count):
    return [pl.BlockSpec(memory_space=pltpu.VMEM)] * count


SMEM = pl.BlockSpec(memory_space=pltpu.SMEM)
ANY = pl.BlockSpec(memory_space=pl.ANY)


def per_device(x, y, p, coulomb, w, pairs, q_slot):
    n_ka = lax.axis_size("ka")
    me = lax.axis_index("ka")
    a = lax.axis_index("ga")
    nk, nt, gl = x.shape
    qs = w.shape[0]
    npair = pairs.shape[0]
    nslot = n_ka * CAP

    with jax.named_scope("pack"):
        x_far = lax.ppermute(x, "ga", [(0, 1), (1, 0), (2, 3), (3, 2)])
        y_far = lax.ppermute(y, "ga", [(0, 3), (3, 0), (1, 2), (2, 1)])
        payload = jnp.concatenate([widen(v) for v in (x, x_far, y, y_far)], axis=2)
    with jax.named_scope("spread"):
        big = lax.all_gather(payload, "ka", axis=0, tiled=True)

    with jax.named_scope("exchange_pack"):
        rows = nt // 4
        c1 = lax.reduce_precision(coulomb, 8, 7)
        c2 = lax.reduce_precision(coulomb - c1, 8, 7)
        c3 = coulomb - c1 - c2
        pieces = jnp.pad(jnp.stack([c1, c2, c3]).astype(BF16), ((0, 13), (0, 0)))
        held = jnp.concatenate([p.reshape(nk * nt, gl), pieces], axis=0)
        held = lax.all_gather(widen(held), "ga", axis=1, tiled=True)
        full = held[: nk * nt]
        c_full = jnp.sum(held[nk * nt : nk * nt + 3].astype(F32), axis=0, keepdims=True)
        p_rows = lax.dynamic_slice_in_dim(full.reshape(nk, nt, 4 * QW), a * rows, rows, axis=1)
        p_big = lax.all_gather(p_rows, "ka", axis=0, tiled=True)
        weighted = full.astype(F32) * c_full
        w_hi = lax.reduce_precision(weighted, 8, 7)
        w_lo = (weighted - w_hi).astype(BF16)
        w_hi = w_hi.astype(BF16)

    with jax.named_scope("weights"):
        cols = jnp.stack([w[:, :, i * gl : (i + 1) * gl] for i in range(4)])
        cols = jnp.pad(cols, ((0, 0), (0, 0), (0, QW - gl), (0, QW - gl)))

        def columns_of(b):
            return jnp.concatenate(
                [
                    lax.dynamic_index_in_dim(cols, b, 0, keepdims=False),
                    lax.dynamic_index_in_dim(cols, 3 - b, 0, keepdims=False),
                ],
                axis=2,
            )

        near = columns_of(a)
        far = lax.ppermute(
            columns_of(jnp.bitwise_xor(a, 1)), "ga", [(0, 1), (1, 0), (2, 3), (3, 2)]
        )
        wk = jnp.concatenate([near, far], axis=1)

    with jax.named_scope("tables"):
        every = lax.all_gather(pairs, "ka", axis=0, tiled=True).reshape(n_ka, npair, 3)

        def routes(rows):
            slot = jnp.sum(
                jnp.where(
                    rows[..., 2, None] == jnp.arange(q_slot.shape[0]), q_slot, 0
                ),
                axis=-1,
            )
            q_owner = slot // qs
            k_owner = rows[..., 1] // nk
            return slot % qs, q_owner, rank_in_group(q_owner), k_owner, rank_in_group(k_owner)

        local, q_owner, q_rank, k_owner, k_rank = routes(every)
        ranks = jnp.arange(CAP)
        hot_q = (q_owner == me)[..., None] & (q_rank[..., None] == ranks)
        hot_k = (k_owner == me)[..., None] & (k_rank[..., None] == ranks)

        def pick(hot, v):
            return jnp.sum(jnp.where(hot, v[..., None], 0), axis=1).reshape(nslot)

        ones = jnp.ones_like(local)
        tab = jnp.stack(
            [
                pick(hot_q, ones),
                pick(hot_q, every[..., 0]),
                pick(hot_q, every[..., 1]),
                pick(hot_q, local),
                pick(hot_k, ones),
                pick(hot_k, every[..., 1] - me * nk),
                pick(hot_k, every[..., 0]),
            ]
        )
        _, o1, r1, _, _ = routes(pairs)
        own = jnp.stack([pairs[:, 0] - me * nk, pairs[:, 1], o1, r1])

    npos = nslot + qs * CH
    part = pl.pallas_call(
        direct_kernel,
        out_shape=jax.ShapeDtypeStruct((4, nslot, 8, 128), F32),
        in_specs=[SMEM, ANY, *in_vmem(1)],
        out_specs=pl.BlockSpec(memory_space=pltpu.VMEM),
        scratch_shapes=[
            pltpu.VMEM((npos, nt, 2 * QW), BF16),
            pltpu.VMEM((npos, nt, 2 * QW), BF16),
            pltpu.VMEM((CH * nt, nt), F32),
            pltpu.SMEM((npos,), jnp.int32),
            pltpu.SemaphoreType.DMA((npos,)),
            pltpu.SemaphoreType.DMA((npos,)),
        ],
        compiler_params=pltpu.CompilerParams(vmem_limit_bytes=48 * 1024 * 1024),
        name="direct",
    )(tab, big, wk)
    with jax.named_scope("to_quarters"):
        parts = lax.all_to_all(part, "ga", 0, 0, tiled=True)
    send = pl.pallas_call(
        route_kernel,
        out_shape=jax.ShapeDtypeStruct((n_ka, CAP + nk, 8, 128), F32),
        in_specs=[SMEM, *in_vmem(1)],
        out_specs=pl.BlockSpec(memory_space=pltpu.VMEM),
        name="route",
    )(tab, parts)
    with jax.named_scope("to_holders"):
        got = lax.all_to_all(send, "ka", 0, 0, tiled=True)
    exch = pl.pallas_call(
        exchange_kernel,
        out_shape=jax.ShapeDtypeStruct((npair + nk, 8, 128), F32),
        in_specs=[SMEM, SMEM, ANY, *in_vmem(4)],
        out_specs=pl.BlockSpec(memory_space=pltpu.VMEM),
        scratch_shapes=[
            pltpu.VMEM((nslot, rows, 4 * QW), BF16),
            pltpu.VMEM((npair, rows, 4 * QW), BF16),
            pltpu.VMEM((nk, rows, 4 * QW), F32),
            pltpu.VMEM((nk, npair * rows, nt), F32),
            pltpu.VMEM(((npair + nk) * rows, nt), F32),
            pltpu.SemaphoreType.DMA((nslot,)),
            pltpu.SemaphoreType.DMA((npair,)),
        ],
        compiler_params=pltpu.CompilerParams(vmem_limit_bytes=32 * 1024 * 1024),
        name="exchange",
    )(tab, own, p_big, full, w_hi, w_lo, c_full)
    both = pl.pallas_call(
        combine_kernel,
        out_shape=jax.ShapeDtypeStruct((npair + 2 * nk, 8, 128), F32),
        in_specs=[SMEM, *in_vmem(2)],
        out_specs=pl.BlockSpec(memory_space=pltpu.VMEM),
        name="combine",
    )(own, exch, got)
    with jax.named_scope("copies"):
        whole = lax.all_gather(both, "ga", axis=0)
        whole = jnp.transpose(whole, (1, 0, 2, 3)).reshape(npair + 2 * nk, nt, nt)
        flipped = jnp.transpose(whole[: npair + nk], (0, 2, 1))
        mirrored = flipped[npair:] + whole[npair + nk :]
    return flipped[:npair].reshape(npair, nt * nt), mirrored.reshape(nk, nt * nt)


def solution(mesh):
    in_specs = (
        P("ka", None, "ga"),
        P("ka", None, "ga"),
        P("ka", None, "ga"),
        P("ga"),
        P("ka", "ga", None),
        P("ka", None),
        P(),
    )
    out_specs = (P("ka", None), P("ka", None))
    return jax.shard_map(
        per_device, mesh=mesh, in_specs=in_specs, out_specs=out_specs, check_vma=False
    )
```

```python
import jax
import jax.numpy as jnp
from jax import lax
from jax.experimental import pallas as pl
from jax.experimental.pallas import tpu as pltpu
from jax.sharding import PartitionSpec as P

CAP = 2
QW = 384
CH = 8
F32 = jnp.float32
BF16 = jnp.bfloat16
NT_DIMS = (((1,), (1,)), ((), ()))


def rank_in_group(owners):
    n = owners.shape[-1]
    same = owners[..., :, None] == owners[..., None, :]
    before = jnp.arange(n)[:, None] > jnp.arange(n)[None, :]
    return jnp.sum(jnp.logical_and(same, before).astype(jnp.int32), axis=-1)


def widen(v):
    return jnp.pad(v, ((0, 0),) * (v.ndim - 1) + ((0, QW - v.shape[-1]),))


def flat_tiles(tmp, rows):
    even = tmp[pl.ds(0, rows // 2, stride=2), :]
    odd = tmp[pl.ds(1, rows // 2, stride=2), :]
    return jnp.concatenate([even, odd], axis=1)


def direct_kernel(tab, big, w, send, xs, ys, prod, where_, sx, sy):
    nslot = tab.shape[1]
    half = xs.shape[1]
    nk = send.shape[1] - CAP

    def x_copy(k, pos):
        return pltpu.make_async_copy(big.at[k, pl.ds(0, half)], xs.at[pos], sx.at[pos])

    def y_copy(k, pos):
        return pltpu.make_async_copy(big.at[k, pl.ds(half, half)], ys.at[pos], sy.at[pos])

    def clear(i, carry):
        where_[i] = nslot
        return carry

    lax.fori_loop(0, where_.shape[0], clear, 0)

    def count(t, n):
        return n + jnp.where((tab[0, t] == 1) & (tab[3, t] == 0), 1, 0)

    n_first = lax.fori_loop(0, nslot, count, 0)
    chunks_first = (n_first + CH - 1) // CH

    def place(t, carry):
        c0, c1 = carry
        first = tab[3, t] == 0
        used = tab[0, t] == 1
        pos = jnp.where(first, c0, chunks_first * CH + c1)

        @pl.when(used)
        def _():
            where_[pos] = t
            x_copy(tab[1, t], pos).start()
            y_copy(tab[2, t], pos).start()

        add = jnp.where(used, 1, 0)
        return c0 + jnp.where(first, add, 0), c1 + jnp.where(first, 0, add)

    _, n_second = lax.fori_loop(0, nslot, place, (0, 0))
    chunks = chunks_first + (n_second + CH - 1) // CH
    send[...] = jnp.zeros_like(send)

    def chunk(c, carry):
        for i in range(CH):
            pos = c * CH + i
            t = where_[pos]

            @pl.when(t < nslot)
            def _():
                x_copy(0, pos).wait()
                y_copy(0, pos).wait()

        slot = jnp.where(c < chunks_first, 0, 1)
        x = xs[pl.ds(c * CH, CH)].reshape(CH * half, xs.shape[2])
        y = ys[pl.ds(c * CH, CH)].reshape(CH * half, ys.shape[2])
        u = jnp.dot(x, w[slot], preferred_element_type=F32).astype(BF16)
        d = lax.dot_general(u, y, NT_DIMS, preferred_element_type=F32)
        for i in range(0, CH * half, 128):
            prod[i : i + 128] = d[i : i + 128, i : i + 128]
        quads = [prod[pl.ds(q, CH * half // 4, stride=4), :] for q in range(4)]
        for i in range(CH):
            t = where_[c * CH + i]
            tile = jnp.concatenate(
                [v[8 * i : 8 * i + 8, half * i % 128 : half * i % 128 + half] for v in quads],
                axis=1,
            )

            @pl.when(t < nslot)
            def _():
                send[t // CAP, t % CAP] = tile
                owner = tab[2, t] // nk
                row = CAP + tab[2, t] % nk
                send[owner, row] = send[owner, row] + tile

        return carry

    lax.fori_loop(0, chunks, chunk, 0)


def exchange_kernel(tab, own, big, mine, whi, wlo, cw, out, p1, p2, tot, prod, flat, s1, s2):
    nslot = tab.shape[1]
    npair = own.shape[1]
    nk = tot.shape[0]
    rows = p2.shape[1]
    nt = mine.shape[0] // nk
    wide = p2.shape[2]

    def second(j):
        return pltpu.make_async_copy(big.at[own[1, j], pl.ds(nt, rows)], p2.at[j], s2.at[j])

    def first(t):
        return pltpu.make_async_copy(big.at[tab[6, t], pl.ds(nt, rows)], p1.at[t], s1.at[t])

    for j in range(npair):
        second(j).start()

    def begin(t, carry):
        @pl.when(tab[4, t] == 1)
        def _():
            first(t).start()

        return carry

    lax.fori_loop(0, nslot, begin, 0)
    tot[...] = jnp.zeros_like(tot)
    for j in range(npair):
        second(j).wait()
    b = p2[...].reshape(npair * rows, wide)
    e = lax.dot_general(b, whi[...], NT_DIMS, preferred_element_type=F32)
    e = e + lax.dot_general(b, wlo[...], NT_DIMS, preferred_element_type=F32)
    e = e + e
    for k in range(nk):
        prod[k] = e[:, k * nt : (k + 1) * nt]
    for j in range(npair):
        r = pl.ds(j * rows, rows)
        flat[r, :] = prod[own[0, j], r, :]

    def gather(t, carry):
        @pl.when(tab[4, t] == 1)
        def _():
            first(t).wait()
            k = tab[5, t]
            tot[k] = tot[k] + p1[t].astype(F32)

        return carry

    lax.fori_loop(0, nslot, gather, 0)
    w = tot[...].reshape(nk * rows, wide) * cw[...]
    hi = w.astype(BF16)
    lo = (w - hi.astype(F32)).astype(BF16)
    m = lax.dot_general(
        jnp.concatenate([hi, lo], axis=0), mine[...], NT_DIMS, preferred_element_type=F32
    )
    m = m[: nk * rows] + m[nk * rows :]
    m = m + m
    for k in range(nk):
        flat[pl.ds((npair + k) * rows, rows), :] = m[
            k * rows : (k + 1) * rows, k * nt : (k + 1) * nt
        ]
    z = flat_tiles(flat, (npair + nk) * rows)
    for j in range(npair + nk):
        out[j] = z[8 * j : 8 * j + 8]


def collect_kernel(own, e, got, out):
    nk = got.shape[1] - CAP
    npair = own.shape[1]
    for j in range(npair):
        out[j] = got[own[2, j], own[3, j]]
    for k in range(nk):
        out[npair + k] = jnp.sum(got[:, CAP + k], axis=0)
    out[npair + nk :] = e[...]


def finish_kernel(whole, blocks, mirrored, dmat, emat, rows):
    npair, nk = blocks.shape[0], mirrored.shape[0]
    nt = dmat.shape[1]
    half = nt // 2
    n = npair + nk
    for j in range(n):
        for a in range(2):
            left, right = whole[2 * a, j], whole[2 * a + 1, j]
            for q in range(4):
                cut = slice(half * q, half * (q + 1))
                dmat[j, pl.ds(half * a + q, 8, stride=4), :] = jnp.concatenate(
                    [left[:, cut], right[:, cut]], axis=1
                )
        for a in range(4):
            tile = whole[a, n + j]
            emat[j, pl.ds(16 * a, 8, stride=2), :] = tile[:, :nt]
            emat[j, pl.ds(16 * a + 1, 8, stride=2), :] = tile[:, nt:]
    for j in range(n):
        if j < npair:
            dmat[j] = emat[j].T - dmat[j]
        else:
            dmat[j] = (emat[j] - dmat[j]).T
        even = dmat[j, pl.ds(0, half, stride=2), :]
        odd = dmat[j, pl.ds(1, half, stride=2), :]
        rows[pl.ds(j * half, half), :] = jnp.concatenate([even, odd], axis=1)
    for r in range(half):
        lanes = pl.ds(2 * nt * r, 2 * nt)
        blocks[:, lanes] = rows[pl.ds(r, npair, stride=half), :]
        mirrored[:, lanes] = rows[pl.ds(npair * half + r, nk, stride=half), :]


def in_vmem(count):
    return [pl.BlockSpec(memory_space=pltpu.VMEM)] * count


SMEM = pl.BlockSpec(memory_space=pltpu.SMEM)
ANY = pl.BlockSpec(memory_space=pl.ANY)


def per_device(x, y, p, coulomb, w, pairs, q_slot):
    n_ka = lax.axis_size("ka")
    me = lax.axis_index("ka")
    a = lax.axis_index("ga")
    nk, nt, gl = x.shape
    qs = w.shape[0]
    npair = pairs.shape[0]
    nslot = n_ka * CAP

    half, rows = nt // 2, nt // 4
    with jax.named_scope("pack"):
        sent = [
            jnp.concatenate(
                [
                    x[:, half * (b // 2) : half * (b // 2) + half],
                    y[:, half * (b % 2) : half * (b % 2) + half],
                    p[:, rows * b : rows * (b + 1)],
                ],
                axis=1,
            )
            for b in range(4)
        ]
        parts = lax.all_to_all(widen(jnp.stack(sent)), "ga", 0, 0, tiled=True)
        payload = jnp.concatenate([parts[b] for b in range(4)], axis=2)
    with jax.named_scope("spread"):
        big = lax.all_gather(payload, "ka", axis=0, tiled=True)

    with jax.named_scope("weights"):
        up = [(i, (i + 1) % 4) for i in range(4)]
        down = [(i, (i - 1) % 4) for i in range(4)]
        here = jnp.concatenate([widen(w[:, :, i * gl : (i + 1) * gl]) for i in range(4)], axis=2)
        here = jnp.pad(here, ((0, 0), (0, QW - gl), (0, 0)))
        below = lax.ppermute(here, "ga", up)
        above = lax.ppermute(here, "ga", down)
        across = [lax.ppermute(below[:1], "ga", up), lax.ppermute(above[1:], "ga", down)]
        wk = jnp.zeros((qs, 4, QW, 4 * QW), BF16)
        for step, v in ((0, here), (1, above), (3, below)):
            wk = lax.dynamic_update_slice_in_dim(wk, v[:, None], (a + step) % 4, 1)
        for i, v in enumerate(across):
            wk = lax.dynamic_update_slice(wk, v[:, None], (i, (a + 2) % 4, 0, 0))
        wk = wk.reshape(qs, 4 * QW, 4 * QW)

    with jax.named_scope("exchange_pack"):
        c1 = lax.reduce_precision(coulomb, 8, 7)
        c2 = lax.reduce_precision(coulomb - c1, 8, 7)
        c3 = coulomb - c1 - c2
        pieces = jnp.pad(jnp.stack([c1, c2, c3]).astype(BF16), ((0, 13), (0, 0)))
        held = jnp.concatenate([p.reshape(nk * nt, gl), pieces], axis=0)
        held = lax.all_gather(widen(held), "ga", axis=1, tiled=True)
        full = held[: nk * nt]
        c_full = jnp.sum(held[nk * nt : nk * nt + 3].astype(F32), axis=0, keepdims=True)
        weighted = full.astype(F32) * c_full
        w_hi = lax.reduce_precision(weighted, 8, 7)
        w_lo = (weighted - w_hi).astype(BF16)
        w_hi = w_hi.astype(BF16)

    with jax.named_scope("tables"):
        every = lax.all_gather(pairs, "ka", axis=0, tiled=True).reshape(n_ka, npair, 3)

        def routes(rows):
            slot = jnp.sum(
                jnp.where(
                    rows[..., 2, None] == jnp.arange(q_slot.shape[0]), q_slot, 0
                ),
                axis=-1,
            )
            q_owner = slot // qs
            k_owner = rows[..., 1] // nk
            return slot % qs, q_owner, rank_in_group(q_owner), k_owner, rank_in_group(k_owner)

        local, q_owner, q_rank, k_owner, k_rank = routes(every)
        ranks = jnp.arange(CAP)
        hot_q = (q_owner == me)[..., None] & (q_rank[..., None] == ranks)
        hot_k = (k_owner == me)[..., None] & (k_rank[..., None] == ranks)

        def pick(hot, v):
            return jnp.sum(jnp.where(hot, v[..., None], 0), axis=1).reshape(nslot)

        ones = jnp.ones_like(local)
        tab = jnp.stack(
            [
                pick(hot_q, ones),
                pick(hot_q, every[..., 0]),
                pick(hot_q, every[..., 1]),
                pick(hot_q, local),
                pick(hot_k, ones),
                pick(hot_k, every[..., 1] - me * nk),
                pick(hot_k, every[..., 0]),
            ]
        )
        _, o1, r1, _, _ = routes(pairs)
        own = jnp.stack([pairs[:, 0] - me * nk, pairs[:, 1], o1, r1])

    npos = nslot + qs * CH
    send = pl.pallas_call(
        direct_kernel,
        out_shape=jax.ShapeDtypeStruct((n_ka, CAP + nk, 8, 128), F32),
        in_specs=[SMEM, ANY, *in_vmem(1)],
        out_specs=pl.BlockSpec(memory_space=pltpu.VMEM),
        scratch_shapes=[
            pltpu.VMEM((npos, half, 4 * QW), BF16),
            pltpu.VMEM((npos, half, 4 * QW), BF16),
            pltpu.VMEM((CH * half, 128), F32),
            pltpu.SMEM((npos,), jnp.int32),
            pltpu.SemaphoreType.DMA((npos,)),
            pltpu.SemaphoreType.DMA((npos,)),
        ],
        compiler_params=pltpu.CompilerParams(vmem_limit_bytes=48 * 1024 * 1024),
        name="direct",
    )(tab, big, wk)
    with jax.named_scope("to_holders"):
        got = lax.all_to_all(send, "ka", 0, 0, tiled=True)
    exch = pl.pallas_call(
        exchange_kernel,
        out_shape=jax.ShapeDtypeStruct((npair + nk, 8, 128), F32),
        in_specs=[SMEM, SMEM, ANY, *in_vmem(4)],
        out_specs=pl.BlockSpec(memory_space=pltpu.VMEM),
        scratch_shapes=[
            pltpu.VMEM((nslot, rows, 4 * QW), BF16),
            pltpu.VMEM((npair, rows, 4 * QW), BF16),
            pltpu.VMEM((nk, rows, 4 * QW), F32),
            pltpu.VMEM((nk, npair * rows, nt), F32),
            pltpu.VMEM(((npair + nk) * rows, nt), F32),
            pltpu.SemaphoreType.DMA((nslot,)),
            pltpu.SemaphoreType.DMA((npair,)),
        ],
        compiler_params=pltpu.CompilerParams(vmem_limit_bytes=32 * 1024 * 1024),
        name="exchange",
    )(tab, own, big, full, w_hi, w_lo, c_full)
    both = pl.pallas_call(
        collect_kernel,
        out_shape=jax.ShapeDtypeStruct((2 * (npair + nk), 8, 128), F32),
        in_specs=[SMEM, *in_vmem(2)],
        out_specs=pl.BlockSpec(memory_space=pltpu.VMEM),
        name="collect",
    )(own, exch, got)
    with jax.named_scope("copies"):
        whole = lax.all_gather(both, "ga", axis=0)
    return pl.pallas_call(
        finish_kernel,
        out_shape=(
            jax.ShapeDtypeStruct((npair, nt * nt), F32),
            jax.ShapeDtypeStruct((nk, nt * nt), F32),
        ),
        in_specs=in_vmem(1),
        out_specs=tuple(in_vmem(2)),
        scratch_shapes=[
            pltpu.VMEM((npair + nk, nt, nt), F32),
            pltpu.VMEM((npair + nk, nt, nt), F32),
            pltpu.VMEM(((npair + nk) * half, 2 * nt), F32),
        ],
        name="finish",
    )(whole)


def solution(mesh):
    in_specs = (
        P("ka", None, "ga"),
        P("ka", None, "ga"),
        P("ka", None, "ga"),
        P("ga"),
        P("ka", "ga", None),
        P("ka", None),
        P(),
    )
    out_specs = (P("ka", None), P("ka", None))
    return jax.shard_map(
        per_device, mesh=mesh, in_specs=in_specs, out_specs=out_specs, check_vma=False
    )
```

```python
import jax
import jax.numpy as jnp
from jax import lax
from jax.experimental import pallas as pl
from jax.experimental.pallas import tpu as pltpu
from jax.sharding import PartitionSpec as P

CAP = 2
QW = 384
CH = 8
F32 = jnp.float32
BF16 = jnp.bfloat16
NT_DIMS = (((1,), (1,)), ((), ()))


def rank_in_group(owners):
    n = owners.shape[-1]
    same = owners[..., :, None] == owners[..., None, :]
    before = jnp.arange(n)[:, None] > jnp.arange(n)[None, :]
    return jnp.sum(jnp.logical_and(same, before).astype(jnp.int32), axis=-1)


def widen(v):
    return jnp.pad(v, ((0, 0),) * (v.ndim - 1) + ((0, QW - v.shape[-1]),))


def flat_tiles(tmp, rows):
    even = tmp[pl.ds(0, rows // 2, stride=2), :]
    odd = tmp[pl.ds(1, rows // 2, stride=2), :]
    return jnp.concatenate([even, odd], axis=1)


def direct_kernel(plan, big, wk, keep, away, w, xs, ys, prod, sw, sx, sy):
    half = prod.shape[0] // CH
    nt = 2 * half
    deep = xs.shape[3]
    nslot = keep.shape[0]
    chunks_first, chunks, parity = plan[3, 0], plan[3, 1], plan[3, 2]

    def x_copy(pos, buf, i):
        return pltpu.make_async_copy(big.at[plan[1, pos], pl.ds(0, nt)], xs.at[buf, i], sx.at[buf, i])

    def y_copy(pos, buf, i):
        return pltpu.make_async_copy(big.at[plan[2, pos], pl.ds(nt, nt)], ys.at[buf, i], sy.at[buf, i])

    def w_copy(slot):
        return pltpu.make_async_copy(wk.at[slot], w.at[slot], sw.at[slot])

    def begin(c, buf):
        for i in range(CH):
            x_copy(c * CH + i, buf, i).start()
            y_copy(c * CH + i, buf, i).start()

    @pl.when(chunks > 0)
    def _():
        begin(0, 0)

    for slot in range(w.shape[0]):
        w_copy(slot).start()
    for slot in range(w.shape[0]):
        w_copy(slot).wait()

    def chunk(c, carry):
        buf = lax.rem(c, 2)

        @pl.when(c + 1 < chunks)
        def _():
            begin(c + 1, 1 - buf)

        for i in range(CH):
            x_copy(c * CH + i, buf, i).wait()
            y_copy(c * CH + i, buf, i).wait()
        slot = jnp.where(c < chunks_first, 0, 1)
        u = jnp.dot(
            xs[buf, :, :half].reshape(CH * half, deep),
            w[slot, :deep],
            preferred_element_type=F32,
        )
        u = u + jnp.dot(
            xs[buf, :, half:].reshape(CH * half, deep),
            w[slot, deep:],
            preferred_element_type=F32,
        )
        y = ys[buf].reshape(CH * nt, deep)
        d = lax.dot_general(u.astype(BF16), y, NT_DIMS, preferred_element_type=F32)
        for i in range(CH * nt // 128):
            prod[nt * i : nt * i + nt] = d[nt * i : nt * i + nt, 128 * i : 128 * i + 128]
        quads = [prod[pl.ds(q, CH * half // 4, stride=4), :] for q in range(4)]
        for i in range(CH):
            t = plan[0, c * CH + i]
            tiles = []
            for h in range(2):
                lane = nt * i % 128 + half * h
                tiles.append(
                    jnp.concatenate(
                        [v[8 * i : 8 * i + 8, lane : lane + half] for v in quads], axis=1
                    )
                )

            @pl.when(t < nslot)
            def _():
                keep[t] = jnp.where(parity == 0, tiles[0], tiles[1])
                away[t] = jnp.where(parity == 0, tiles[1], tiles[0])

        return carry

    lax.fori_loop(0, chunks, chunk, 0)


def route_kernel(tab, keep, came, send):
    nk = send.shape[1] - CAP
    send[:, CAP:] = jnp.zeros((send.shape[0], nk, *send.shape[2:]), F32)
    for t in range(tab.shape[1]):
        v = keep[t] + came[t]
        send[t // CAP, t % CAP] = v

        @pl.when(tab[0, t] == 1)
        def _():
            owner = tab[2, t] // nk
            row = CAP + tab[2, t] % nk
            send[owner, row] = send[owner, row] + v


def exchange_kernel(tab, own, big, got, mine, whi, wlo, cw, out, p1, p2, tot, prod, flat, s1, s2):
    nslot = tab.shape[1]
    npair = own.shape[1]
    nk = tot.shape[0]
    rows = p2.shape[1]
    nt = mine.shape[0] // nk
    wide = p2.shape[2]

    def second(j):
        return pltpu.make_async_copy(big.at[own[1, j]], p2.at[j], s2.at[j])

    def first(t):
        return pltpu.make_async_copy(big.at[tab[6, t]], p1.at[t], s1.at[t])

    for j in range(npair):
        second(j).start()

    def begin(t, carry):
        @pl.when(tab[4, t] == 1)
        def _():
            first(t).start()

        return carry

    lax.fori_loop(0, nslot, begin, 0)
    tot[...] = jnp.zeros_like(tot)
    for j in range(npair):
        second(j).wait()
    b = p2[...].reshape(npair * rows, wide)
    e = lax.dot_general(b, whi[...], NT_DIMS, preferred_element_type=F32)
    e = e + lax.dot_general(b, wlo[...], NT_DIMS, preferred_element_type=F32)
    e = e + e
    for k in range(nk):
        prod[k] = e[:, k * nt : (k + 1) * nt]
    for j in range(npair):
        r = pl.ds(j * rows, rows)
        flat[r, :] = prod[own[0, j], r, :]

    def gather(t, carry):
        @pl.when(tab[4, t] == 1)
        def _():
            first(t).wait()
            k = tab[5, t]
            tot[k] = tot[k] + p1[t].astype(F32)

        return carry

    lax.fori_loop(0, nslot, gather, 0)
    w = tot[...].reshape(nk * rows, wide) * cw[...]
    hi = w.astype(BF16)
    lo = (w - hi.astype(F32)).astype(BF16)
    m = lax.dot_general(
        jnp.concatenate([hi, lo], axis=0), mine[...], NT_DIMS, preferred_element_type=F32
    )
    m = m[: nk * rows] + m[nk * rows :]
    m = m + m
    for k in range(nk):
        flat[pl.ds((npair + k) * rows, rows), :] = m[
            k * rows : (k + 1) * rows, k * nt : (k + 1) * nt
        ]
    z = flat_tiles(flat, (npair + nk) * rows)
    n = npair + nk
    for j in range(n):
        out[n + j] = z[8 * j : 8 * j + 8]
    for j in range(npair):
        out[j] = got[own[2, j], own[3, j]]
    for k in range(nk):
        out[npair + k] = jnp.sum(got[:, CAP + k], axis=0)


def finish_kernel(place, r0, r1, r2, r3, blocks, mirrored, whole, dmat, emat, rows):
    npair, nk = blocks.shape[0], mirrored.shape[0]
    nt = dmat.shape[1]
    half = nt // 2
    n = npair + nk
    for i, r in enumerate((r0, r1, r2, r3)):
        whole[place[i]] = r[...]
    for j in range(n):
        for a in range(2):
            left, right = whole[2 * a, j], whole[2 * a + 1, j]
            for q in range(4):
                cut = slice(half * q, half * (q + 1))
                dmat[j, pl.ds(half * a + q, 8, stride=4), :] = jnp.concatenate(
                    [left[:, cut], right[:, cut]], axis=1
                )
        for a in range(4):
            tile = whole[a, n + j]
            emat[j, pl.ds(16 * a, 8, stride=2), :] = tile[:, :nt]
            emat[j, pl.ds(16 * a + 1, 8, stride=2), :] = tile[:, nt:]
    for j in range(n):
        if j < npair:
            dmat[j] = emat[j].T - dmat[j]
        else:
            dmat[j] = (emat[j] - dmat[j]).T
        even = dmat[j, pl.ds(0, half, stride=2), :]
        odd = dmat[j, pl.ds(1, half, stride=2), :]
        rows[pl.ds(j * half, half), :] = jnp.concatenate([even, odd], axis=1)
    for r in range(half):
        lanes = pl.ds(2 * nt * r, 2 * nt)
        blocks[:, lanes] = rows[pl.ds(r, npair, stride=half), :]
        mirrored[:, lanes] = rows[pl.ds(npair * half + r, nk, stride=half), :]


def in_vmem(count):
    return [pl.BlockSpec(memory_space=pltpu.VMEM)] * count


SMEM = pl.BlockSpec(memory_space=pltpu.SMEM)
HBM = pl.BlockSpec(memory_space=pltpu.HBM)
ANY = pl.BlockSpec(memory_space=pl.ANY)


def per_device(x, y, p, coulomb, w, pairs, q_slot):
    n_ka = lax.axis_size("ka")
    me = lax.axis_index("ka")
    a = lax.axis_index("ga")
    nk, nt, gl = x.shape
    qs = w.shape[0]
    npair = pairs.shape[0]
    nslot = n_ka * CAP

    half, rows = nt // 2, nt // 4

    def shift(r):
        return [(i, (i + r) % 4) for i in range(4)]

    with jax.named_scope("pack"):
        y_far = lax.ppermute(y, "ga", [(i, 3 - i) for i in range(4)])
        cut = [jnp.where((a + r) % 4 < 2, x[:, :half], x[:, half:]) for r in range(4)]
        cut = cut[:1] + [lax.ppermute(cut[r], "ga", shift(r)) for r in range(1, 4)]
        payload = jnp.concatenate(
            [
                jnp.concatenate([widen(cut[0]), widen(cut[1])], axis=2),
                jnp.concatenate([widen(cut[2]), widen(cut[3])], axis=2),
                jnp.concatenate(
                    [widen(jnp.where(a < 2, y, y_far)), widen(jnp.where(a < 2, y_far, y))], axis=2
                ),
            ],
            axis=1,
        )
    with jax.named_scope("spread"):
        big = lax.all_gather(payload, "ka", axis=0, tiled=True)

    with jax.named_scope("weights"):
        cols = [
            jnp.pad(w[:, :, i * gl : (i + 1) * gl], ((0, 0), (0, QW - gl), (0, QW - gl)))
            for i in range(4)
        ]
        outer = jnp.concatenate([cols[0], cols[3]], axis=2)
        inner = jnp.concatenate([cols[1], cols[2]], axis=2)
        wk = []
        for r in range(4):
            to = (a + r) % 4
            v = jnp.where((to == 0) | (to == 3), outer, inner)
            wk.append(lax.ppermute(v, "ga", shift(r)) if r else v)
        wk = jnp.concatenate(wk, axis=1)

    with jax.named_scope("exchange_pack"):
        c1 = lax.reduce_precision(coulomb, 8, 7)
        c2 = lax.reduce_precision(coulomb - c1, 8, 7)
        c3 = coulomb - c1 - c2
        pieces = jnp.pad(jnp.stack([c1, c2, c3]).astype(BF16), ((0, 13), (0, 0)))
        held = jnp.concatenate([p.reshape(nk * nt, gl), pieces], axis=0)
        held = lax.all_gather(widen(held), "ga", axis=1, tiled=True)
        full = held[: nk * nt]
        p_rows = lax.dynamic_slice_in_dim(full.reshape(nk, nt, 4 * QW), a * rows, rows, axis=1)
        p_big = lax.all_gather(p_rows, "ka", axis=0, tiled=True)
        c_full = jnp.sum(held[nk * nt : nk * nt + 3].astype(F32), axis=0, keepdims=True)
        weighted = full.astype(F32) * c_full
        w_hi = lax.reduce_precision(weighted, 8, 7)
        w_lo = (weighted - w_hi).astype(BF16)
        w_hi = w_hi.astype(BF16)

    with jax.named_scope("tables"):
        every = lax.all_gather(pairs, "ka", axis=0, tiled=True).reshape(n_ka, npair, 3)

        def routes(rows):
            slot = jnp.sum(
                jnp.where(
                    rows[..., 2, None] == jnp.arange(q_slot.shape[0]), q_slot, 0
                ),
                axis=-1,
            )
            q_owner = slot // qs
            k_owner = rows[..., 1] // nk
            return slot % qs, q_owner, rank_in_group(q_owner), k_owner, rank_in_group(k_owner)

        local, q_owner, q_rank, k_owner, k_rank = routes(every)
        ranks = jnp.arange(CAP)
        hot_q = (q_owner == me)[..., None] & (q_rank[..., None] == ranks)
        hot_k = (k_owner == me)[..., None] & (k_rank[..., None] == ranks)

        def pick(hot, v):
            return jnp.sum(jnp.where(hot, v[..., None], 0), axis=1).reshape(nslot)

        ones = jnp.ones_like(local)
        tab = jnp.stack(
            [
                pick(hot_q, ones),
                pick(hot_q, every[..., 0]),
                pick(hot_q, every[..., 1]),
                pick(hot_q, local),
                pick(hot_k, ones),
                pick(hot_k, every[..., 1] - me * nk),
                pick(hot_k, every[..., 0]),
            ]
        )
        _, o1, r1, _, _ = routes(pairs)
        own = jnp.stack([pairs[:, 0] - me * nk, pairs[:, 1], o1, r1])

    with jax.named_scope("plan"):
        npos = nslot + qs * CH
        used, slot = tab[0], tab[3]
        same = (slot[:, None] == slot[None, :]) & (used[None, :] == 1)
        order = jnp.arange(nslot)
        rank = jnp.sum((same & (order[:, None] > order[None, :])).astype(jnp.int32), axis=1)
        first = jnp.sum(used * (slot == 0))
        second = jnp.sum(used * (slot == 1))
        chunks_first = (first + CH - 1) // CH
        chunks = chunks_first + (second + CH - 1) // CH
        pos = jnp.where(slot == 0, rank, chunks_first * CH + rank)
        hot = (pos[None, :] == jnp.arange(npos)[:, None]) & (used == 1)[None, :]

        def at_pos(v):
            return jnp.sum(jnp.where(hot, v[None, :], 0), axis=1)

        heads = jnp.pad(jnp.stack([chunks_first, chunks, a % 2]), (0, npos - 3))
        plan = jnp.stack([at_pos(order - nslot) + nslot, at_pos(tab[1]), at_pos(tab[2]), heads])
    keep, away = pl.pallas_call(
        direct_kernel,
        out_shape=(jax.ShapeDtypeStruct((nslot, 8, 128), F32),) * 2,
        in_specs=[SMEM, ANY, ANY],
        out_specs=tuple(in_vmem(2)),
        scratch_shapes=[
            pltpu.VMEM((qs, 4 * QW, 2 * QW), BF16),
            pltpu.VMEM((2, CH, nt, 2 * QW), BF16),
            pltpu.VMEM((2, CH, nt, 2 * QW), BF16),
            pltpu.VMEM((CH * half, 128), F32),
            pltpu.SemaphoreType.DMA((qs,)),
            pltpu.SemaphoreType.DMA((2, CH)),
            pltpu.SemaphoreType.DMA((2, CH)),
        ],
        compiler_params=pltpu.CompilerParams(vmem_limit_bytes=60 * 1024 * 1024),
        name="direct",
    )(plan, big, wk)
    with jax.named_scope("to_neighbour"):
        came = lax.ppermute(away, "ga", [(0, 1), (1, 0), (2, 3), (3, 2)])
    send = pl.pallas_call(
        route_kernel,
        out_shape=jax.ShapeDtypeStruct((n_ka, CAP + nk, 8, 128), F32),
        in_specs=[SMEM, *in_vmem(2)],
        out_specs=pl.BlockSpec(memory_space=pltpu.VMEM),
        name="route",
    )(tab, keep, came)
    with jax.named_scope("to_holders"):
        got = lax.all_to_all(send, "ka", 0, 0, tiled=True)
    both = pl.pallas_call(
        exchange_kernel,
        out_shape=jax.ShapeDtypeStruct((2 * (npair + nk), 8, 128), F32),
        in_specs=[SMEM, SMEM, HBM, *in_vmem(5)],
        out_specs=pl.BlockSpec(memory_space=pltpu.VMEM),
        scratch_shapes=[
            pltpu.VMEM((nslot, rows, 4 * QW), BF16),
            pltpu.VMEM((npair, rows, 4 * QW), BF16),
            pltpu.VMEM((nk, rows, 4 * QW), F32),
            pltpu.VMEM((nk, npair * rows, nt), F32),
            pltpu.VMEM(((npair + nk) * rows, nt), F32),
            pltpu.SemaphoreType.DMA((nslot,)),
            pltpu.SemaphoreType.DMA((npair,)),
        ],
        compiler_params=pltpu.CompilerParams(vmem_limit_bytes=60 * 1024 * 1024),
        name="exchange",
    )(tab, own, p_big, got, full, w_hi, w_lo, c_full)
    with jax.named_scope("copies"):
        others = [lax.ppermute(both, "ga", shift(r)) for r in range(1, 4)]
        place = jnp.stack([(a - r) % 4 for r in range(4)])
    return pl.pallas_call(
        finish_kernel,
        out_shape=(
            jax.ShapeDtypeStruct((npair, nt * nt), F32),
            jax.ShapeDtypeStruct((nk, nt * nt), F32),
        ),
        in_specs=[SMEM, *in_vmem(4)],
        out_specs=tuple(in_vmem(2)),
        scratch_shapes=[
            pltpu.VMEM((4, 2 * (npair + nk), 8, 128), F32),
            pltpu.VMEM((npair + nk, nt, nt), F32),
            pltpu.VMEM((npair + nk, nt, nt), F32),
            pltpu.VMEM(((npair + nk) * half, 2 * nt), F32),
        ],
        name="finish",
    )(place, both, *others)


def solution(mesh):
    in_specs = (
        P("ka", None, "ga"),
        P("ka", None, "ga"),
        P("ka", None, "ga"),
        P("ga"),
        P("ka", "ga", None),
        P("ka", None),
        P(),
    )
    out_specs = (P("ka", None), P("ka", None))
    return jax.shard_map(
        per_device, mesh=mesh, in_specs=in_specs, out_specs=out_specs, check_vma=False
    )
```

```python
import jax
import jax.numpy as jnp
from jax import lax
from jax.experimental import pallas as pl
from jax.experimental.pallas import tpu as pltpu
from jax.sharding import PartitionSpec as P

CAP = 2
QW = 384
CH = 8
F32 = jnp.float32
BF16 = jnp.bfloat16
NT_DIMS = (((1,), (1,)), ((), ()))


def rank_in_group(owners):
    n = owners.shape[-1]
    same = owners[..., :, None] == owners[..., None, :]
    before = jnp.arange(n)[:, None] > jnp.arange(n)[None, :]
    return jnp.sum(jnp.logical_and(same, before).astype(jnp.int32), axis=-1)


def widen(v):
    return jnp.pad(v, ((0, 0),) * (v.ndim - 1) + ((0, QW - v.shape[-1]),))


def flat_tiles(tmp, rows):
    even = tmp[pl.ds(0, rows // 2, stride=2), :]
    odd = tmp[pl.ds(1, rows // 2, stride=2), :]
    return jnp.concatenate([even, odd], axis=1)


def direct_kernel(plan, big, w, keep, away, xs, ys, us, prod, kept, sent, sx, sy):
    half = prod.shape[0] // CH
    nt = 2 * half
    deep = xs.shape[3]
    nslot = keep.shape[0]
    chunks_first, chunks, parity = plan[3, 0], plan[3, 1], plan[3, 2]

    def x_copy(pos, buf, i):
        return pltpu.make_async_copy(big.at[plan[1, pos], pl.ds(0, nt)], xs.at[buf, i], sx.at[buf, i])

    def y_copy(pos, buf, i):
        return pltpu.make_async_copy(big.at[plan[2, pos], pl.ds(nt, nt)], ys.at[buf, i], sy.at[buf, i])

    def begin(c):
        for i in range(CH):
            x_copy(c * CH + i, lax.rem(c, 2), i).start()
            y_copy(c * CH + i, lax.rem(c, 3), i).start()

    def products(c):
        u = us[lax.rem(c + 2, 2)]
        y = ys[lax.rem(c + 3, 3)].reshape(CH * nt, deep)
        for i in range(0, CH, 4):
            d = lax.dot_general(
                u[half * i : half * (i + 4)],
                y[nt * i : nt * (i + 4)],
                NT_DIMS,
                preferred_element_type=F32,
            )
            for j in range(2):
                prod[half * i + nt * j : half * i + nt * j + nt] = d[
                    nt * j : nt * j + nt, 128 * j : 128 * j + 128
                ]
        lane = lax.broadcasted_iota(jnp.int32, (8, 128), 1)
        for i in range(CH):
            t = jnp.where(c < 0, nslot, plan[0, jnp.maximum(c, 0) * CH + i])
            rows = [prod[half * i + 8 * g : half * i + 8 * g + 8] for g in range(4)]
            tiles = []
            for h in range(2):
                start = nt * (i % 2) + half * h
                moved = [pltpu.roll(v, (half * g - start) % 128, 1) for g, v in enumerate(rows)]
                low = jnp.where(lane < half, moved[0], moved[1])
                high = jnp.where(lane < 3 * half, moved[2], moved[3])
                tiles.append(jnp.where(lane < nt, low, high))
            kept[t] = jnp.where(parity == 0, tiles[0], tiles[1])
            sent[t] = jnp.where(parity == 0, tiles[1], tiles[0])

    @pl.when(chunks > 0)
    def _():
        begin(0)

    def chunk(c, carry):
        @pl.when(c + 1 < chunks)
        def _():
            begin(c + 1)

        bx, by = lax.rem(c, 2), lax.rem(c, 3)
        for i in range(CH):
            x_copy(c * CH + i, bx, i).wait()
            y_copy(c * CH + i, by, i).wait()
        products(c - 1)
        slot = jnp.where(c < chunks_first, 0, 1)
        u = jnp.dot(
            xs[bx, :, :half].reshape(CH * half, deep), w[slot, :deep], preferred_element_type=F32
        )
        u = u + jnp.dot(
            xs[bx, :, half:].reshape(CH * half, deep), w[slot, deep:], preferred_element_type=F32
        )
        us[bx] = u.astype(BF16)
        return carry

    lax.fori_loop(0, chunks, chunk, 0)

    @pl.when(chunks > 0)
    def _():
        products(chunks - 1)

    keep[...] = kept[:nslot]
    away[...] = sent[:nslot]


def route_kernel(tab, keep, came, exch, send, done, mine, theirs, sem):
    copies = [
        pltpu.make_async_copy(keep, mine, sem.at[0]),
        pltpu.make_async_copy(came, theirs, sem.at[1]),
    ]
    for c in copies:
        c.start()
    nk = send.shape[1] - CAP
    send[:, CAP:] = jnp.zeros((send.shape[0], nk, *send.shape[2:]), F32)
    done[...] = exch[...]
    for c in copies:
        c.wait()
    for t in range(tab.shape[1]):
        v = mine[t] + theirs[t]
        send[t // CAP, t % CAP] = v

        @pl.when(tab[0, t] == 1)
        def _():
            owner = tab[2, t] // nk
            row = CAP + tab[2, t] % nk
            send[owner, row] = send[owner, row] + v


def exchange_kernel(tab, own, big, full, whi, wlo, cw, out, p1, p2, tot, prod, flat, s1, s2):
    nslot = tab.shape[1]
    npair = own.shape[1]
    nk = tot.shape[0]
    rows = p2.shape[1] // 2
    nt = whi.shape[0] // nk
    deep = p2.shape[2]
    start = big.shape[1] - 2 * rows

    def second(j):
        return pltpu.make_async_copy(big.at[own[1, j], pl.ds(start, 2 * rows)], p2.at[j], s2.at[j])

    def first(t):
        return pltpu.make_async_copy(big.at[tab[6, t], pl.ds(start, 2 * rows)], p1.at[t], s1.at[t])

    for j in range(npair):
        second(j).start()

    def begin(t, carry):
        @pl.when(tab[4, t] == 1)
        def _():
            first(t).start()

        return carry

    lax.fori_loop(0, nslot, begin, 0)
    tot[...] = jnp.zeros_like(tot)
    for j in range(npair):
        second(j).wait()

    def contract(left, right):
        return lax.dot_general(left, right, NT_DIMS, preferred_element_type=F32)

    e = None
    for h in range(2):
        b = p2[:, rows * h : rows * (h + 1)].reshape(npair * rows, deep)
        lanes = slice(deep * h, deep * (h + 1))
        part = contract(b, whi[:, lanes]) + contract(b, wlo[:, lanes])
        e = part if e is None else e + part
    e = e + e
    for k in range(nk):
        prod[k] = e[:, k * nt : (k + 1) * nt]
    for j in range(npair):
        r = pl.ds(j * rows, rows)
        flat[r, :] = prod[own[0, j], r, :]

    def gather(t, carry):
        @pl.when(tab[4, t] == 1)
        def _():
            first(t).wait()
            k = tab[5, t]
            tot[k] = tot[k] + p1[t].astype(F32)

        return carry

    lax.fori_loop(0, nslot, gather, 0)
    m = None
    for h in range(2):
        lanes = slice(deep * h, deep * (h + 1))
        w = tot[:, rows * h : rows * (h + 1)].reshape(nk * rows, deep) * cw[:, lanes]
        hi = w.astype(BF16)
        lo = (w - hi.astype(F32)).astype(BF16)
        part = contract(jnp.concatenate([hi, lo], axis=0), full[: nk * nt, lanes])
        m = part if m is None else m + part
    m = m[: nk * rows] + m[nk * rows :]
    m = m + m
    for k in range(nk):
        flat[pl.ds((npair + k) * rows, rows), :] = m[
            k * rows : (k + 1) * rows, k * nt : (k + 1) * nt
        ]
    z = flat_tiles(flat, (npair + nk) * rows)
    for j in range(npair + nk):
        out[j] = z[8 * j : 8 * j + 8]


def collect_kernel(own, exch, got, out, here, sem):
    copy = pltpu.make_async_copy(got, here, sem)
    copy.start()
    nk = got.shape[1] - CAP
    npair = own.shape[1]
    out[npair + nk :] = exch[...]
    copy.wait()
    for j in range(npair):
        out[j] = here[own[2, j], own[3, j]]
    for k in range(nk):
        out[npair + k] = jnp.sum(here[:, CAP + k], axis=0)


def finish_kernel(place, r0, r1, r2, r3, blocks, mirrored, whole, dmat, emat, rows, sem):
    npair, nk = blocks.shape[0], mirrored.shape[0]
    nt = dmat.shape[1]
    half = nt // 2
    n = npair + nk
    copies = [
        pltpu.make_async_copy(r, whole.at[place[i]], sem.at[i])
        for i, r in enumerate((r0, r1, r2, r3))
    ]
    for c in copies:
        c.start()
    for c in copies:
        c.wait()
    for j in range(n):
        for a in range(2):
            left, right = whole[2 * a, j], whole[2 * a + 1, j]
            for g in range(4):
                cut = slice(half * g, half * (g + 1))
                dmat[j, pl.ds(half * a + 8 * g, 8), :] = jnp.concatenate(
                    [left[:, cut], right[:, cut]], axis=1
                )
        for a in range(4):
            tile = whole[a, n + j]
            emat[j, pl.ds(16 * a, 8, stride=2), :] = tile[:, :nt]
            emat[j, pl.ds(16 * a + 1, 8, stride=2), :] = tile[:, nt:]
    for j in range(n):
        if j < npair:
            dmat[j] = emat[j].T - dmat[j]
        else:
            dmat[j] = (emat[j] - dmat[j]).T
        even = dmat[j, pl.ds(0, half, stride=2), :]
        odd = dmat[j, pl.ds(1, half, stride=2), :]
        rows[pl.ds(j * half, half), :] = jnp.concatenate([even, odd], axis=1)
    for r in range(half):
        lanes = pl.ds(2 * nt * r, 2 * nt)
        blocks[:, lanes] = rows[pl.ds(r, npair, stride=half), :]
        mirrored[:, lanes] = rows[pl.ds(npair * half + r, nk, stride=half), :]


def in_vmem(count):
    return [pl.BlockSpec(memory_space=pltpu.VMEM)] * count


SMEM = pl.BlockSpec(memory_space=pltpu.SMEM)
ANY = pl.BlockSpec(memory_space=pl.ANY)


def per_device(x, y, p, coulomb, w, pairs, q_slot):
    n_ka = lax.axis_size("ka")
    me = lax.axis_index("ka")
    a = lax.axis_index("ga")
    nk, nt, gl = x.shape
    qs = w.shape[0]
    npair = pairs.shape[0]
    nslot = n_ka * CAP

    half, rows = nt // 2, nt // 4

    def shift(r):
        return [(i, (i + r) % 4) for i in range(4)]

    with jax.named_scope("pack"):
        y_far = lax.ppermute(y, "ga", [(i, 3 - i) for i in range(4)])
        cut = []
        for r in range(4):
            to = (a + r) % 4
            x_cut = jnp.where(to < 2, x[:, :half], x[:, half:])
            p_low = jnp.where(to == 0, p[:, :rows], p[:, rows : 2 * rows])
            p_high = jnp.where(to == 2, p[:, 2 * rows : 3 * rows], p[:, 3 * rows :])
            v = jnp.concatenate([x_cut, jnp.where(to < 2, p_low, p_high)], axis=1)
            cut.append(lax.ppermute(v, "ga", shift(r)) if r else v)

        def side(left, right):
            return jnp.concatenate([widen(left), widen(right)], axis=2)

        near, far = side(cut[0], cut[1]), side(cut[2], cut[3])
        y_both = side(jnp.where(a < 2, y, y_far), jnp.where(a < 2, y_far, y))
        payload = jnp.concatenate(
            [near[:, :half], far[:, :half], y_both, near[:, half:], far[:, half:]], axis=1
        )
    with jax.named_scope("spread"):
        big = lax.all_gather(payload, "ka", axis=0, tiled=True)

    with jax.named_scope("weights"):
        cols = [
            jnp.pad(w[:, :, i * gl : (i + 1) * gl], ((0, 0), (0, QW - gl), (0, QW - gl)))
            for i in range(4)
        ]
        outer = jnp.concatenate([cols[0], cols[3]], axis=2)
        inner = jnp.concatenate([cols[1], cols[2]], axis=2)
        wk = []
        for r in range(4):
            to = (a + r) % 4
            v = jnp.where((to == 0) | (to == 3), outer, inner)
            wk.append(lax.ppermute(v, "ga", shift(r)) if r else v)
        wk = jnp.concatenate(wk, axis=1)

    with jax.named_scope("exchange_pack"):
        c1 = lax.reduce_precision(coulomb, 8, 7)
        c2 = lax.reduce_precision(coulomb - c1, 8, 7)
        c3 = coulomb - c1 - c2
        pieces = jnp.pad(jnp.stack([c1, c2, c3]).astype(BF16), ((0, 13), (0, 0)))
        held = jnp.concatenate([p.reshape(nk * nt, gl), pieces], axis=0)
        held = widen(held)
        held = [held] + [lax.ppermute(held, "ga", shift(r)) for r in range(1, 4)]
        full = jnp.concatenate(held, axis=1)
        c_full = jnp.sum(full[nk * nt : nk * nt + 3].astype(F32), axis=0, keepdims=True)
        weighted = full[: nk * nt].astype(F32) * c_full
        w_hi = lax.reduce_precision(weighted, 8, 7)
        w_lo = (weighted - w_hi).astype(BF16)
        w_hi = w_hi.astype(BF16)

    with jax.named_scope("tables"):
        every = lax.all_gather(pairs, "ka", axis=0, tiled=True).reshape(n_ka, npair, 3)

        def routes(rows):
            slot = jnp.sum(
                jnp.where(
                    rows[..., 2, None] == jnp.arange(q_slot.shape[0]), q_slot, 0
                ),
                axis=-1,
            )
            q_owner = slot // qs
            k_owner = rows[..., 1] // nk
            return slot % qs, q_owner, rank_in_group(q_owner), k_owner, rank_in_group(k_owner)

        local, q_owner, q_rank, k_owner, k_rank = routes(every)
        ranks = jnp.arange(CAP)
        hot_q = (q_owner == me)[..., None] & (q_rank[..., None] == ranks)
        hot_k = (k_owner == me)[..., None] & (k_rank[..., None] == ranks)

        def pick(hot, v):
            return jnp.sum(jnp.where(hot, v[..., None], 0), axis=1).reshape(nslot)

        ones = jnp.ones_like(local)
        tab = jnp.stack(
            [
                pick(hot_q, ones),
                pick(hot_q, every[..., 0]),
                pick(hot_q, every[..., 1]),
                pick(hot_q, local),
                pick(hot_k, ones),
                pick(hot_k, every[..., 1] - me * nk),
                pick(hot_k, every[..., 0]),
            ]
        )
        _, o1, r1, _, _ = routes(pairs)
        own = jnp.stack([pairs[:, 0] - me * nk, pairs[:, 1], o1, r1])

    with jax.named_scope("plan"):
        npos = nslot + qs * CH
        used, slot = tab[0], tab[3]
        same = (slot[:, None] == slot[None, :]) & (used[None, :] == 1)
        order = jnp.arange(nslot)
        rank = jnp.sum((same & (order[:, None] > order[None, :])).astype(jnp.int32), axis=1)
        first = jnp.sum(used * (slot == 0))
        second = jnp.sum(used * (slot == 1))
        chunks_first = (first + CH - 1) // CH
        chunks = chunks_first + (second + CH - 1) // CH
        pos = jnp.where(slot == 0, rank, chunks_first * CH + rank)
        hot = (pos[None, :] == jnp.arange(npos)[:, None]) & (used == 1)[None, :]

        def at_pos(v):
            return jnp.sum(jnp.where(hot, v[None, :], 0), axis=1)

        heads = jnp.pad(jnp.stack([chunks_first, chunks, a % 2]), (0, npos - 3))
        plan = jnp.stack([at_pos(order - nslot) + nslot, at_pos(tab[1]), at_pos(tab[2]), heads])
    keep, away = pl.pallas_call(
        direct_kernel,
        out_shape=(jax.ShapeDtypeStruct((nslot, 8, 128), F32),) * 2,
        in_specs=[SMEM, ANY, *in_vmem(1)],
        out_specs=tuple(in_vmem(2)),
        scratch_shapes=[
            pltpu.VMEM((2, CH, nt, 2 * QW), BF16),
            pltpu.VMEM((3, CH, nt, 2 * QW), BF16),
            pltpu.VMEM((2, CH * half, 2 * QW), BF16),
            pltpu.VMEM((CH * half, 128), F32),
            pltpu.VMEM((nslot + 1, 8, 128), F32),
            pltpu.VMEM((nslot + 1, 8, 128), F32),
            pltpu.SemaphoreType.DMA((2, CH)),
            pltpu.SemaphoreType.DMA((3, CH)),
        ],
        compiler_params=pltpu.CompilerParams(vmem_limit_bytes=32 * 1024 * 1024),
        name="direct",
    )(plan, big, wk)
    with jax.named_scope("to_neighbour"):
        came = lax.ppermute(away, "ga", [(0, 1), (1, 0), (2, 3), (3, 2)])
    exch = pl.pallas_call(
        exchange_kernel,
        out_shape=jax.ShapeDtypeStruct((npair + nk, 8, 128), F32),
        in_specs=[SMEM, SMEM, ANY, *in_vmem(4)],
        out_specs=pl.BlockSpec(memory_space=pltpu.VMEM),
        scratch_shapes=[
            pltpu.VMEM((nslot, 2 * rows, 2 * QW), BF16),
            pltpu.VMEM((npair, 2 * rows, 2 * QW), BF16),
            pltpu.VMEM((nk, 2 * rows, 2 * QW), F32),
            pltpu.VMEM((nk, npair * rows, nt), F32),
            pltpu.VMEM(((npair + nk) * rows, nt), F32),
            pltpu.SemaphoreType.DMA((nslot,)),
            pltpu.SemaphoreType.DMA((npair,)),
        ],
        compiler_params=pltpu.CompilerParams(vmem_limit_bytes=32 * 1024 * 1024),
        name="exchange",
    )(tab, own, big, full, w_hi, w_lo, c_full)
    send, exch = pl.pallas_call(
        route_kernel,
        out_shape=(
            jax.ShapeDtypeStruct((n_ka, CAP + nk, 8, 128), F32),
            jax.ShapeDtypeStruct(exch.shape, F32),
        ),
        in_specs=[SMEM, ANY, ANY, *in_vmem(1)],
        out_specs=tuple(in_vmem(2)),
        scratch_shapes=[
            pltpu.VMEM((nslot, 8, 128), F32),
            pltpu.VMEM((nslot, 8, 128), F32),
            pltpu.SemaphoreType.DMA((2,)),
        ],
        compiler_params=pltpu.CompilerParams(vmem_limit_bytes=8 * 1024 * 1024),
        name="route",
    )(tab, keep, came, exch)
    with jax.named_scope("to_holders"):
        got = lax.all_to_all(send, "ka", 0, 0, tiled=True)
    both = pl.pallas_call(
        collect_kernel,
        out_shape=jax.ShapeDtypeStruct((2 * (npair + nk), 8, 128), F32),
        in_specs=[SMEM, *in_vmem(1), ANY],
        out_specs=pl.BlockSpec(memory_space=pltpu.VMEM),
        scratch_shapes=[pltpu.VMEM(send.shape, F32), pltpu.SemaphoreType.DMA],
        compiler_params=pltpu.CompilerParams(vmem_limit_bytes=8 * 1024 * 1024),
        name="collect",
    )(own, exch, got)
    with jax.named_scope("copies"):
        others = [lax.ppermute(both, "ga", shift(r)) for r in range(1, 4)]
        place = jnp.stack([(a - r) % 4 for r in range(4)])
    return pl.pallas_call(
        finish_kernel,
        out_shape=(
            jax.ShapeDtypeStruct((npair, nt * nt), F32),
            jax.ShapeDtypeStruct((nk, nt * nt), F32),
        ),
        in_specs=[SMEM, ANY, ANY, ANY, ANY],
        out_specs=tuple(in_vmem(2)),
        scratch_shapes=[
            pltpu.VMEM((4, 2 * (npair + nk), 8, 128), F32),
            pltpu.VMEM((npair + nk, nt, nt), F32),
            pltpu.VMEM((npair + nk, nt, nt), F32),
            pltpu.VMEM(((npair + nk) * half, 2 * nt), F32),
            pltpu.SemaphoreType.DMA((4,)),
        ],
        compiler_params=pltpu.CompilerParams(vmem_limit_bytes=16 * 1024 * 1024),
        name="finish",
    )(place, both, *others)


def solution(mesh):
    in_specs = (
        P("ka", None, "ga"),
        P("ka", None, "ga"),
        P("ka", None, "ga"),
        P("ga"),
        P("ka", "ga", None),
        P("ka", None),
        P(),
    )
    out_specs = (P("ka", None), P("ka", None))
    return jax.shard_map(
        per_device, mesh=mesh, in_specs=in_specs, out_specs=out_specs, check_vma=False
    )
```

```python
import jax
import jax.numpy as jnp
from jax import lax
from jax.experimental import pallas as pl
from jax.experimental.pallas import tpu as pltpu
from jax.sharding import PartitionSpec as P

CAP = 2
QW = 384
CH = 8
F32 = jnp.float32
BF16 = jnp.bfloat16
NT_DIMS = (((1,), (1,)), ((), ()))


def rank_in_group(owners):
    n = owners.shape[-1]
    same = owners[..., :, None] == owners[..., None, :]
    before = jnp.arange(n)[:, None] > jnp.arange(n)[None, :]
    return jnp.sum(jnp.logical_and(same, before).astype(jnp.int32), axis=-1)


def widen(v):
    return jnp.pad(v, ((0, 0),) * (v.ndim - 1) + ((0, QW - v.shape[-1]),))


def flat_tiles(tmp, rows):
    even = tmp[pl.ds(0, rows // 2, stride=2), :]
    odd = tmp[pl.ds(1, rows // 2, stride=2), :]
    return jnp.concatenate([even, odd], axis=1)


def direct_kernel(plan, big, w, keep, away, xs, ys, us, prod, kept, sent, sx, sy):
    half = prod.shape[0] // CH
    nt = 2 * half
    deep = xs.shape[3]
    nslot = keep.shape[0]
    chunks_first, chunks, parity = plan[3, 0], plan[3, 1], plan[3, 2]

    def x_copy(pos, buf, i):
        return pltpu.make_async_copy(big.at[plan[1, pos], pl.ds(0, nt)], xs.at[buf, i], sx.at[buf, i])

    def y_copy(pos, buf, i):
        return pltpu.make_async_copy(big.at[plan[2, pos], pl.ds(nt, nt)], ys.at[buf, i], sy.at[buf, i])

    def begin(c):
        for i in range(CH):
            x_copy(c * CH + i, lax.rem(c, 2), i).start()
            y_copy(c * CH + i, lax.rem(c, 3), i).start()

    def products(c):
        u = us[lax.rem(c + 2, 2)]
        y = ys[lax.rem(c + 3, 3)].reshape(CH * nt, deep)
        for i in range(0, CH, 4):
            d = lax.dot_general(
                u[half * i : half * (i + 4)],
                y[nt * i : nt * (i + 4)],
                NT_DIMS,
                preferred_element_type=F32,
            )
            for j in range(2):
                prod[half * i + nt * j : half * i + nt * j + nt] = d[
                    nt * j : nt * j + nt, 128 * j : 128 * j + 128
                ]
        lane = lax.broadcasted_iota(jnp.int32, (8, 128), 1)
        for i in range(CH):
            t = jnp.where(c < 0, nslot, plan[0, jnp.maximum(c, 0) * CH + i])
            rows = [prod[half * i + 8 * g : half * i + 8 * g + 8] for g in range(4)]
            tiles = []
            for h in range(2):
                start = nt * (i % 2) + half * h
                moved = [pltpu.roll(v, (half * g - start) % 128, 1) for g, v in enumerate(rows)]
                low = jnp.where(lane < half, moved[0], moved[1])
                high = jnp.where(lane < 3 * half, moved[2], moved[3])
                tiles.append(jnp.where(lane < nt, low, high))
            kept[t] = jnp.where(parity == 0, tiles[0], tiles[1])
            sent[t] = jnp.where(parity == 0, tiles[1], tiles[0])

    @pl.when(chunks > 0)
    def _():
        begin(0)

    def chunk(c, carry):
        @pl.when(c + 1 < chunks)
        def _():
            begin(c + 1)

        bx, by = lax.rem(c, 2), lax.rem(c, 3)
        for i in range(CH):
            x_copy(c * CH + i, bx, i).wait()
            y_copy(c * CH + i, by, i).wait()
        products(c - 1)
        slot = jnp.where(c < chunks_first, 0, 1)
        u = jnp.dot(
            xs[bx, :, :half].reshape(CH * half, deep), w[slot, :deep], preferred_element_type=F32
        )
        u = u + jnp.dot(
            xs[bx, :, half:].reshape(CH * half, deep), w[slot, deep:], preferred_element_type=F32
        )
        us[bx] = u.astype(BF16)
        return carry

    lax.fori_loop(0, chunks, chunk, 0)

    @pl.when(chunks > 0)
    def _():
        products(chunks - 1)

    keep[...] = kept[:nslot]
    away[...] = sent[:nslot]


def route_kernel(tab, keep, came, send, mine, theirs, sem):
    copies = [
        pltpu.make_async_copy(keep, mine, sem.at[0]),
        pltpu.make_async_copy(came, theirs, sem.at[1]),
    ]
    for c in copies:
        c.start()
    nk = send.shape[1] - CAP
    send[:, CAP:] = jnp.zeros((send.shape[0], nk, *send.shape[2:]), F32)
    for c in copies:
        c.wait()
    for t in range(tab.shape[1]):
        v = mine[t] + theirs[t]
        send[t // CAP, t % CAP] = v

        @pl.when(tab[0, t] == 1)
        def _():
            owner = tab[2, t] // nk
            row = CAP + tab[2, t] % nk
            send[owner, row] = send[owner, row] + v


def exchange_kernel(
    tab, own, big, full_in, whi_in, wlo_in, dmat, cw, out, full, whi, wlo, p1, p2, tot, prod, flat, s0, s1, s2
):
    nslot = tab.shape[1]
    npair = own.shape[1]
    nk, rows, wide = tot.shape
    nt = whi_in.shape[0] // nk

    def second(j):
        return pltpu.make_async_copy(big.at[own[1, j]], p2.at[j], s2.at[j])

    def first(t):
        return pltpu.make_async_copy(big.at[tab[6, t]], p1.at[t], s1.at[t])

    loads = [
        pltpu.make_async_copy(whi_in, whi, s0.at[0]),
        pltpu.make_async_copy(wlo_in, wlo, s0.at[1]),
        pltpu.make_async_copy(full_in.at[pl.ds(0, nk * nt)], full, s0.at[2]),
    ]
    for j in range(npair):
        second(j).start()
    for c in loads:
        c.start()

    def begin(t, carry):
        @pl.when(tab[4, t] == 1)
        def _():
            first(t).start()

        return carry

    lax.fori_loop(0, nslot, begin, 0)
    tot[...] = jnp.zeros_like(tot)
    for j in range(npair):
        second(j).wait()
    for c in loads:
        c.wait()

    def contract(left, right):
        return lax.dot_general(left, right, NT_DIMS, preferred_element_type=F32)

    b = p2[...].reshape(npair * rows, wide)
    e = contract(b, whi[...]) + contract(b, wlo[...])
    e = e + e
    for k in range(nk):
        prod[k] = e[:, k * nt : (k + 1) * nt]
    for j in range(npair):
        r = pl.ds(j * rows, rows)
        flat[r, :] = prod[own[0, j], r, :]

    def gather(t, carry):
        @pl.when(tab[4, t] == 1)
        def _():
            first(t).wait()
            k = tab[5, t]
            tot[k] = tot[k] + p1[t].astype(F32)

        return carry

    lax.fori_loop(0, nslot, gather, 0)
    w = tot[...].reshape(nk * rows, wide) * cw[...]
    hi = w.astype(BF16)
    lo = (w - hi.astype(F32)).astype(BF16)
    m = contract(jnp.concatenate([hi, lo], axis=0), full[...])
    m = m[: nk * rows] + m[nk * rows :]
    m = m + m
    for k in range(nk):
        flat[pl.ds((npair + k) * rows, rows), :] = m[
            k * rows : (k + 1) * rows, k * nt : (k + 1) * nt
        ]
    z = flat_tiles(flat, (npair + nk) * rows)
    for j in range(npair + nk):
        out[j] = z[8 * j : 8 * j + 8]


def collect_kernel(own, got, out, here, sem):
    copy = pltpu.make_async_copy(got, here, sem)
    copy.start()
    copy.wait()
    nk = got.shape[1] - CAP
    npair = own.shape[1]
    for j in range(npair):
        out[j] = here[own[2, j], own[3, j]]
    for k in range(nk):
        out[npair + k] = jnp.sum(here[:, CAP + k], axis=0)


def bring(place, refs, whole, sem):
    copies = [
        pltpu.make_async_copy(r, whole.at[place[i]], sem.at[i]) for i, r in enumerate(refs)
    ]
    for c in copies:
        c.start()
    for c in copies:
        c.wait()


def arrange_kernel(place, r0, r1, r2, r3, dmat, whole, sem):
    bring(place, (r0, r1, r2, r3), whole, sem)
    half = dmat.shape[1] // 2
    for j in range(dmat.shape[0]):
        for a in range(2):
            left, right = whole[2 * a, j], whole[2 * a + 1, j]
            for g in range(4):
                cut = slice(half * g, half * (g + 1))
                dmat[j, pl.ds(half * a + 8 * g, 8), :] = jnp.concatenate(
                    [left[:, cut], right[:, cut]], axis=1
                )


def finish_kernel(place, dmat, r0, r1, r2, r3, blocks, mirrored, whole, emat, bmat, rows, sem):
    bring(place, (r0, r1, r2, r3), whole, sem)
    npair, nk = blocks.shape[0], mirrored.shape[0]
    nt = dmat.shape[1]
    half = nt // 2
    n = npair + nk
    for j in range(n):
        for a in range(4):
            tile = whole[a, j]
            emat[j, pl.ds(16 * a, 8, stride=2), :] = tile[:, :nt]
            emat[j, pl.ds(16 * a + 1, 8, stride=2), :] = tile[:, nt:]
    for j in range(n):
        if j < npair:
            bmat[j] = emat[j].T - dmat[j]
        else:
            bmat[j] = (emat[j] - dmat[j]).T
        even = bmat[j, pl.ds(0, half, stride=2), :]
        odd = bmat[j, pl.ds(1, half, stride=2), :]
        rows[pl.ds(j * half, half), :] = jnp.concatenate([even, odd], axis=1)
    for r in range(half):
        lanes = pl.ds(2 * nt * r, 2 * nt)
        blocks[:, lanes] = rows[pl.ds(r, npair, stride=half), :]
        mirrored[:, lanes] = rows[pl.ds(npair * half + r, nk, stride=half), :]


def in_vmem(count):
    return [pl.BlockSpec(memory_space=pltpu.VMEM)] * count


SMEM = pl.BlockSpec(memory_space=pltpu.SMEM)
ANY = pl.BlockSpec(memory_space=pl.ANY)


def per_device(x, y, p, coulomb, w, pairs, q_slot):
    n_ka = lax.axis_size("ka")
    me = lax.axis_index("ka")
    a = lax.axis_index("ga")
    nk, nt, gl = x.shape
    qs = w.shape[0]
    npair = pairs.shape[0]
    nslot = n_ka * CAP

    half, rows = nt // 2, nt // 4

    def shift(r):
        return [(i, (i + r) % 4) for i in range(4)]

    with jax.named_scope("pack"):
        y_far = lax.ppermute(y, "ga", [(i, 3 - i) for i in range(4)])
        cut = [jnp.where((a + r) % 4 < 2, x[:, :half], x[:, half:]) for r in range(4)]
        cut = cut[:1] + [lax.ppermute(cut[r], "ga", shift(r)) for r in range(1, 4)]

        def side(left, right):
            return jnp.concatenate([widen(left), widen(right)], axis=2)

        payload = jnp.concatenate(
            [side(cut[0], cut[1]), side(cut[2], cut[3]), side(y, y_far)], axis=1
        )
    with jax.named_scope("spread"):
        big = lax.all_gather(payload, "ka", axis=0, tiled=True)

    with jax.named_scope("weights"):
        cols = [
            jnp.pad(w[:, :, i * gl : (i + 1) * gl], ((0, 0), (0, QW - gl), (0, QW - gl)))
            for i in range(4)
        ]
        wk = []
        for r in range(4):
            to = (a + r) % 4
            left = jnp.where(
                to < 2, jnp.where(to == 0, cols[0], cols[1]), jnp.where(to == 2, cols[2], cols[3])
            )
            right = jnp.where(
                to < 2, jnp.where(to == 0, cols[3], cols[2]), jnp.where(to == 2, cols[1], cols[0])
            )
            v = jnp.concatenate([left, right], axis=2)
            wk.append(lax.ppermute(v, "ga", shift(r)) if r else v)
        wk = jnp.concatenate(wk, axis=1)

    with jax.named_scope("exchange_pack"):
        c1 = lax.reduce_precision(coulomb, 8, 7)
        c2 = lax.reduce_precision(coulomb - c1, 8, 7)
        c3 = coulomb - c1 - c2
        pieces = jnp.pad(jnp.stack([c1, c2, c3]).astype(BF16), ((0, 13), (0, 0)))
        held = jnp.concatenate([p.reshape(nk * nt, gl), pieces], axis=0)
        full = lax.all_gather(widen(held), "ga", axis=1, tiled=True)
        p_rows = full[: nk * nt].reshape(nk, nt, 4 * QW)
        p_rows = lax.dynamic_slice_in_dim(p_rows, a * rows, rows, axis=1)
        p_big = lax.all_gather(p_rows, "ka", axis=0, tiled=True)
        c_full = jnp.sum(full[nk * nt : nk * nt + 3].astype(F32), axis=0, keepdims=True)
        weighted = full[: nk * nt].astype(F32) * c_full
        w_hi = lax.reduce_precision(weighted, 8, 7)
        w_lo = (weighted - w_hi).astype(BF16)
        w_hi = w_hi.astype(BF16)

    with jax.named_scope("tables"):
        every = lax.all_gather(pairs, "ka", axis=0, tiled=True).reshape(n_ka, npair, 3)

        def routes(rows):
            slot = jnp.sum(
                jnp.where(
                    rows[..., 2, None] == jnp.arange(q_slot.shape[0]), q_slot, 0
                ),
                axis=-1,
            )
            q_owner = slot // qs
            k_owner = rows[..., 1] // nk
            return slot % qs, q_owner, rank_in_group(q_owner), k_owner, rank_in_group(k_owner)

        local, q_owner, q_rank, k_owner, k_rank = routes(every)
        ranks = jnp.arange(CAP)
        hot_q = (q_owner == me)[..., None] & (q_rank[..., None] == ranks)
        hot_k = (k_owner == me)[..., None] & (k_rank[..., None] == ranks)

        def pick(hot, v):
            return jnp.sum(jnp.where(hot, v[..., None], 0), axis=1).reshape(nslot)

        ones = jnp.ones_like(local)
        tab = jnp.stack(
            [
                pick(hot_q, ones),
                pick(hot_q, every[..., 0]),
                pick(hot_q, every[..., 1]),
                pick(hot_q, local),
                pick(hot_k, ones),
                pick(hot_k, every[..., 1] - me * nk),
                pick(hot_k, every[..., 0]),
            ]
        )
        _, o1, r1, _, _ = routes(pairs)
        own = jnp.stack([pairs[:, 0] - me * nk, pairs[:, 1], o1, r1])

    with jax.named_scope("plan"):
        npos = nslot + qs * CH
        used, slot = tab[0], tab[3]
        same = (slot[:, None] == slot[None, :]) & (used[None, :] == 1)
        order = jnp.arange(nslot)
        rank = jnp.sum((same & (order[:, None] > order[None, :])).astype(jnp.int32), axis=1)
        first = jnp.sum(used * (slot == 0))
        second = jnp.sum(used * (slot == 1))
        chunks_first = (first + CH - 1) // CH
        chunks = chunks_first + (second + CH - 1) // CH
        pos = jnp.where(slot == 0, rank, chunks_first * CH + rank)
        hot = (pos[None, :] == jnp.arange(npos)[:, None]) & (used == 1)[None, :]

        def at_pos(v):
            return jnp.sum(jnp.where(hot, v[None, :], 0), axis=1)

        heads = jnp.pad(jnp.stack([chunks_first, chunks, a % 2]), (0, npos - 3))
        plan = jnp.stack([at_pos(order - nslot) + nslot, at_pos(tab[1]), at_pos(tab[2]), heads])
    keep, away = pl.pallas_call(
        direct_kernel,
        out_shape=(jax.ShapeDtypeStruct((nslot, 8, 128), F32),) * 2,
        in_specs=[SMEM, ANY, *in_vmem(1)],
        out_specs=tuple(in_vmem(2)),
        scratch_shapes=[
            pltpu.VMEM((2, CH, nt, 2 * QW), BF16),
            pltpu.VMEM((3, CH, nt, 2 * QW), BF16),
            pltpu.VMEM((2, CH * half, 2 * QW), BF16),
            pltpu.VMEM((CH * half, 128), F32),
            pltpu.VMEM((nslot + 1, 8, 128), F32),
            pltpu.VMEM((nslot + 1, 8, 128), F32),
            pltpu.SemaphoreType.DMA((2, CH)),
            pltpu.SemaphoreType.DMA((3, CH)),
        ],
        compiler_params=pltpu.CompilerParams(vmem_limit_bytes=32 * 1024 * 1024),
        name="direct",
    )(plan, big, wk)
    with jax.named_scope("to_neighbour"):
        came = lax.ppermute(away, "ga", [(0, 1), (1, 0), (2, 3), (3, 2)])
    send = pl.pallas_call(
        route_kernel,
        out_shape=jax.ShapeDtypeStruct((n_ka, CAP + nk, 8, 128), F32),
        in_specs=[SMEM, ANY, ANY],
        out_specs=pl.BlockSpec(memory_space=pltpu.VMEM),
        scratch_shapes=[
            pltpu.VMEM((nslot, 8, 128), F32),
            pltpu.VMEM((nslot, 8, 128), F32),
            pltpu.SemaphoreType.DMA((2,)),
        ],
        compiler_params=pltpu.CompilerParams(vmem_limit_bytes=8 * 1024 * 1024),
        name="route",
    )(tab, keep, came)
    with jax.named_scope("to_holders"):
        got = lax.all_to_all(send, "ka", 0, 0, tiled=True)
    n = npair + nk
    mine = pl.pallas_call(
        collect_kernel,
        out_shape=jax.ShapeDtypeStruct((n, 8, 128), F32),
        in_specs=[SMEM, ANY],
        out_specs=pl.BlockSpec(memory_space=pltpu.VMEM),
        scratch_shapes=[pltpu.VMEM(send.shape, F32), pltpu.SemaphoreType.DMA],
        compiler_params=pltpu.CompilerParams(vmem_limit_bytes=8 * 1024 * 1024),
        name="collect",
    )(own, got)
    with jax.named_scope("direct_copies"):
        others = [lax.ppermute(mine, "ga", shift(r)) for r in range(1, 4)]
        place = jnp.stack([(a - r) % 4 for r in range(4)])
    dmat = pl.pallas_call(
        arrange_kernel,
        out_shape=jax.ShapeDtypeStruct((n, nt, nt), F32),
        in_specs=[SMEM, ANY, ANY, ANY, ANY],
        out_specs=pl.BlockSpec(memory_space=pltpu.VMEM),
        scratch_shapes=[pltpu.VMEM((4, n, 8, 128), F32), pltpu.SemaphoreType.DMA((4,))],
        compiler_params=pltpu.CompilerParams(vmem_limit_bytes=8 * 1024 * 1024),
        name="arrange",
    )(place, mine, *others)
    exch = pl.pallas_call(
        exchange_kernel,
        out_shape=jax.ShapeDtypeStruct((n, 8, 128), F32),
        in_specs=[SMEM, SMEM, ANY, ANY, ANY, ANY, ANY, *in_vmem(1)],
        out_specs=pl.BlockSpec(memory_space=pltpu.VMEM),
        scratch_shapes=[
            pltpu.VMEM((nk * nt, 4 * QW), BF16),
            pltpu.VMEM((nk * nt, 4 * QW), BF16),
            pltpu.VMEM((nk * nt, 4 * QW), BF16),
            pltpu.VMEM((nslot, rows, 4 * QW), BF16),
            pltpu.VMEM((npair, rows, 4 * QW), BF16),
            pltpu.VMEM((nk, rows, 4 * QW), F32),
            pltpu.VMEM((nk, npair * rows, nt), F32),
            pltpu.VMEM((n * rows, nt), F32),
            pltpu.SemaphoreType.DMA((3,)),
            pltpu.SemaphoreType.DMA((nslot,)),
            pltpu.SemaphoreType.DMA((npair,)),
        ],
        compiler_params=pltpu.CompilerParams(vmem_limit_bytes=60 * 1024 * 1024),
        name="exchange",
    )(tab, own, p_big, full, w_hi, w_lo, dmat, c_full)
    with jax.named_scope("exchange_copies"):
        others = [lax.ppermute(exch, "ga", shift(r)) for r in range(1, 4)]
    return pl.pallas_call(
        finish_kernel,
        out_shape=(
            jax.ShapeDtypeStruct((npair, nt * nt), F32),
            jax.ShapeDtypeStruct((nk, nt * nt), F32),
        ),
        in_specs=[SMEM, *in_vmem(1), ANY, ANY, ANY, ANY],
        out_specs=tuple(in_vmem(2)),
        scratch_shapes=[
            pltpu.VMEM((4, n, 8, 128), F32),
            pltpu.VMEM((n, nt, nt), F32),
            pltpu.VMEM((n, nt, nt), F32),
            pltpu.VMEM((n * half, 2 * nt), F32),
            pltpu.SemaphoreType.DMA((4,)),
        ],
        compiler_params=pltpu.CompilerParams(vmem_limit_bytes=16 * 1024 * 1024),
        name="finish",
    )(place, dmat, exch, *others)


def solution(mesh):
    in_specs = (
        P("ka", None, "ga"),
        P("ka", None, "ga"),
        P("ka", None, "ga"),
        P("ga"),
        P("ka", "ga", None),
        P("ka", None),
        P(),
    )
    out_specs = (P("ka", None), P("ka", None))
    return jax.shard_map(
        per_device, mesh=mesh, in_specs=in_specs, out_specs=out_specs, check_vma=False
    )
```

```python
import jax
import jax.numpy as jnp
from jax import lax
from jax.experimental import pallas as pl
from jax.experimental.pallas import tpu as pltpu
from jax.sharding import PartitionSpec as P

CAP = 2
QW = 384
CH = 8
F32 = jnp.float32
BF16 = jnp.bfloat16
NT_DIMS = (((1,), (1,)), ((), ()))


def rank_in_group(owners):
    n = owners.shape[-1]
    same = owners[..., :, None] == owners[..., None, :]
    before = jnp.arange(n)[:, None] > jnp.arange(n)[None, :]
    return jnp.sum(jnp.logical_and(same, before).astype(jnp.int32), axis=-1)


def widen(v):
    return jnp.pad(v, ((0, 0),) * (v.ndim - 1) + ((0, QW - v.shape[-1]),))


def flat_tiles(tmp, rows):
    even = tmp[pl.ds(0, rows // 2, stride=2), :]
    odd = tmp[pl.ds(1, rows // 2, stride=2), :]
    return jnp.concatenate([even, odd], axis=1)


def direct_kernel(plan, big, w, keep, away, xs, ys, us, prod, kept, sent, sx, sy):
    half = prod.shape[0] // CH
    nt = 2 * half
    deep = xs.shape[3]
    nslot = keep.shape[0]
    chunks_first, chunks, parity = plan[3, 0], plan[3, 1], plan[3, 2]

    def x_copy(pos, buf, i):
        return pltpu.make_async_copy(big.at[plan[1, pos], pl.ds(0, nt)], xs.at[buf, i], sx.at[buf, i])

    def y_copy(pos, buf, i):
        return pltpu.make_async_copy(big.at[plan[2, pos], pl.ds(nt, nt)], ys.at[buf, i], sy.at[buf, i])

    def begin(c):
        for i in range(CH):
            x_copy(c * CH + i, lax.rem(c, 2), i).start()
            y_copy(c * CH + i, lax.rem(c, 3), i).start()

    def products(c):
        u = us[lax.rem(c + 2, 2)]
        y = ys[lax.rem(c + 3, 3)].reshape(CH * nt, deep)
        for i in range(0, CH, 4):
            d = lax.dot_general(
                u[half * i : half * (i + 4)],
                y[nt * i : nt * (i + 4)],
                NT_DIMS,
                preferred_element_type=F32,
            )
            for j in range(2):
                prod[half * i + nt * j : half * i + nt * j + nt] = d[
                    nt * j : nt * j + nt, 128 * j : 128 * j + 128
                ]
        lane = lax.broadcasted_iota(jnp.int32, (8, 128), 1)
        for i in range(CH):
            t = jnp.where(c < 0, nslot, plan[0, jnp.maximum(c, 0) * CH + i])
            rows = [prod[half * i + 8 * g : half * i + 8 * g + 8] for g in range(4)]
            tiles = []
            for h in range(2):
                start = nt * (i % 2) + half * h
                moved = [pltpu.roll(v, (half * g - start) % 128, 1) for g, v in enumerate(rows)]
                low = jnp.where(lane < half, moved[0], moved[1])
                high = jnp.where(lane < 3 * half, moved[2], moved[3])
                tiles.append(jnp.where(lane < nt, low, high))
            kept[t] = jnp.where(parity == 0, tiles[0], tiles[1])
            sent[t] = jnp.where(parity == 0, tiles[1], tiles[0])

    @pl.when(chunks > 0)
    def _():
        begin(0)

    def chunk(c, carry):
        @pl.when(c + 1 < chunks)
        def _():
            begin(c + 1)

        bx, by = lax.rem(c, 2), lax.rem(c, 3)
        for i in range(CH):
            x_copy(c * CH + i, bx, i).wait()
            y_copy(c * CH + i, by, i).wait()
        products(c - 1)
        slot = jnp.where(c < chunks_first, 0, 1)
        u = jnp.dot(
            xs[bx, :, :half].reshape(CH * half, deep), w[slot, :deep], preferred_element_type=F32
        )
        u = u + jnp.dot(
            xs[bx, :, half:].reshape(CH * half, deep), w[slot, deep:], preferred_element_type=F32
        )
        us[bx] = u.astype(BF16)
        return carry

    lax.fori_loop(0, chunks, chunk, 0)

    @pl.when(chunks > 0)
    def _():
        products(chunks - 1)

    keep[...] = kept[:nslot]
    away[...] = sent[:nslot]


def route_kernel(tab, keep, came, send, mine, theirs, sem):
    copies = [
        pltpu.make_async_copy(keep, mine, sem.at[0]),
        pltpu.make_async_copy(came, theirs, sem.at[1]),
    ]
    for c in copies:
        c.start()
    nk = send.shape[1] - CAP
    send[:, CAP:] = jnp.zeros((send.shape[0], nk, *send.shape[2:]), F32)
    for c in copies:
        c.wait()
    for t in range(tab.shape[1]):
        v = mine[t] + theirs[t]
        send[t // CAP, t % CAP] = v

        @pl.when(tab[0, t] == 1)
        def _():
            owner = tab[2, t] // nk
            row = CAP + tab[2, t] % nk
            send[owner, row] = send[owner, row] + v


def exchange_kernel(
    firsts, own, big, full_in, whi_in, wlo_in, early, late, cw, out, full, whi, wlo, p1, p2, tot, prod, flat, s0, s1, s2
):
    count = firsts[2, 0]
    npair = own.shape[1]
    nk, rows, wide = tot.shape
    nt = whi_in.shape[0] // nk

    def second(j):
        return pltpu.make_async_copy(big.at[own[1, j]], p2.at[j], s2.at[j])

    def first(t):
        return pltpu.make_async_copy(big.at[firsts[0, t]], p1.at[t], s1.at[t])

    loads = [
        pltpu.make_async_copy(whi_in, whi, s0.at[0]),
        pltpu.make_async_copy(wlo_in, wlo, s0.at[1]),
        pltpu.make_async_copy(full_in.at[pl.ds(0, nk * nt)], full, s0.at[2]),
    ]
    for j in range(npair):
        second(j).start()
    for c in loads:
        c.start()

    def begin(t, carry):
        first(t).start()
        return carry

    lax.fori_loop(0, count, begin, 0)
    tot[...] = jnp.zeros_like(tot)
    for j in range(npair):
        second(j).wait()
    for c in loads:
        c.wait()

    def contract(left, right):
        return lax.dot_general(left, right, NT_DIMS, preferred_element_type=F32)

    b = p2[...].reshape(npair * rows, wide)
    e = contract(b, whi[...]) + contract(b, wlo[...])
    e = e + e
    for k in range(nk):
        prod[k] = e[:, k * nt : (k + 1) * nt]
    for j in range(npair):
        r = pl.ds(j * rows, rows)
        flat[r, :] = prod[own[0, j], r, :]

    def gather(t, carry):
        first(t).wait()
        k = firsts[1, t]
        tot[k] = tot[k] + p1[t].astype(F32)
        return carry

    lax.fori_loop(0, count, gather, 0)
    w = tot[...].reshape(nk * rows, wide) * cw[...]
    hi = w.astype(BF16)
    lo = (w - hi.astype(F32)).astype(BF16)
    m = contract(jnp.concatenate([hi, lo], axis=0), full[...])
    m = m[: nk * rows] + m[nk * rows :]
    m = m + m
    for k in range(nk):
        flat[pl.ds((npair + k) * rows, rows), :] = m[
            k * rows : (k + 1) * rows, k * nt : (k + 1) * nt
        ]
    z = flat_tiles(flat, (npair + nk) * rows)
    for j in range(npair + nk):
        out[j] = z[8 * j : 8 * j + 8]


def collect_kernel(own, got, out, here, sem):
    copy = pltpu.make_async_copy(got, here, sem)
    copy.start()
    copy.wait()
    nk = got.shape[1] - CAP
    npair = own.shape[1]
    for j in range(npair):
        out[j] = here[own[2, j], own[3, j]]
    for k in range(nk):
        out[npair + k] = jnp.sum(here[:, CAP + k], axis=0)


def bring(place, refs, whole, sem):
    copies = [
        pltpu.make_async_copy(r, whole.at[place[i]], sem.at[i]) for i, r in enumerate(refs)
    ]
    for c in copies:
        c.start()
    for c in copies:
        c.wait()


def arrange_kernel(place, r0, r1, r2, r3, dmat, whole, sem):
    bring(place, (r0, r1, r2, r3), whole, sem)
    half = dmat.shape[1] // 2
    for j in range(dmat.shape[0]):
        for a in range(2):
            left, right = whole[2 * a, j], whole[2 * a + 1, j]
            for g in range(4):
                cut = slice(half * g, half * (g + 1))
                dmat[j, pl.ds(half * a + 8 * g, 8), :] = jnp.concatenate(
                    [left[:, cut], right[:, cut]], axis=1
                )


def finish_kernel(place, dmat, r0, r1, r2, r3, blocks, mirrored, whole, emat, bmat, rows, sem):
    bring(place, (r0, r1, r2, r3), whole, sem)
    npair, nk = blocks.shape[0], mirrored.shape[0]
    nt = dmat.shape[1]
    half = nt // 2
    n = npair + nk
    for j in range(n):
        for a in range(4):
            tile = whole[a, j]
            emat[j, pl.ds(16 * a, 8, stride=2), :] = tile[:, :nt]
            emat[j, pl.ds(16 * a + 1, 8, stride=2), :] = tile[:, nt:]
    for j in range(n):
        if j < npair:
            bmat[j] = emat[j].T - dmat[j]
        else:
            bmat[j] = (emat[j] - dmat[j]).T
        even = bmat[j, pl.ds(0, half, stride=2), :]
        odd = bmat[j, pl.ds(1, half, stride=2), :]
        rows[pl.ds(j * half, half), :] = jnp.concatenate([even, odd], axis=1)
    for r in range(half):
        lanes = pl.ds(2 * nt * r, 2 * nt)
        blocks[:, lanes] = rows[pl.ds(r, npair, stride=half), :]
        mirrored[:, lanes] = rows[pl.ds(npair * half + r, nk, stride=half), :]


def in_vmem(count):
    return [pl.BlockSpec(memory_space=pltpu.VMEM)] * count


SMEM = pl.BlockSpec(memory_space=pltpu.SMEM)
ANY = pl.BlockSpec(memory_space=pl.ANY)


def per_device(x, y, p, coulomb, w, pairs, q_slot):
    n_ka = lax.axis_size("ka")
    me = lax.axis_index("ka")
    a = lax.axis_index("ga")
    nk, nt, gl = x.shape
    qs = w.shape[0]
    npair = pairs.shape[0]
    nslot = n_ka * CAP

    half, rows = nt // 2, nt // 4

    def shift(r):
        return [(i, (i + r) % 4) for i in range(4)]

    with jax.named_scope("pack"):
        y_far = lax.ppermute(y, "ga", [(i, 3 - i) for i in range(4)])
        cut = [jnp.where((a + r) % 4 < 2, x[:, :half], x[:, half:]) for r in range(4)]
        cut = cut[:1] + [lax.ppermute(cut[r], "ga", shift(r)) for r in range(1, 4)]

        def side(left, right):
            return jnp.concatenate([widen(left), widen(right)], axis=2)

        y_both = side(jnp.where(a < 2, y, y_far), jnp.where(a < 2, y_far, y))
        payload = jnp.concatenate([side(cut[0], cut[1]), side(cut[2], cut[3]), y_both], axis=1)
    with jax.named_scope("spread"):
        big = lax.all_gather(payload, "ka", axis=0, tiled=True)

    with jax.named_scope("weights"):
        cols = [
            jnp.pad(w[:, :, i * gl : (i + 1) * gl], ((0, 0), (0, QW - gl), (0, QW - gl)))
            for i in range(4)
        ]
        outer = jnp.concatenate([cols[0], cols[3]], axis=2)
        inner = jnp.concatenate([cols[1], cols[2]], axis=2)
        wk = []
        for r in range(4):
            to = (a + r) % 4
            v = jnp.where((to == 0) | (to == 3), outer, inner)
            wk.append(lax.ppermute(v, "ga", shift(r)) if r else v)
        wk = jnp.concatenate(wk, axis=1)

    with jax.named_scope("exchange_pack"):
        c1 = lax.reduce_precision(coulomb, 8, 7)
        c2 = lax.reduce_precision(coulomb - c1, 8, 7)
        c3 = coulomb - c1 - c2
        pieces = jnp.pad(jnp.stack([c1, c2, c3]).astype(BF16), ((0, 13), (0, 0)))
        held = jnp.concatenate([p.reshape(nk * nt, gl), pieces], axis=0)
        full = lax.all_gather(widen(held), "ga", axis=1, tiled=True)
        p_rows = full[: nk * nt].reshape(nk, nt, 4 * QW)
        p_rows = lax.dynamic_slice_in_dim(p_rows, a * rows, rows, axis=1)
        p_big = lax.all_gather(p_rows, "ka", axis=0, tiled=True)
        c_full = jnp.sum(full[nk * nt : nk * nt + 3].astype(F32), axis=0, keepdims=True)
        weighted = full[: nk * nt].astype(F32) * c_full
        w_hi = lax.reduce_precision(weighted, 8, 7)
        w_lo = (weighted - w_hi).astype(BF16)
        w_hi = w_hi.astype(BF16)

    with jax.named_scope("tables"):
        every = lax.all_gather(pairs, "ka", axis=0, tiled=True).reshape(n_ka, npair, 3)

        def routes(rows):
            slot = jnp.sum(
                jnp.where(
                    rows[..., 2, None] == jnp.arange(q_slot.shape[0]), q_slot, 0
                ),
                axis=-1,
            )
            q_owner = slot // qs
            k_owner = rows[..., 1] // nk
            return slot % qs, q_owner, rank_in_group(q_owner), k_owner, rank_in_group(k_owner)

        local, q_owner, q_rank, k_owner, k_rank = routes(every)
        ranks = jnp.arange(CAP)
        hot_q = (q_owner == me)[..., None] & (q_rank[..., None] == ranks)
        hot_k = (k_owner == me)[..., None] & (k_rank[..., None] == ranks)

        def pick(hot, v):
            return jnp.sum(jnp.where(hot, v[..., None], 0), axis=1).reshape(nslot)

        ones = jnp.ones_like(local)
        tab = jnp.stack(
            [
                pick(hot_q, ones),
                pick(hot_q, every[..., 0]),
                pick(hot_q, every[..., 1]),
                pick(hot_q, local),
                pick(hot_k, ones),
                pick(hot_k, every[..., 1] - me * nk),
                pick(hot_k, every[..., 0]),
            ]
        )
        _, o1, r1, _, _ = routes(pairs)
        own = jnp.stack([pairs[:, 0] - me * nk, pairs[:, 1], o1, r1])

    with jax.named_scope("plan"):
        npos = nslot + qs * CH
        used, slot = tab[0], tab[3]
        same = (slot[:, None] == slot[None, :]) & (used[None, :] == 1)
        order = jnp.arange(nslot)
        rank = jnp.sum((same & (order[:, None] > order[None, :])).astype(jnp.int32), axis=1)
        first = jnp.sum(used * (slot == 0))
        second = jnp.sum(used * (slot == 1))
        chunks_first = (first + CH - 1) // CH
        chunks = chunks_first + (second + CH - 1) // CH
        pos = jnp.where(slot == 0, rank, chunks_first * CH + rank)
        hot = (pos[None, :] == jnp.arange(npos)[:, None]) & (used == 1)[None, :]

        def at_pos(v, hot):
            return jnp.sum(jnp.where(hot, v[None, :], 0), axis=1)

        heads = jnp.pad(jnp.stack([chunks_first, chunks, a % 2]), (0, npos - 3))
        plan = jnp.stack(
            [at_pos(order - nslot, hot) + nslot, at_pos(tab[1], hot), at_pos(tab[2], hot), heads]
        )
        named = tab[4]
        rank = jnp.sum(jnp.where(order[:, None] > order[None, :], named[None, :], 0), axis=1)
        hot = (rank[None, :] == order[:, None]) & (named == 1)[None, :]
        total = jnp.broadcast_to(jnp.sum(named), (nslot,))
        firsts = jnp.stack([at_pos(tab[6], hot), at_pos(tab[5], hot), total])
    keep, away = pl.pallas_call(
        direct_kernel,
        out_shape=(jax.ShapeDtypeStruct((nslot, 8, 128), F32),) * 2,
        in_specs=[SMEM, ANY, *in_vmem(1)],
        out_specs=tuple(in_vmem(2)),
        scratch_shapes=[
            pltpu.VMEM((2, CH, nt, 2 * QW), BF16),
            pltpu.VMEM((3, CH, nt, 2 * QW), BF16),
            pltpu.VMEM((2, CH * half, 2 * QW), BF16),
            pltpu.VMEM((CH * half, 128), F32),
            pltpu.VMEM((nslot + 1, 8, 128), F32),
            pltpu.VMEM((nslot + 1, 8, 128), F32),
            pltpu.SemaphoreType.DMA((2, CH)),
            pltpu.SemaphoreType.DMA((3, CH)),
        ],
        compiler_params=pltpu.CompilerParams(vmem_limit_bytes=32 * 1024 * 1024),
        name="direct",
    )(plan, big, wk)
    with jax.named_scope("to_neighbour"):
        came = lax.ppermute(away, "ga", [(0, 1), (1, 0), (2, 3), (3, 2)])
    send = pl.pallas_call(
        route_kernel,
        out_shape=jax.ShapeDtypeStruct((n_ka, CAP + nk, 8, 128), F32),
        in_specs=[SMEM, ANY, ANY],
        out_specs=pl.BlockSpec(memory_space=pltpu.VMEM),
        scratch_shapes=[
            pltpu.VMEM((nslot, 8, 128), F32),
            pltpu.VMEM((nslot, 8, 128), F32),
            pltpu.SemaphoreType.DMA((2,)),
        ],
        compiler_params=pltpu.CompilerParams(vmem_limit_bytes=8 * 1024 * 1024),
        name="route",
    )(tab, keep, came)
    with jax.named_scope("to_holders"):
        got = lax.all_to_all(send, "ka", 0, 0, tiled=True)
    n = npair + nk
    mine = pl.pallas_call(
        collect_kernel,
        out_shape=jax.ShapeDtypeStruct((n, 8, 128), F32),
        in_specs=[SMEM, ANY],
        out_specs=pl.BlockSpec(memory_space=pltpu.VMEM),
        scratch_shapes=[pltpu.VMEM(send.shape, F32), pltpu.SemaphoreType.DMA],
        compiler_params=pltpu.CompilerParams(vmem_limit_bytes=8 * 1024 * 1024),
        name="collect",
    )(own, got)
    with jax.named_scope("direct_copies"):
        others = [lax.ppermute(mine, "ga", shift(r)) for r in range(1, 4)]
        place = jnp.stack([(a - r) % 4 for r in range(4)])
    dmat = pl.pallas_call(
        arrange_kernel,
        out_shape=jax.ShapeDtypeStruct((n, nt, nt), F32),
        in_specs=[SMEM, ANY, ANY, ANY, ANY],
        out_specs=pl.BlockSpec(memory_space=pltpu.VMEM),
        scratch_shapes=[pltpu.VMEM((4, n, 8, 128), F32), pltpu.SemaphoreType.DMA((4,))],
        compiler_params=pltpu.CompilerParams(vmem_limit_bytes=8 * 1024 * 1024),
        name="arrange",
    )(place, mine, *others)
    exch = pl.pallas_call(
        exchange_kernel,
        out_shape=jax.ShapeDtypeStruct((n, 8, 128), F32),
        in_specs=[SMEM, SMEM, ANY, ANY, ANY, ANY, ANY, ANY, *in_vmem(1)],
        out_specs=pl.BlockSpec(memory_space=pltpu.VMEM),
        scratch_shapes=[
            pltpu.VMEM((nk * nt, 4 * QW), BF16),
            pltpu.VMEM((nk * nt, 4 * QW), BF16),
            pltpu.VMEM((nk * nt, 4 * QW), BF16),
            pltpu.VMEM((nslot, rows, 4 * QW), BF16),
            pltpu.VMEM((npair, rows, 4 * QW), BF16),
            pltpu.VMEM((nk, rows, 4 * QW), F32),
            pltpu.VMEM((nk, npair * rows, nt), F32),
            pltpu.VMEM((n * rows, nt), F32),
            pltpu.SemaphoreType.DMA((3,)),
            pltpu.SemaphoreType.DMA((nslot,)),
            pltpu.SemaphoreType.DMA((npair,)),
        ],
        compiler_params=pltpu.CompilerParams(vmem_limit_bytes=50 * 1024 * 1024),
        name="exchange",
    )(firsts, own, p_big, full, w_hi, w_lo, others[0], others[2], c_full)
    with jax.named_scope("exchange_copies"):
        exch_others = [lax.ppermute(exch, "ga", shift(r)) for r in range(1, 4)]
    return pl.pallas_call(
        finish_kernel,
        out_shape=(
            jax.ShapeDtypeStruct((npair, nt * nt), F32),
            jax.ShapeDtypeStruct((nk, nt * nt), F32),
        ),
        in_specs=[SMEM, *in_vmem(2), ANY, ANY, ANY],
        out_specs=tuple(in_vmem(2)),
        scratch_shapes=[
            pltpu.VMEM((4, n, 8, 128), F32),
            pltpu.VMEM((n, nt, nt), F32),
            pltpu.VMEM((n, nt, nt), F32),
            pltpu.VMEM((n * half, 2 * nt), F32),
            pltpu.SemaphoreType.DMA((4,)),
        ],
        compiler_params=pltpu.CompilerParams(vmem_limit_bytes=16 * 1024 * 1024),
        name="finish",
    )(place, dmat, exch, *exch_others)


def solution(mesh):
    in_specs = (
        P("ka", None, "ga"),
        P("ka", None, "ga"),
        P("ka", None, "ga"),
        P("ga"),
        P("ka", "ga", None),
        P("ka", None),
        P(),
    )
    out_specs = (P("ka", None), P("ka", None))
    return jax.shard_map(
        per_device, mesh=mesh, in_specs=in_specs, out_specs=out_specs, check_vma=False
    )
```

```python
import jax
import jax.numpy as jnp
from jax import lax
from jax.experimental import pallas as pl
from jax.experimental.pallas import tpu as pltpu
from jax.sharding import PartitionSpec as P

CAP = 2
QW = 384
CH = 8
F32 = jnp.float32
BF16 = jnp.bfloat16
NT_DIMS = (((1,), (1,)), ((), ()))


def rank_in_group(owners):
    n = owners.shape[-1]
    same = owners[..., :, None] == owners[..., None, :]
    before = jnp.arange(n)[:, None] > jnp.arange(n)[None, :]
    return jnp.sum(jnp.logical_and(same, before).astype(jnp.int32), axis=-1)


def widen(v):
    return jnp.pad(v, ((0, 0),) * (v.ndim - 1) + ((0, QW - v.shape[-1]),))


def flat_tiles(tmp, rows):
    even = tmp[pl.ds(0, rows // 2, stride=2), :]
    odd = tmp[pl.ds(1, rows // 2, stride=2), :]
    return jnp.concatenate([even, odd], axis=1)


def direct_kernel(plan, big, w, keep, away, xs, ys, us, prod, kept, sent, sx, sy):
    half = prod.shape[0] // CH
    nt = 2 * half
    deep = xs.shape[3]
    nslot = keep.shape[0]
    chunks_first, chunks, parity = plan[3, 0], plan[3, 1], plan[3, 2]

    def x_copy(pos, buf, i):
        return pltpu.make_async_copy(big.at[plan[1, pos], pl.ds(0, nt)], xs.at[buf, i], sx.at[buf, i])

    def y_copy(pos, buf, i):
        return pltpu.make_async_copy(big.at[plan[2, pos], pl.ds(nt, nt)], ys.at[buf, i], sy.at[buf, i])

    def begin(c):
        for i in range(CH):
            x_copy(c * CH + i, lax.rem(c, 2), i).start()
            y_copy(c * CH + i, lax.rem(c, 3), i).start()

    def products(c):
        u = us[lax.rem(c + 2, 2)]
        y = ys[lax.rem(c + 3, 3)].reshape(CH * nt, deep)
        for i in range(0, CH, 4):
            d = lax.dot_general(
                u[half * i : half * (i + 4)],
                y[nt * i : nt * (i + 4)],
                NT_DIMS,
                preferred_element_type=F32,
            )
            for j in range(2):
                prod[half * i + nt * j : half * i + nt * j + nt] = d[
                    nt * j : nt * j + nt, 128 * j : 128 * j + 128
                ]
        lane = lax.broadcasted_iota(jnp.int32, (8, 128), 1)
        for i in range(CH):
            t = jnp.where(c < 0, nslot, plan[0, jnp.maximum(c, 0) * CH + i])
            rows = [prod[half * i + 8 * g : half * i + 8 * g + 8] for g in range(4)]
            tiles = []
            for h in range(2):
                start = nt * (i % 2) + half * h
                moved = [pltpu.roll(v, (half * g - start) % 128, 1) for g, v in enumerate(rows)]
                low = jnp.where(lane < half, moved[0], moved[1])
                high = jnp.where(lane < 3 * half, moved[2], moved[3])
                tiles.append(jnp.where(lane < nt, low, high))
            kept[t] = jnp.where(parity == 0, tiles[0], tiles[1])
            sent[t] = jnp.where(parity == 0, tiles[1], tiles[0])

    @pl.when(chunks > 0)
    def _():
        begin(0)

    def chunk(c, carry):
        @pl.when(c + 1 < chunks)
        def _():
            begin(c + 1)

        bx, by = lax.rem(c, 2), lax.rem(c, 3)
        for i in range(CH):
            x_copy(c * CH + i, bx, i).wait()
            y_copy(c * CH + i, by, i).wait()
        products(c - 1)
        slot = jnp.where(c < chunks_first, 0, 1)
        u = jnp.dot(
            xs[bx, :, :half].reshape(CH * half, deep), w[slot, :deep], preferred_element_type=F32
        )
        u = u + jnp.dot(
            xs[bx, :, half:].reshape(CH * half, deep), w[slot, deep:], preferred_element_type=F32
        )
        us[bx] = u.astype(BF16)
        return carry

    lax.fori_loop(0, chunks, chunk, 0)

    @pl.when(chunks > 0)
    def _():
        products(chunks - 1)

    keep[...] = kept[:nslot]
    away[...] = sent[:nslot]


def route_kernel(tab, keep, came, send, mine, theirs, sem):
    copies = [
        pltpu.make_async_copy(keep, mine, sem.at[0]),
        pltpu.make_async_copy(came, theirs, sem.at[1]),
    ]
    for c in copies:
        c.start()
    nk = send.shape[1] - CAP
    send[:, CAP:] = jnp.zeros((send.shape[0], nk, *send.shape[2:]), F32)
    for c in copies:
        c.wait()
    for t in range(tab.shape[1]):
        v = mine[t] + theirs[t]
        send[t // CAP, t % CAP] = v

        @pl.when(tab[0, t] == 1)
        def _():
            owner = tab[2, t] // nk
            row = CAP + tab[2, t] % nk
            send[owner, row] = send[owner, row] + v


def exchange_kernel(
    firsts, own, big, full_in, whi_in, wlo_in, early, late, cw, out, full, whi, wlo, p1, p2, tot, prod, flat, s0, s1, s2
):
    count = firsts[2, 0]
    npair = own.shape[1]
    nk, rows, wide = tot.shape
    nt = whi_in.shape[0] // nk

    def second(j):
        return pltpu.make_async_copy(big.at[own[1, j]], p2.at[j], s2.at[j])

    def first(t):
        return pltpu.make_async_copy(big.at[firsts[0, t]], p1.at[t], s1.at[t])

    loads = [
        pltpu.make_async_copy(whi_in, whi, s0.at[0]),
        pltpu.make_async_copy(wlo_in, wlo, s0.at[1]),
        pltpu.make_async_copy(full_in.at[pl.ds(0, nk * nt)], full, s0.at[2]),
    ]
    for j in range(npair):
        second(j).start()
    for c in loads:
        c.start()

    def begin(t, carry):
        first(t).start()
        return carry

    lax.fori_loop(0, count, begin, 0)
    tot[...] = jnp.zeros_like(tot)
    for j in range(npair):
        second(j).wait()
    for c in loads:
        c.wait()

    def contract(left, right):
        return lax.dot_general(left, right, NT_DIMS, preferred_element_type=F32)

    b = p2[...].reshape(npair * rows, wide)
    e = contract(b, whi[...]) + contract(b, wlo[...])
    e = e + e
    for k in range(nk):
        prod[k] = e[:, k * nt : (k + 1) * nt]
    for j in range(npair):
        r = pl.ds(j * rows, rows)
        flat[r, :] = prod[own[0, j], r, :]

    def gather(t, carry):
        first(t).wait()
        k = firsts[1, t]
        tot[k] = tot[k] + p1[t].astype(F32)
        return carry

    lax.fori_loop(0, count, gather, 0)
    w = tot[...].reshape(nk * rows, wide) * cw[...]
    hi = w.astype(BF16)
    lo = (w - hi.astype(F32)).astype(BF16)
    m = contract(jnp.concatenate([hi, lo], axis=0), full[...])
    m = m[: nk * rows] + m[nk * rows :]
    m = m + m
    for k in range(nk):
        flat[pl.ds((npair + k) * rows, rows), :] = m[
            k * rows : (k + 1) * rows, k * nt : (k + 1) * nt
        ]
    z = flat_tiles(flat, (npair + nk) * rows)
    for j in range(npair + nk):
        out[j] = z[8 * j : 8 * j + 8]


def collect_kernel(own, got, out, here, sem):
    copy = pltpu.make_async_copy(got, here, sem)
    copy.start()
    copy.wait()
    nk = got.shape[1] - CAP
    npair = own.shape[1]
    for j in range(npair):
        out[j] = here[own[2, j], own[3, j]]
    for k in range(nk):
        out[npair + k] = jnp.sum(here[:, CAP + k], axis=0)


def bring(place, refs, whole, sem):
    copies = [
        pltpu.make_async_copy(r, whole.at[place[i]], sem.at[i]) for i, r in enumerate(refs)
    ]
    for c in copies:
        c.start()
    for c in copies:
        c.wait()


def arrange_kernel(place, r0, r1, r2, r3, dmat, whole, sem):
    bring(place, (r0, r1, r2, r3), whole, sem)
    half = dmat.shape[1] // 2
    for j in range(dmat.shape[0]):
        for a in range(2):
            left, right = whole[a, j], whole[a + 2, j]
            for g in range(4):
                cut = slice(half * g, half * (g + 1))
                dmat[j, pl.ds(half * a + 8 * g, 8), :] = jnp.concatenate(
                    [left[:, cut], right[:, cut]], axis=1
                )


def finish_kernel(place, dmat, r0, r1, r2, r3, blocks, mirrored, whole, emat, bmat, rows, sem):
    bring(place, (r0, r1, r2, r3), whole, sem)
    npair, nk = blocks.shape[0], mirrored.shape[0]
    nt = dmat.shape[1]
    half = nt // 2
    n = npair + nk
    for j in range(n):
        for a in range(4):
            tile = whole[a, j]
            emat[j, pl.ds(16 * a, 8, stride=2), :] = tile[:, :nt]
            emat[j, pl.ds(16 * a + 1, 8, stride=2), :] = tile[:, nt:]
    for j in range(n):
        if j < npair:
            bmat[j] = emat[j].T - dmat[j]
        else:
            bmat[j] = (emat[j] - dmat[j]).T
        even = bmat[j, pl.ds(0, half, stride=2), :]
        odd = bmat[j, pl.ds(1, half, stride=2), :]
        rows[pl.ds(j * half, half), :] = jnp.concatenate([even, odd], axis=1)
    for r in range(half):
        lanes = pl.ds(2 * nt * r, 2 * nt)
        blocks[:, lanes] = rows[pl.ds(r, npair, stride=half), :]
        mirrored[:, lanes] = rows[pl.ds(npair * half + r, nk, stride=half), :]


def in_vmem(count):
    return [pl.BlockSpec(memory_space=pltpu.VMEM)] * count


SMEM = pl.BlockSpec(memory_space=pltpu.SMEM)
ANY = pl.BlockSpec(memory_space=pl.ANY)


def per_device(x, y, p, coulomb, w, pairs, q_slot):
    n_ka = lax.axis_size("ka")
    me = lax.axis_index("ka")
    a = lax.axis_index("ga")
    nk, nt, gl = x.shape
    qs = w.shape[0]
    npair = pairs.shape[0]
    nslot = n_ka * CAP

    half, rows = nt // 2, nt // 4

    def shift(r):
        return [(i, (i + r) % 4) for i in range(4)]

    with jax.named_scope("pack"):
        y_far = lax.ppermute(y, "ga", shift(3))
        cut = [jnp.where((a + r) % 2 == 0, x[:, :half], x[:, half:]) for r in range(2)] * 2
        cut = cut[:1] + [lax.ppermute(cut[r], "ga", shift(r)) for r in range(1, 4)]

        def side(left, right):
            return jnp.concatenate([widen(left), widen(right)], axis=2)

        payload = jnp.concatenate(
            [side(cut[0], cut[1]), side(cut[2], cut[3]), side(y, y_far)], axis=1
        )
    with jax.named_scope("spread"):
        big = lax.all_gather(payload, "ka", axis=0, tiled=True)

    with jax.named_scope("weights"):
        cols = [
            jnp.pad(w[:, :, i * gl : (i + 1) * gl], ((0, 0), (0, QW - gl), (0, QW - gl)))
            for i in range(4)
        ]
        sets = [jnp.concatenate([cols[i], cols[(i + 1) % 4]], axis=2) for i in range(4)]
        wk = []
        for r in range(4):
            to = (a + r) % 4
            v = jnp.where(
                to < 2, jnp.where(to == 0, sets[0], sets[1]), jnp.where(to == 2, sets[2], sets[3])
            )
            wk.append(lax.ppermute(v, "ga", shift(r)) if r else v)
        wk = jnp.concatenate(wk, axis=1)

    with jax.named_scope("exchange_pack"):
        c1 = lax.reduce_precision(coulomb, 8, 7)
        c2 = lax.reduce_precision(coulomb - c1, 8, 7)
        c3 = coulomb - c1 - c2
        pieces = jnp.pad(jnp.stack([c1, c2, c3]).astype(BF16), ((0, 13), (0, 0)))
        held = jnp.concatenate([p.reshape(nk * nt, gl), pieces], axis=0)
        full = lax.all_gather(widen(held), "ga", axis=1, tiled=True)
        p_rows = full[: nk * nt].reshape(nk, nt, 4 * QW)
        p_rows = lax.dynamic_slice_in_dim(p_rows, a * rows, rows, axis=1)
        p_big = lax.all_gather(p_rows, "ka", axis=0, tiled=True)
        c_full = jnp.sum(full[nk * nt : nk * nt + 3].astype(F32), axis=0, keepdims=True)
        weighted = full[: nk * nt].astype(F32) * c_full
        w_hi = lax.reduce_precision(weighted, 8, 7)
        w_lo = (weighted - w_hi).astype(BF16)
        w_hi = w_hi.astype(BF16)

    with jax.named_scope("tables"):
        every = lax.all_gather(pairs, "ka", axis=0, tiled=True).reshape(n_ka, npair, 3)

        def routes(rows):
            slot = jnp.sum(
                jnp.where(
                    rows[..., 2, None] == jnp.arange(q_slot.shape[0]), q_slot, 0
                ),
                axis=-1,
            )
            q_owner = slot // qs
            k_owner = rows[..., 1] // nk
            return slot % qs, q_owner, rank_in_group(q_owner), k_owner, rank_in_group(k_owner)

        local, q_owner, q_rank, k_owner, k_rank = routes(every)
        ranks = jnp.arange(CAP)
        hot_q = (q_owner == me)[..., None] & (q_rank[..., None] == ranks)
        hot_k = (k_owner == me)[..., None] & (k_rank[..., None] == ranks)

        def pick(hot, v):
            return jnp.sum(jnp.where(hot, v[..., None], 0), axis=1).reshape(nslot)

        ones = jnp.ones_like(local)
        tab = jnp.stack(
            [
                pick(hot_q, ones),
                pick(hot_q, every[..., 0]),
                pick(hot_q, every[..., 1]),
                pick(hot_q, local),
                pick(hot_k, ones),
                pick(hot_k, every[..., 1] - me * nk),
                pick(hot_k, every[..., 0]),
            ]
        )
        _, o1, r1, _, _ = routes(pairs)
        own = jnp.stack([pairs[:, 0] - me * nk, pairs[:, 1], o1, r1])

    with jax.named_scope("plan"):
        npos = nslot + qs * CH
        used, slot = tab[0], tab[3]
        same = (slot[:, None] == slot[None, :]) & (used[None, :] == 1)
        order = jnp.arange(nslot)
        rank = jnp.sum((same & (order[:, None] > order[None, :])).astype(jnp.int32), axis=1)
        first = jnp.sum(used * (slot == 0))
        second = jnp.sum(used * (slot == 1))
        chunks_first = (first + CH - 1) // CH
        chunks = chunks_first + (second + CH - 1) // CH
        pos = jnp.where(slot == 0, rank, chunks_first * CH + rank)
        hot = (pos[None, :] == jnp.arange(npos)[:, None]) & (used == 1)[None, :]

        def at_pos(v, hot):
            return jnp.sum(jnp.where(hot, v[None, :], 0), axis=1)

        heads = jnp.pad(jnp.stack([chunks_first, chunks, a // 2]), (0, npos - 3))
        plan = jnp.stack(
            [at_pos(order - nslot, hot) + nslot, at_pos(tab[1], hot), at_pos(tab[2], hot), heads]
        )
        named = tab[4]
        rank = jnp.sum(jnp.where(order[:, None] > order[None, :], named[None, :], 0), axis=1)
        hot = (rank[None, :] == order[:, None]) & (named == 1)[None, :]
        total = jnp.broadcast_to(jnp.sum(named), (nslot,))
        firsts = jnp.stack([at_pos(tab[6], hot), at_pos(tab[5], hot), total])
    keep, away = pl.pallas_call(
        direct_kernel,
        out_shape=(jax.ShapeDtypeStruct((nslot, 8, 128), F32),) * 2,
        in_specs=[SMEM, ANY, *in_vmem(1)],
        out_specs=tuple(in_vmem(2)),
        scratch_shapes=[
            pltpu.VMEM((2, CH, nt, 2 * QW), BF16),
            pltpu.VMEM((3, CH, nt, 2 * QW), BF16),
            pltpu.VMEM((2, CH * half, 2 * QW), BF16),
            pltpu.VMEM((CH * half, 128), F32),
            pltpu.VMEM((nslot + 1, 8, 128), F32),
            pltpu.VMEM((nslot + 1, 8, 128), F32),
            pltpu.SemaphoreType.DMA((2, CH)),
            pltpu.SemaphoreType.DMA((3, CH)),
        ],
        compiler_params=pltpu.CompilerParams(vmem_limit_bytes=32 * 1024 * 1024),
        name="direct",
    )(plan, big, wk)
    with jax.named_scope("to_neighbour"):
        came = lax.ppermute(away, "ga", shift(2))
    send = pl.pallas_call(
        route_kernel,
        out_shape=jax.ShapeDtypeStruct((n_ka, CAP + nk, 8, 128), F32),
        in_specs=[SMEM, ANY, ANY],
        out_specs=pl.BlockSpec(memory_space=pltpu.VMEM),
        scratch_shapes=[
            pltpu.VMEM((nslot, 8, 128), F32),
            pltpu.VMEM((nslot, 8, 128), F32),
            pltpu.SemaphoreType.DMA((2,)),
        ],
        compiler_params=pltpu.CompilerParams(vmem_limit_bytes=8 * 1024 * 1024),
        name="route",
    )(tab, keep, came)
    with jax.named_scope("to_holders"):
        got = lax.all_to_all(send, "ka", 0, 0, tiled=True)
    n = npair + nk
    mine = pl.pallas_call(
        collect_kernel,
        out_shape=jax.ShapeDtypeStruct((n, 8, 128), F32),
        in_specs=[SMEM, ANY],
        out_specs=pl.BlockSpec(memory_space=pltpu.VMEM),
        scratch_shapes=[pltpu.VMEM(send.shape, F32), pltpu.SemaphoreType.DMA],
        compiler_params=pltpu.CompilerParams(vmem_limit_bytes=8 * 1024 * 1024),
        name="collect",
    )(own, got)
    with jax.named_scope("direct_copies"):
        others = [lax.ppermute(mine, "ga", shift(r)) for r in range(1, 4)]
        place = jnp.stack([(a - r) % 4 for r in range(4)])
    dmat = pl.pallas_call(
        arrange_kernel,
        out_shape=jax.ShapeDtypeStruct((n, nt, nt), F32),
        in_specs=[SMEM, ANY, ANY, ANY, ANY],
        out_specs=pl.BlockSpec(memory_space=pltpu.VMEM),
        scratch_shapes=[pltpu.VMEM((4, n, 8, 128), F32), pltpu.SemaphoreType.DMA((4,))],
        compiler_params=pltpu.CompilerParams(vmem_limit_bytes=8 * 1024 * 1024),
        name="arrange",
    )(place, mine, *others)
    exch = pl.pallas_call(
        exchange_kernel,
        out_shape=jax.ShapeDtypeStruct((n, 8, 128), F32),
        in_specs=[SMEM, SMEM, ANY, ANY, ANY, ANY, ANY, ANY, *in_vmem(1)],
        out_specs=pl.BlockSpec(memory_space=pltpu.VMEM),
        scratch_shapes=[
            pltpu.VMEM((nk * nt, 4 * QW), BF16),
            pltpu.VMEM((nk * nt, 4 * QW), BF16),
            pltpu.VMEM((nk * nt, 4 * QW), BF16),
            pltpu.VMEM((nslot, rows, 4 * QW), BF16),
            pltpu.VMEM((npair, rows, 4 * QW), BF16),
            pltpu.VMEM((nk, rows, 4 * QW), F32),
            pltpu.VMEM((nk, npair * rows, nt), F32),
            pltpu.VMEM((n * rows, nt), F32),
            pltpu.SemaphoreType.DMA((3,)),
            pltpu.SemaphoreType.DMA((nslot,)),
            pltpu.SemaphoreType.DMA((npair,)),
        ],
        compiler_params=pltpu.CompilerParams(vmem_limit_bytes=50 * 1024 * 1024),
        name="exchange",
    )(firsts, own, p_big, full, w_hi, w_lo, others[2], others[2], c_full)
    with jax.named_scope("exchange_copies"):
        exch_others = [lax.ppermute(exch, "ga", shift(r)) for r in range(1, 4)]
    return pl.pallas_call(
        finish_kernel,
        out_shape=(
            jax.ShapeDtypeStruct((npair, nt * nt), F32),
            jax.ShapeDtypeStruct((nk, nt * nt), F32),
        ),
        in_specs=[SMEM, *in_vmem(2), ANY, ANY, ANY],
        out_specs=tuple(in_vmem(2)),
        scratch_shapes=[
            pltpu.VMEM((4, n, 8, 128), F32),
            pltpu.VMEM((n, nt, nt), F32),
            pltpu.VMEM((n, nt, nt), F32),
            pltpu.VMEM((n * half, 2 * nt), F32),
            pltpu.SemaphoreType.DMA((4,)),
        ],
        compiler_params=pltpu.CompilerParams(vmem_limit_bytes=16 * 1024 * 1024),
        name="finish",
    )(place, dmat, exch, *exch_others)


def solution(mesh):
    in_specs = (
        P("ka", None, "ga"),
        P("ka", None, "ga"),
        P("ka", None, "ga"),
        P("ga"),
        P("ka", "ga", None),
        P("ka", None),
        P(),
    )
    out_specs = (P("ka", None), P("ka", None))
    return jax.shard_map(
        per_device, mesh=mesh, in_specs=in_specs, out_specs=out_specs, check_vma=False
    )
```

```python
import jax
import jax.numpy as jnp
from jax import lax
from jax.experimental import pallas as pl
from jax.experimental.pallas import tpu as pltpu
from jax.sharding import PartitionSpec as P

CAP = 2
QW = 384
CH = 8
F32 = jnp.float32
BF16 = jnp.bfloat16
NT_DIMS = (((1,), (1,)), ((), ()))


def rank_in_group(owners):
    n = owners.shape[-1]
    same = owners[..., :, None] == owners[..., None, :]
    before = jnp.arange(n)[:, None] > jnp.arange(n)[None, :]
    return jnp.sum(jnp.logical_and(same, before).astype(jnp.int32), axis=-1)


def widen(v):
    return jnp.pad(v, ((0, 0),) * (v.ndim - 1) + ((0, QW - v.shape[-1]),))


def flat_tiles(tmp, rows):
    even = tmp[pl.ds(0, rows // 2, stride=2), :]
    odd = tmp[pl.ds(1, rows // 2, stride=2), :]
    return jnp.concatenate([even, odd], axis=1)


def direct_kernel(plan, big, w, keep, away, xs, ys, us, prod, kept, sent, sx, sy):
    half = prod.shape[0] // CH
    nt = 2 * half
    deep = xs.shape[3]
    nslot = keep.shape[0]
    chunks_first, chunks, parity = plan[3, 0], plan[3, 1], plan[3, 2]

    def x_copy(pos, buf, i):
        return pltpu.make_async_copy(big.at[plan[1, pos], pl.ds(0, nt)], xs.at[buf, i], sx.at[buf, i])

    def y_copy(pos, buf, i):
        return pltpu.make_async_copy(big.at[plan[2, pos], pl.ds(nt, nt)], ys.at[buf, i], sy.at[buf, i])

    def begin(c):
        for i in range(CH):
            x_copy(c * CH + i, lax.rem(c, 2), i).start()
            y_copy(c * CH + i, lax.rem(c, 3), i).start()

    def products(c):
        u = us[lax.rem(c + 2, 2)]
        y = ys[lax.rem(c + 3, 3)].reshape(CH * nt, deep)
        for i in range(0, CH, 4):
            d = lax.dot_general(
                u[half * i : half * (i + 4)],
                y[nt * i : nt * (i + 4)],
                NT_DIMS,
                preferred_element_type=F32,
            )
            for j in range(2):
                prod[half * i + nt * j : half * i + nt * j + nt] = d[
                    nt * j : nt * j + nt, 128 * j : 128 * j + 128
                ]
        lane = lax.broadcasted_iota(jnp.int32, (8, 128), 1)
        for i in range(CH):
            t = jnp.where(c < 0, nslot, plan[0, jnp.maximum(c, 0) * CH + i])
            rows = [prod[half * i + 8 * g : half * i + 8 * g + 8] for g in range(4)]
            tiles = []
            for h in range(2):
                start = nt * (i % 2) + half * h
                moved = [pltpu.roll(v, (half * g - start) % 128, 1) for g, v in enumerate(rows)]
                low = jnp.where(lane < half, moved[0], moved[1])
                high = jnp.where(lane < 3 * half, moved[2], moved[3])
                tiles.append(jnp.where(lane < nt, low, high))
            kept[t] = jnp.where(parity == 0, tiles[0], tiles[1])
            sent[t] = jnp.where(parity == 0, tiles[1], tiles[0])

    @pl.when(chunks > 0)
    def _():
        begin(0)

    def chunk(c, carry):
        @pl.when(c + 1 < chunks)
        def _():
            begin(c + 1)

        bx, by = lax.rem(c, 2), lax.rem(c, 3)
        for i in range(CH):
            x_copy(c * CH + i, bx, i).wait()
            y_copy(c * CH + i, by, i).wait()
        products(c - 1)
        slot = jnp.where(c < chunks_first, 0, 1)
        u = jnp.dot(
            xs[bx, :, :half].reshape(CH * half, deep), w[slot, :deep], preferred_element_type=F32
        )
        u = u + jnp.dot(
            xs[bx, :, half:].reshape(CH * half, deep), w[slot, deep:], preferred_element_type=F32
        )
        us[bx] = u.astype(BF16)
        return carry

    lax.fori_loop(0, chunks, chunk, 0)

    @pl.when(chunks > 0)
    def _():
        products(chunks - 1)

    keep[...] = kept[:nslot]
    away[...] = sent[:nslot]


def route_kernel(tab, keep, came, send, mine, theirs, sem):
    copies = [
        pltpu.make_async_copy(keep, mine, sem.at[0]),
        pltpu.make_async_copy(came, theirs, sem.at[1]),
    ]
    for c in copies:
        c.start()
    nk = send.shape[1] - CAP
    send[:, CAP:] = jnp.zeros((send.shape[0], nk, *send.shape[2:]), F32)
    for c in copies:
        c.wait()
    for t in range(tab.shape[1]):
        v = mine[t] + theirs[t]
        send[t // CAP, t % CAP] = v

        @pl.when(tab[0, t] == 1)
        def _():
            owner = tab[2, t] // nk
            row = CAP + tab[2, t] % nk
            send[owner, row] = send[owner, row] + v


def exchange_kernel(
    firsts, own, big, early, full, whi, wlo, cw, out, p1, p2, tot, prod, flat, s1, s2
):
    count = firsts[2, 0]
    npair = own.shape[1]
    nk, rows, wide = tot.shape
    nt = whi.shape[0] // nk

    def second(j):
        return pltpu.make_async_copy(big.at[own[1, j]], p2.at[j], s2.at[j])

    def first(t):
        return pltpu.make_async_copy(big.at[firsts[0, t]], p1.at[t], s1.at[t])

    for j in range(npair):
        second(j).start()

    def begin(t, carry):
        first(t).start()
        return carry

    lax.fori_loop(0, count, begin, 0)
    tot[...] = jnp.zeros_like(tot)
    for j in range(npair):
        second(j).wait()

    def contract(left, right):
        return lax.dot_general(left, right, NT_DIMS, preferred_element_type=F32)

    b = p2[...].reshape(npair * rows, wide)
    e = contract(b, whi[...]) + contract(b, wlo[...])
    e = e + e
    for k in range(nk):
        prod[k] = e[:, k * nt : (k + 1) * nt]
    for j in range(npair):
        r = pl.ds(j * rows, rows)
        flat[r, :] = prod[own[0, j], r, :]

    def gather(t, carry):
        first(t).wait()
        k = firsts[1, t]
        tot[k] = tot[k] + p1[t].astype(F32)
        return carry

    lax.fori_loop(0, count, gather, 0)
    w = tot[...].reshape(nk * rows, wide) * cw[...]
    hi = w.astype(BF16)
    lo = (w - hi.astype(F32)).astype(BF16)
    m = contract(jnp.concatenate([hi, lo], axis=0), full[: nk * nt])
    m = m[: nk * rows] + m[nk * rows :]
    m = m + m
    for k in range(nk):
        flat[pl.ds((npair + k) * rows, rows), :] = m[
            k * rows : (k + 1) * rows, k * nt : (k + 1) * nt
        ]
    z = flat_tiles(flat, (npair + nk) * rows)
    for j in range(npair + nk):
        out[j] = z[8 * j : 8 * j + 8]


def collect_kernel(own, got, out, here, sem):
    copy = pltpu.make_async_copy(got, here, sem)
    copy.start()
    copy.wait()
    nk = got.shape[1] - CAP
    npair = own.shape[1]
    for j in range(npair):
        out[j] = here[own[2, j], own[3, j]]
    for k in range(nk):
        out[npair + k] = jnp.sum(here[:, CAP + k], axis=0)


def bring(place, refs, whole, sem):
    copies = [
        pltpu.make_async_copy(r, whole.at[place[i]], sem.at[i]) for i, r in enumerate(refs)
    ]
    for c in copies:
        c.start()
    for c in copies:
        c.wait()


def arrange_kernel(place, r0, r1, r2, r3, dmat, whole, sem):
    bring(place, (r0, r1, r2, r3), whole, sem)
    half = dmat.shape[1] // 2
    for j in range(dmat.shape[0]):
        for a in range(2):
            left, right = whole[2 * a, j], whole[2 * a + 1, j]
            for g in range(4):
                cut = slice(half * g, half * (g + 1))
                dmat[j, pl.ds(half * a + 8 * g, 8), :] = jnp.concatenate(
                    [left[:, cut], right[:, cut]], axis=1
                )


def finish_kernel(place, dmat, r0, r1, r2, r3, blocks, mirrored, whole, emat, bmat, rows, sem):
    bring(place, (r0, r1, r2, r3), whole, sem)
    npair, nk = blocks.shape[0], mirrored.shape[0]
    nt = dmat.shape[1]
    half = nt // 2
    n = npair + nk
    for j in range(n):
        for a in range(4):
            tile = whole[a, j]
            emat[j, pl.ds(16 * a, 8, stride=2), :] = tile[:, :nt]
            emat[j, pl.ds(16 * a + 1, 8, stride=2), :] = tile[:, nt:]
    for j in range(n):
        if j < npair:
            bmat[j] = emat[j].T - dmat[j]
        else:
            bmat[j] = (emat[j] - dmat[j]).T
        even = bmat[j, pl.ds(0, half, stride=2), :]
        odd = bmat[j, pl.ds(1, half, stride=2), :]
        rows[pl.ds(j * half, half), :] = jnp.concatenate([even, odd], axis=1)
    for r in range(half):
        lanes = pl.ds(2 * nt * r, 2 * nt)
        blocks[:, lanes] = rows[pl.ds(r, npair, stride=half), :]
        mirrored[:, lanes] = rows[pl.ds(npair * half + r, nk, stride=half), :]


def in_vmem(count):
    return [pl.BlockSpec(memory_space=pltpu.VMEM)] * count


SMEM = pl.BlockSpec(memory_space=pltpu.SMEM)
ANY = pl.BlockSpec(memory_space=pl.ANY)


def per_device(x, y, p, coulomb, w, pairs, q_slot):
    n_ka = lax.axis_size("ka")
    me = lax.axis_index("ka")
    a = lax.axis_index("ga")
    nk, nt, gl = x.shape
    qs = w.shape[0]
    npair = pairs.shape[0]
    nslot = n_ka * CAP

    half, rows = nt // 2, nt // 4

    def shift(r):
        return [(i, (i + r) % 4) for i in range(4)]

    with jax.named_scope("pack"):
        y_far = lax.ppermute(y, "ga", [(i, 3 - i) for i in range(4)])
        cut = [jnp.where((a + r) % 4 < 2, x[:, :half], x[:, half:]) for r in range(4)]
        cut = cut[:1] + [lax.ppermute(cut[r], "ga", shift(r)) for r in range(1, 4)]

        def side(left, right):
            return jnp.concatenate([widen(left), widen(right)], axis=2)

        y_both = side(jnp.where(a < 2, y, y_far), jnp.where(a < 2, y_far, y))
        payload = jnp.concatenate([side(cut[0], cut[1]), side(cut[2], cut[3]), y_both], axis=1)
    with jax.named_scope("spread"):
        big = lax.all_gather(payload, "ka", axis=0, tiled=True)

    with jax.named_scope("weights"):
        cols = [
            jnp.pad(w[:, :, i * gl : (i + 1) * gl], ((0, 0), (0, QW - gl), (0, QW - gl)))
            for i in range(4)
        ]
        outer = jnp.concatenate([cols[0], cols[3]], axis=2)
        inner = jnp.concatenate([cols[1], cols[2]], axis=2)
        wk = []
        for r in range(4):
            to = (a + r) % 4
            v = jnp.where((to == 0) | (to == 3), outer, inner)
            wk.append(lax.ppermute(v, "ga", shift(r)) if r else v)
        wk = jnp.concatenate(wk, axis=1)

    with jax.named_scope("exchange_pack"):
        c1 = lax.reduce_precision(coulomb, 8, 7)
        c2 = lax.reduce_precision(coulomb - c1, 8, 7)
        c3 = coulomb - c1 - c2
        pieces = jnp.pad(jnp.stack([c1, c2, c3]).astype(BF16), ((0, 13), (0, 0)))
        held = jnp.concatenate([p.reshape(nk * nt, gl), pieces], axis=0)
        full = lax.all_gather(widen(held), "ga", axis=1, tiled=True)
        p_rows = full[: nk * nt].reshape(nk, nt, 4 * QW)
        p_rows = lax.dynamic_slice_in_dim(p_rows, a * rows, rows, axis=1)
        p_big = lax.all_gather(p_rows, "ka", axis=0, tiled=True)
        c_full = jnp.sum(full[nk * nt : nk * nt + 3].astype(F32), axis=0, keepdims=True)
        weighted = full[: nk * nt].astype(F32) * c_full
        w_hi = lax.reduce_precision(weighted, 8, 7)
        w_lo = (weighted - w_hi).astype(BF16)
        w_hi = w_hi.astype(BF16)

    with jax.named_scope("tables"):
        every = lax.all_gather(pairs, "ka", axis=0, tiled=True).reshape(n_ka, npair, 3)

        def routes(rows):
            slot = jnp.sum(
                jnp.where(
                    rows[..., 2, None] == jnp.arange(q_slot.shape[0]), q_slot, 0
                ),
                axis=-1,
            )
            q_owner = slot // qs
            k_owner = rows[..., 1] // nk
            return slot % qs, q_owner, rank_in_group(q_owner), k_owner, rank_in_group(k_owner)

        local, q_owner, q_rank, k_owner, k_rank = routes(every)
        ranks = jnp.arange(CAP)
        hot_q = (q_owner == me)[..., None] & (q_rank[..., None] == ranks)
        hot_k = (k_owner == me)[..., None] & (k_rank[..., None] == ranks)

        def pick(hot, v):
            return jnp.sum(jnp.where(hot, v[..., None], 0), axis=1).reshape(nslot)

        ones = jnp.ones_like(local)
        tab = jnp.stack(
            [
                pick(hot_q, ones),
                pick(hot_q, every[..., 0]),
                pick(hot_q, every[..., 1]),
                pick(hot_q, local),
                pick(hot_k, ones),
                pick(hot_k, every[..., 1] - me * nk),
                pick(hot_k, every[..., 0]),
            ]
        )
        _, o1, r1, _, _ = routes(pairs)
        own = jnp.stack([pairs[:, 0] - me * nk, pairs[:, 1], o1, r1])

    with jax.named_scope("plan"):
        npos = nslot + qs * CH
        used, slot = tab[0], tab[3]
        same = (slot[:, None] == slot[None, :]) & (used[None, :] == 1)
        order = jnp.arange(nslot)
        rank = jnp.sum((same & (order[:, None] > order[None, :])).astype(jnp.int32), axis=1)
        first = jnp.sum(used * (slot == 0))
        second = jnp.sum(used * (slot == 1))
        chunks_first = (first + CH - 1) // CH
        chunks = chunks_first + (second + CH - 1) // CH
        pos = jnp.where(slot == 0, rank, chunks_first * CH + rank)
        hot = (pos[None, :] == jnp.arange(npos)[:, None]) & (used == 1)[None, :]

        def at_pos(v, hot):
            return jnp.sum(jnp.where(hot, v[None, :], 0), axis=1)

        heads = jnp.pad(jnp.stack([chunks_first, chunks, a % 2]), (0, npos - 3))
        plan = jnp.stack(
            [at_pos(order - nslot, hot) + nslot, at_pos(tab[1], hot), at_pos(tab[2], hot), heads]
        )
        named = tab[4]
        rank = jnp.sum(jnp.where(order[:, None] > order[None, :], named[None, :], 0), axis=1)
        hot = (rank[None, :] == order[:, None]) & (named == 1)[None, :]
        total = jnp.broadcast_to(jnp.sum(named), (nslot,))
        firsts = jnp.stack([at_pos(tab[6], hot), at_pos(tab[5], hot), total])
    keep, away = pl.pallas_call(
        direct_kernel,
        out_shape=(jax.ShapeDtypeStruct((nslot, 8, 128), F32),) * 2,
        in_specs=[SMEM, ANY, *in_vmem(1)],
        out_specs=tuple(in_vmem(2)),
        scratch_shapes=[
            pltpu.VMEM((2, CH, nt, 2 * QW), BF16),
            pltpu.VMEM((3, CH, nt, 2 * QW), BF16),
            pltpu.VMEM((2, CH * half, 2 * QW), BF16),
            pltpu.VMEM((CH * half, 128), F32),
            pltpu.VMEM((nslot + 1, 8, 128), F32),
            pltpu.VMEM((nslot + 1, 8, 128), F32),
            pltpu.SemaphoreType.DMA((2, CH)),
            pltpu.SemaphoreType.DMA((3, CH)),
        ],
        compiler_params=pltpu.CompilerParams(vmem_limit_bytes=32 * 1024 * 1024),
        name="direct",
    )(plan, big, wk)
    with jax.named_scope("to_neighbour"):
        came = lax.ppermute(away, "ga", [(0, 1), (1, 0), (2, 3), (3, 2)])
    send = pl.pallas_call(
        route_kernel,
        out_shape=jax.ShapeDtypeStruct((n_ka, CAP + nk, 8, 128), F32),
        in_specs=[SMEM, ANY, ANY],
        out_specs=pl.BlockSpec(memory_space=pltpu.VMEM),
        scratch_shapes=[
            pltpu.VMEM((nslot, 8, 128), F32),
            pltpu.VMEM((nslot, 8, 128), F32),
            pltpu.SemaphoreType.DMA((2,)),
        ],
        compiler_params=pltpu.CompilerParams(vmem_limit_bytes=8 * 1024 * 1024),
        name="route",
    )(tab, keep, came)
    with jax.named_scope("to_holders"):
        got = lax.all_to_all(send, "ka", 0, 0, tiled=True)
    n = npair + nk
    mine = pl.pallas_call(
        collect_kernel,
        out_shape=jax.ShapeDtypeStruct((n, 8, 128), F32),
        in_specs=[SMEM, ANY],
        out_specs=pl.BlockSpec(memory_space=pltpu.VMEM),
        scratch_shapes=[pltpu.VMEM(send.shape, F32), pltpu.SemaphoreType.DMA],
        compiler_params=pltpu.CompilerParams(vmem_limit_bytes=8 * 1024 * 1024),
        name="collect",
    )(own, got)
    with jax.named_scope("direct_copies"):
        others = [lax.ppermute(mine, "ga", shift(r)) for r in range(1, 4)]
        place = jnp.stack([(a - r) % 4 for r in range(4)])
    dmat = pl.pallas_call(
        arrange_kernel,
        out_shape=jax.ShapeDtypeStruct((n, nt, nt), F32),
        in_specs=[SMEM, ANY, ANY, ANY, ANY],
        out_specs=pl.BlockSpec(memory_space=pltpu.VMEM),
        scratch_shapes=[pltpu.VMEM((4, n, 8, 128), F32), pltpu.SemaphoreType.DMA((4,))],
        compiler_params=pltpu.CompilerParams(vmem_limit_bytes=8 * 1024 * 1024),
        name="arrange",
    )(place, mine, *others)
    exch = pl.pallas_call(
        exchange_kernel,
        out_shape=jax.ShapeDtypeStruct((n, 8, 128), F32),
        in_specs=[SMEM, SMEM, ANY, ANY, *in_vmem(4)],
        out_specs=pl.BlockSpec(memory_space=pltpu.VMEM),
        scratch_shapes=[
            pltpu.VMEM((nslot, rows, 4 * QW), BF16),
            pltpu.VMEM((npair, rows, 4 * QW), BF16),
            pltpu.VMEM((nk, rows, 4 * QW), F32),
            pltpu.VMEM((nk, npair * rows, nt), F32),
            pltpu.VMEM((n * rows, nt), F32),
            pltpu.SemaphoreType.DMA((nslot,)),
            pltpu.SemaphoreType.DMA((npair,)),
        ],
        compiler_params=pltpu.CompilerParams(vmem_limit_bytes=50 * 1024 * 1024),
        name="exchange",
    )(firsts, own, p_big, others[2], full, w_hi, w_lo, c_full)
    with jax.named_scope("exchange_copies"):
        exch_others = [lax.ppermute(exch, "ga", shift(r)) for r in range(1, 4)]
    return pl.pallas_call(
        finish_kernel,
        out_shape=(
            jax.ShapeDtypeStruct((npair, nt * nt), F32),
            jax.ShapeDtypeStruct((nk, nt * nt), F32),
        ),
        in_specs=[SMEM, *in_vmem(2), ANY, ANY, ANY],
        out_specs=tuple(in_vmem(2)),
        scratch_shapes=[
            pltpu.VMEM((4, n, 8, 128), F32),
            pltpu.VMEM((n, nt, nt), F32),
            pltpu.VMEM((n, nt, nt), F32),
            pltpu.VMEM((n * half, 2 * nt), F32),
            pltpu.SemaphoreType.DMA((4,)),
        ],
        compiler_params=pltpu.CompilerParams(vmem_limit_bytes=16 * 1024 * 1024),
        name="finish",
    )(place, dmat, exch, *exch_others)


def solution(mesh):
    in_specs = (
        P("ka", None, "ga"),
        P("ka", None, "ga"),
        P("ka", None, "ga"),
        P("ga"),
        P("ka", "ga", None),
        P("ka", None),
        P(),
    )
    out_specs = (P("ka", None), P("ka", None))
    return jax.shard_map(
        per_device, mesh=mesh, in_specs=in_specs, out_specs=out_specs, check_vma=False
    )
```

```python
import jax
import jax.numpy as jnp
from jax import lax
from jax.experimental import pallas as pl
from jax.experimental.pallas import tpu as pltpu
from jax.sharding import PartitionSpec as P

CAP = 2
QW = 384
CH = 8
F32 = jnp.float32
BF16 = jnp.bfloat16
NT_DIMS = (((1,), (1,)), ((), ()))


def rank_in_group(owners):
    n = owners.shape[-1]
    same = owners[..., :, None] == owners[..., None, :]
    before = jnp.arange(n)[:, None] > jnp.arange(n)[None, :]
    return jnp.sum(jnp.logical_and(same, before).astype(jnp.int32), axis=-1)


def widen(v):
    return jnp.pad(v, ((0, 0),) * (v.ndim - 1) + ((0, QW - v.shape[-1]),))


def flat_tiles(tmp, rows):
    even = tmp[pl.ds(0, rows // 2, stride=2), :]
    odd = tmp[pl.ds(1, rows // 2, stride=2), :]
    return jnp.concatenate([even, odd], axis=1)


def direct_kernel(plan, big, wk, keep, away, w, xs, ys, us, prod, kept, sent, sw, sx, sy):
    half = prod.shape[0] // CH
    nt = 2 * half
    deep = xs.shape[3]
    nslot = keep.shape[0]
    chunks_first, chunks, parity = plan[3, 0], plan[3, 1], plan[3, 2]

    def x_copy(pos, buf, i):
        return pltpu.make_async_copy(big.at[plan[1, pos], pl.ds(0, nt)], xs.at[buf, i], sx.at[buf, i])

    def y_copy(pos, buf, i):
        return pltpu.make_async_copy(big.at[plan[2, pos], pl.ds(nt, nt)], ys.at[buf, i], sy.at[buf, i])

    def begin(c):
        for i in range(CH):
            x_copy(c * CH + i, lax.rem(c, 2), i).start()
            y_copy(c * CH + i, lax.rem(c, 3), i).start()

    def products(c):
        u = us[lax.rem(c + 2, 2)]
        y = ys[lax.rem(c + 3, 3)].reshape(CH * nt, deep)
        for i in range(0, CH, 4):
            d = lax.dot_general(
                u[half * i : half * (i + 4)],
                y[nt * i : nt * (i + 4)],
                NT_DIMS,
                preferred_element_type=F32,
            )
            for j in range(2):
                prod[half * i + nt * j : half * i + nt * j + nt] = d[
                    nt * j : nt * j + nt, 128 * j : 128 * j + 128
                ]
        lane = lax.broadcasted_iota(jnp.int32, (8, 128), 1)
        for i in range(CH):
            t = jnp.where(c < 0, nslot, plan[0, jnp.maximum(c, 0) * CH + i])
            rows = [prod[half * i + 8 * g : half * i + 8 * g + 8] for g in range(4)]
            tiles = []
            for h in range(2):
                start = nt * (i % 2) + half * h
                moved = [pltpu.roll(v, (half * g - start) % 128, 1) for g, v in enumerate(rows)]
                low = jnp.where(lane < half, moved[0], moved[1])
                high = jnp.where(lane < 3 * half, moved[2], moved[3])
                tiles.append(jnp.where(lane < nt, low, high))
            kept[t] = jnp.where(parity == 0, tiles[0], tiles[1])
            sent[t] = jnp.where(parity == 0, tiles[1], tiles[0])

    loads = [pltpu.make_async_copy(wk.at[i], w.at[i], sw.at[i]) for i in range(w.shape[0])]
    loads[0].start()

    @pl.when(chunks > 0)
    def _():
        begin(0)

    for c in loads[1:]:
        c.start()
    for c in loads:
        c.wait()

    def chunk(c, carry):
        @pl.when(c + 1 < chunks)
        def _():
            begin(c + 1)

        bx, by = lax.rem(c, 2), lax.rem(c, 3)
        for i in range(CH):
            x_copy(c * CH + i, bx, i).wait()
            y_copy(c * CH + i, by, i).wait()
        products(c - 1)
        slot = jnp.where(c < chunks_first, 0, 1)
        u = jnp.dot(
            xs[bx, :, :half].reshape(CH * half, deep), w[slot, :deep], preferred_element_type=F32
        )
        u = u + jnp.dot(
            xs[bx, :, half:].reshape(CH * half, deep), w[slot, deep:], preferred_element_type=F32
        )
        us[bx] = u.astype(BF16)
        return carry

    lax.fori_loop(0, chunks, chunk, 0)

    @pl.when(chunks > 0)
    def _():
        products(chunks - 1)

    keep[...] = kept[:nslot]
    away[...] = sent[:nslot]


def route_kernel(tab, keep, came, send, mine, theirs, sem):
    copies = [
        pltpu.make_async_copy(keep, mine, sem.at[0]),
        pltpu.make_async_copy(came, theirs, sem.at[1]),
    ]
    for c in copies:
        c.start()
    nk = send.shape[1] - CAP
    send[:, CAP:] = jnp.zeros((send.shape[0], nk, *send.shape[2:]), F32)
    for c in copies:
        c.wait()
    for t in range(tab.shape[1]):
        v = mine[t] + theirs[t]
        send[t // CAP, t % CAP] = v

        @pl.when(tab[0, t] == 1)
        def _():
            owner = tab[2, t] // nk
            row = CAP + tab[2, t] % nk
            send[owner, row] = send[owner, row] + v


def exchange_kernel(
    firsts, own, big, early, full, whi, wlo, cw, out, p1, p2, tot, prod, flat, s1, s2
):
    count = firsts[2, 0]
    npair = own.shape[1]
    nk, rows, wide = tot.shape
    nt = whi.shape[0] // nk

    def second(j):
        return pltpu.make_async_copy(big.at[own[1, j]], p2.at[j], s2.at[j])

    def first(t):
        return pltpu.make_async_copy(big.at[firsts[0, t]], p1.at[t], s1.at[t])

    for j in range(npair):
        second(j).start()

    def begin(t, carry):
        first(t).start()
        return carry

    lax.fori_loop(0, count, begin, 0)
    tot[...] = jnp.zeros_like(tot)
    for j in range(npair):
        second(j).wait()

    def contract(left, right):
        return lax.dot_general(left, right, NT_DIMS, preferred_element_type=F32)

    b = p2[...].reshape(npair * rows, wide)
    e = contract(b, whi[...]) + contract(b, wlo[...])
    e = e + e
    for k in range(nk):
        prod[k] = e[:, k * nt : (k + 1) * nt]
    for j in range(npair):
        r = pl.ds(j * rows, rows)
        flat[r, :] = prod[own[0, j], r, :]

    def gather(t, carry):
        first(t).wait()
        k = firsts[1, t]
        tot[k] = tot[k] + p1[t].astype(F32)
        return carry

    lax.fori_loop(0, count, gather, 0)
    w = tot[...].reshape(nk * rows, wide) * cw[...]
    hi = w.astype(BF16)
    lo = (w - hi.astype(F32)).astype(BF16)
    m = contract(jnp.concatenate([hi, lo], axis=0), full[: nk * nt])
    m = m[: nk * rows] + m[nk * rows :]
    m = m + m
    for k in range(nk):
        flat[pl.ds((npair + k) * rows, rows), :] = m[
            k * rows : (k + 1) * rows, k * nt : (k + 1) * nt
        ]
    z = flat_tiles(flat, (npair + nk) * rows)
    for j in range(npair + nk):
        out[j] = z[8 * j : 8 * j + 8]


def collect_kernel(own, got, out, here, sem):
    copy = pltpu.make_async_copy(got, here, sem)
    copy.start()
    copy.wait()
    nk = got.shape[1] - CAP
    npair = own.shape[1]
    for j in range(npair):
        out[j] = here[own[2, j], own[3, j]]
    for k in range(nk):
        out[npair + k] = jnp.sum(here[:, CAP + k], axis=0)


def bring(place, refs, whole, sem):
    copies = [
        pltpu.make_async_copy(r, whole.at[place[i]], sem.at[i]) for i, r in enumerate(refs)
    ]
    for c in copies:
        c.start()
    for c in copies:
        c.wait()


def arrange_kernel(place, r0, r1, r2, r3, dmat, whole, sem):
    bring(place, (r0, r1, r2, r3), whole, sem)
    half = dmat.shape[1] // 2
    for j in range(dmat.shape[0]):
        for a in range(2):
            left, right = whole[2 * a, j], whole[2 * a + 1, j]
            for g in range(4):
                cut = slice(half * g, half * (g + 1))
                dmat[j, pl.ds(half * a + 8 * g, 8), :] = jnp.concatenate(
                    [left[:, cut], right[:, cut]], axis=1
                )


def finish_kernel(place, dmat, r0, r1, r2, r3, blocks, mirrored, whole, emat, bmat, rows, sem):
    bring(place, (r0, r1, r2, r3), whole, sem)
    npair, nk = blocks.shape[0], mirrored.shape[0]
    nt = dmat.shape[1]
    half = nt // 2
    n = npair + nk
    for j in range(n):
        for a in range(4):
            tile = whole[a, j]
            emat[j, pl.ds(16 * a, 8, stride=2), :] = tile[:, :nt]
            emat[j, pl.ds(16 * a + 1, 8, stride=2), :] = tile[:, nt:]
    for j in range(n):
        if j < npair:
            bmat[j] = emat[j].T - dmat[j]
        else:
            bmat[j] = (emat[j] - dmat[j]).T
        even = bmat[j, pl.ds(0, half, stride=2), :]
        odd = bmat[j, pl.ds(1, half, stride=2), :]
        rows[pl.ds(j * half, half), :] = jnp.concatenate([even, odd], axis=1)
    for r in range(half):
        lanes = pl.ds(2 * nt * r, 2 * nt)
        blocks[:, lanes] = rows[pl.ds(r, npair, stride=half), :]
        mirrored[:, lanes] = rows[pl.ds(npair * half + r, nk, stride=half), :]


def in_vmem(count):
    return [pl.BlockSpec(memory_space=pltpu.VMEM)] * count


SMEM = pl.BlockSpec(memory_space=pltpu.SMEM)
ANY = pl.BlockSpec(memory_space=pl.ANY)


def per_device(x, y, p, coulomb, w, pairs, q_slot):
    n_ka = lax.axis_size("ka")
    me = lax.axis_index("ka")
    a = lax.axis_index("ga")
    nk, nt, gl = x.shape
    qs = w.shape[0]
    npair = pairs.shape[0]
    nslot = n_ka * CAP

    half, rows = nt // 2, nt // 4

    def shift(r):
        return [(i, (i + r) % 4) for i in range(4)]

    with jax.named_scope("pack"):
        y_far = lax.ppermute(y, "ga", [(i, 3 - i) for i in range(4)])
        cut = [jnp.where((a + r) % 4 < 2, x[:, :half], x[:, half:]) for r in range(4)]
        cut = cut[:1] + [lax.ppermute(cut[r], "ga", shift(r)) for r in range(1, 4)]

        def side(left, right):
            return jnp.concatenate([widen(left), widen(right)], axis=2)

        y_both = side(jnp.where(a < 2, y, y_far), jnp.where(a < 2, y_far, y))
        payload = jnp.concatenate([side(cut[0], cut[1]), side(cut[2], cut[3]), y_both], axis=1)
    with jax.named_scope("spread"):
        big = lax.all_gather(payload, "ka", axis=0, tiled=True)

    with jax.named_scope("weights"):
        cols = [
            jnp.pad(w[:, :, i * gl : (i + 1) * gl], ((0, 0), (0, QW - gl), (0, QW - gl)))
            for i in range(4)
        ]
        outer = jnp.concatenate([cols[0], cols[3]], axis=2)
        inner = jnp.concatenate([cols[1], cols[2]], axis=2)
        wk = []
        for r in range(4):
            to = (a + r) % 4
            v = jnp.where((to == 0) | (to == 3), outer, inner)
            wk.append(lax.ppermute(v, "ga", shift(r)) if r else v)
        wk = jnp.concatenate(wk, axis=1)

    with jax.named_scope("exchange_pack"):
        c1 = lax.reduce_precision(coulomb, 8, 7)
        c2 = lax.reduce_precision(coulomb - c1, 8, 7)
        c3 = coulomb - c1 - c2
        pieces = jnp.pad(jnp.stack([c1, c2, c3]).astype(BF16), ((0, 13), (0, 0)))
        held = jnp.concatenate([p.reshape(nk * nt, gl), pieces], axis=0)
        full = lax.all_gather(widen(held), "ga", axis=1, tiled=True)
        p_rows = full[: nk * nt].reshape(nk, nt, 4 * QW)
        p_rows = lax.dynamic_slice_in_dim(p_rows, a * rows, rows, axis=1)
        p_big = lax.all_gather(p_rows, "ka", axis=0, tiled=True)
        c_full = jnp.sum(full[nk * nt : nk * nt + 3].astype(F32), axis=0, keepdims=True)
        weighted = full[: nk * nt].astype(F32) * c_full
        w_hi = lax.reduce_precision(weighted, 8, 7)
        w_lo = (weighted - w_hi).astype(BF16)
        w_hi = w_hi.astype(BF16)

    with jax.named_scope("tables"):
        every = lax.all_gather(pairs, "ka", axis=0, tiled=True).reshape(n_ka, npair, 3)

        def routes(rows):
            slot = jnp.sum(
                jnp.where(
                    rows[..., 2, None] == jnp.arange(q_slot.shape[0]), q_slot, 0
                ),
                axis=-1,
            )
            q_owner = slot // qs
            k_owner = rows[..., 1] // nk
            return slot % qs, q_owner, rank_in_group(q_owner), k_owner, rank_in_group(k_owner)

        local, q_owner, q_rank, k_owner, k_rank = routes(every)
        ranks = jnp.arange(CAP)
        hot_q = (q_owner == me)[..., None] & (q_rank[..., None] == ranks)
        hot_k = (k_owner == me)[..., None] & (k_rank[..., None] == ranks)

        def pick(hot, v):
            return jnp.sum(jnp.where(hot, v[..., None], 0), axis=1).reshape(nslot)

        ones = jnp.ones_like(local)
        tab = jnp.stack(
            [
                pick(hot_q, ones),
                pick(hot_q, every[..., 0]),
                pick(hot_q, every[..., 1]),
                pick(hot_q, local),
                pick(hot_k, ones),
                pick(hot_k, every[..., 1] - me * nk),
                pick(hot_k, every[..., 0]),
            ]
        )
        _, o1, r1, _, _ = routes(pairs)
        own = jnp.stack([pairs[:, 0] - me * nk, pairs[:, 1], o1, r1])

    with jax.named_scope("plan"):
        npos = nslot + qs * CH
        used, slot = tab[0], tab[3]
        same = (slot[:, None] == slot[None, :]) & (used[None, :] == 1)
        order = jnp.arange(nslot)
        rank = jnp.sum((same & (order[:, None] > order[None, :])).astype(jnp.int32), axis=1)
        first = jnp.sum(used * (slot == 0))
        second = jnp.sum(used * (slot == 1))
        chunks_first = (first + CH - 1) // CH
        chunks = chunks_first + (second + CH - 1) // CH
        pos = jnp.where(slot == 0, rank, chunks_first * CH + rank)
        hot = (pos[None, :] == jnp.arange(npos)[:, None]) & (used == 1)[None, :]

        def at_pos(v, hot):
            return jnp.sum(jnp.where(hot, v[None, :], 0), axis=1)

        heads = jnp.pad(jnp.stack([chunks_first, chunks, a % 2]), (0, npos - 3))
        plan = jnp.stack(
            [at_pos(order - nslot, hot) + nslot, at_pos(tab[1], hot), at_pos(tab[2], hot), heads]
        )
        named = tab[4]
        rank = jnp.sum(jnp.where(order[:, None] > order[None, :], named[None, :], 0), axis=1)
        hot = (rank[None, :] == order[:, None]) & (named == 1)[None, :]
        total = jnp.broadcast_to(jnp.sum(named), (nslot,))
        firsts = jnp.stack([at_pos(tab[6], hot), at_pos(tab[5], hot), total])
    keep, away = pl.pallas_call(
        direct_kernel,
        out_shape=(jax.ShapeDtypeStruct((nslot, 8, 128), F32),) * 2,
        in_specs=[SMEM, ANY, ANY],
        out_specs=tuple(in_vmem(2)),
        scratch_shapes=[
            pltpu.VMEM((qs, 4 * QW, 2 * QW), BF16),
            pltpu.VMEM((2, CH, nt, 2 * QW), BF16),
            pltpu.VMEM((3, CH, nt, 2 * QW), BF16),
            pltpu.VMEM((2, CH * half, 2 * QW), BF16),
            pltpu.VMEM((CH * half, 128), F32),
            pltpu.VMEM((nslot + 1, 8, 128), F32),
            pltpu.VMEM((nslot + 1, 8, 128), F32),
            pltpu.SemaphoreType.DMA((qs,)),
            pltpu.SemaphoreType.DMA((2, CH)),
            pltpu.SemaphoreType.DMA((3, CH)),
        ],
        compiler_params=pltpu.CompilerParams(vmem_limit_bytes=52 * 1024 * 1024),
        name="direct",
    )(plan, big, wk)
    with jax.named_scope("to_neighbour"):
        came = lax.ppermute(away, "ga", [(0, 1), (1, 0), (2, 3), (3, 2)])
    send = pl.pallas_call(
        route_kernel,
        out_shape=jax.ShapeDtypeStruct((n_ka, CAP + nk, 8, 128), F32),
        in_specs=[SMEM, ANY, ANY],
        out_specs=pl.BlockSpec(memory_space=pltpu.VMEM),
        scratch_shapes=[
            pltpu.VMEM((nslot, 8, 128), F32),
            pltpu.VMEM((nslot, 8, 128), F32),
            pltpu.SemaphoreType.DMA((2,)),
        ],
        compiler_params=pltpu.CompilerParams(vmem_limit_bytes=8 * 1024 * 1024),
        name="route",
    )(tab, keep, came)
    with jax.named_scope("to_holders"):
        got = lax.all_to_all(send, "ka", 0, 0, tiled=True)
    n = npair + nk
    mine = pl.pallas_call(
        collect_kernel,
        out_shape=jax.ShapeDtypeStruct((n, 8, 128), F32),
        in_specs=[SMEM, ANY],
        out_specs=pl.BlockSpec(memory_space=pltpu.VMEM),
        scratch_shapes=[pltpu.VMEM(send.shape, F32), pltpu.SemaphoreType.DMA],
        compiler_params=pltpu.CompilerParams(vmem_limit_bytes=8 * 1024 * 1024),
        name="collect",
    )(own, got)
    with jax.named_scope("direct_copies"):
        others = [lax.ppermute(mine, "ga", shift(r)) for r in range(1, 4)]
        place = jnp.stack([(a - r) % 4 for r in range(4)])
    dmat = pl.pallas_call(
        arrange_kernel,
        out_shape=jax.ShapeDtypeStruct((n, nt, nt), F32),
        in_specs=[SMEM, ANY, ANY, ANY, ANY],
        out_specs=pl.BlockSpec(memory_space=pltpu.VMEM),
        scratch_shapes=[pltpu.VMEM((4, n, 8, 128), F32), pltpu.SemaphoreType.DMA((4,))],
        compiler_params=pltpu.CompilerParams(vmem_limit_bytes=8 * 1024 * 1024),
        name="arrange",
    )(place, mine, *others)
    exch = pl.pallas_call(
        exchange_kernel,
        out_shape=jax.ShapeDtypeStruct((n, 8, 128), F32),
        in_specs=[SMEM, SMEM, ANY, ANY, *in_vmem(4)],
        out_specs=pl.BlockSpec(memory_space=pltpu.VMEM),
        scratch_shapes=[
            pltpu.VMEM((nslot, rows, 4 * QW), BF16),
            pltpu.VMEM((npair, rows, 4 * QW), BF16),
            pltpu.VMEM((nk, rows, 4 * QW), F32),
            pltpu.VMEM((nk, npair * rows, nt), F32),
            pltpu.VMEM((n * rows, nt), F32),
            pltpu.SemaphoreType.DMA((nslot,)),
            pltpu.SemaphoreType.DMA((npair,)),
        ],
        compiler_params=pltpu.CompilerParams(vmem_limit_bytes=50 * 1024 * 1024),
        name="exchange",
    )(firsts, own, p_big, others[2], full, w_hi, w_lo, c_full)
    with jax.named_scope("exchange_copies"):
        exch_others = [lax.ppermute(exch, "ga", shift(r)) for r in range(1, 4)]
    return pl.pallas_call(
        finish_kernel,
        out_shape=(
            jax.ShapeDtypeStruct((npair, nt * nt), F32),
            jax.ShapeDtypeStruct((nk, nt * nt), F32),
        ),
        in_specs=[SMEM, *in_vmem(2), ANY, ANY, ANY],
        out_specs=tuple(in_vmem(2)),
        scratch_shapes=[
            pltpu.VMEM((4, n, 8, 128), F32),
            pltpu.VMEM((n, nt, nt), F32),
            pltpu.VMEM((n, nt, nt), F32),
            pltpu.VMEM((n * half, 2 * nt), F32),
            pltpu.SemaphoreType.DMA((4,)),
        ],
        compiler_params=pltpu.CompilerParams(vmem_limit_bytes=16 * 1024 * 1024),
        name="finish",
    )(place, dmat, exch, *exch_others)


def solution(mesh):
    in_specs = (
        P("ka", None, "ga"),
        P("ka", None, "ga"),
        P("ka", None, "ga"),
        P("ga"),
        P("ka", "ga", None),
        P("ka", None),
        P(),
    )
    out_specs = (P("ka", None), P("ka", None))
    return jax.shard_map(
        per_device, mesh=mesh, in_specs=in_specs, out_specs=out_specs, check_vma=False
    )
```

```python
import jax
import jax.numpy as jnp
from jax import lax
from jax.experimental import pallas as pl
from jax.experimental.pallas import tpu as pltpu
from jax.sharding import PartitionSpec as P

CAP = 2
QW = 384
CH = 8
F32 = jnp.float32
BF16 = jnp.bfloat16
NT_DIMS = (((1,), (1,)), ((), ()))


def rank_in_group(owners):
    n = owners.shape[-1]
    same = owners[..., :, None] == owners[..., None, :]
    before = jnp.arange(n)[:, None] > jnp.arange(n)[None, :]
    return jnp.sum(jnp.logical_and(same, before).astype(jnp.int32), axis=-1)


def widen(v):
    return jnp.pad(v, ((0, 0),) * (v.ndim - 1) + ((0, QW - v.shape[-1]),))


def flat_tiles(tmp, rows):
    even = tmp[pl.ds(0, rows // 2, stride=2), :]
    odd = tmp[pl.ds(1, rows // 2, stride=2), :]
    return jnp.concatenate([even, odd], axis=1)


def direct_kernel(plan, big, w, keep, away, xs, ys, us, prod, kept, sent, sx, sy):
    half = prod.shape[0] // CH
    nt = 2 * half
    deep = xs.shape[3]
    nslot = keep.shape[0]
    chunks_first, chunks, parity = plan[3, 0], plan[3, 1], plan[3, 2]

    def x_copy(pos, buf, i):
        return pltpu.make_async_copy(big.at[plan[1, pos], pl.ds(0, nt)], xs.at[buf, i], sx.at[buf, i])

    def y_copy(pos, buf, i):
        return pltpu.make_async_copy(big.at[plan[2, pos], pl.ds(nt, nt)], ys.at[buf, i], sy.at[buf, i])

    def begin(c):
        for i in range(CH):
            x_copy(c * CH + i, lax.rem(c, 2), i).start()
            y_copy(c * CH + i, lax.rem(c, 3), i).start()

    def products(c):
        u = us[lax.rem(c + 2, 2)]
        y = ys[lax.rem(c + 3, 3)].reshape(CH * nt, deep)
        for i in range(0, CH, 4):
            d = lax.dot_general(
                u[half * i : half * (i + 4)],
                y[nt * i : nt * (i + 4)],
                NT_DIMS,
                preferred_element_type=F32,
            )
            for j in range(2):
                prod[half * i + nt * j : half * i + nt * j + nt] = d[
                    nt * j : nt * j + nt, 128 * j : 128 * j + 128
                ]
        lane = lax.broadcasted_iota(jnp.int32, (8, 128), 1)
        for i in range(CH):
            t = jnp.where(c < 0, nslot, plan[0, jnp.maximum(c, 0) * CH + i])
            rows = [prod[half * i + 8 * g : half * i + 8 * g + 8] for g in range(4)]
            tiles = []
            for h in range(2):
                start = nt * (i % 2) + half * h
                moved = [pltpu.roll(v, (half * g - start) % 128, 1) for g, v in enumerate(rows)]
                low = jnp.where(lane < half, moved[0], moved[1])
                high = jnp.where(lane < 3 * half, moved[2], moved[3])
                tiles.append(jnp.where(lane < nt, low, high))
            kept[t] = jnp.where(parity == 0, tiles[0], tiles[1])
            sent[t] = jnp.where(parity == 0, tiles[1], tiles[0])

    @pl.when(chunks > 0)
    def _():
        begin(0)

    def chunk(c, carry):
        @pl.when(c + 1 < chunks)
        def _():
            begin(c + 1)

        bx, by = lax.rem(c, 2), lax.rem(c, 3)
        for i in range(CH):
            x_copy(c * CH + i, bx, i).wait()
            y_copy(c * CH + i, by, i).wait()
        products(c - 1)
        slot = jnp.where(c < chunks_first, 0, 1)
        u = jnp.dot(
            xs[bx, :, :half].reshape(CH * half, deep), w[slot, :deep], preferred_element_type=F32
        )
        u = u + jnp.dot(
            xs[bx, :, half:].reshape(CH * half, deep), w[slot, deep:], preferred_element_type=F32
        )
        us[bx] = u.astype(BF16)
        return carry

    lax.fori_loop(0, chunks, chunk, 0)

    @pl.when(chunks > 0)
    def _():
        products(chunks - 1)

    keep[...] = kept[:nslot]
    away[...] = sent[:nslot]


def route_kernel(tab, keep, came, send, mine, theirs, sem):
    copies = [
        pltpu.make_async_copy(keep, mine, sem.at[0]),
        pltpu.make_async_copy(came, theirs, sem.at[1]),
    ]
    for c in copies:
        c.start()
    nk = send.shape[1] - CAP
    send[:, CAP:] = jnp.zeros((send.shape[0], nk, *send.shape[2:]), F32)
    for c in copies:
        c.wait()
    for t in range(tab.shape[1]):
        v = mine[t] + theirs[t]
        send[t // CAP, t % CAP] = v

        @pl.when(tab[0, t] == 1)
        def _():
            owner = tab[2, t] // nk
            row = CAP + tab[2, t] % nk
            send[owner, row] = send[owner, row] + v


def exchange_kernel(
    firsts, own, big, early, full, whi, wlo, cw, out, p1, p2, tot, prod, flat, s1, s2
):
    count = firsts[2, 0]
    npair = own.shape[1]
    nk, rows, wide = tot.shape
    nt = whi.shape[0] // nk

    def second(j):
        return pltpu.make_async_copy(big.at[own[1, j]], p2.at[j], s2.at[j])

    def first(t):
        return pltpu.make_async_copy(big.at[firsts[0, t]], p1.at[t], s1.at[t])


    def begin(t, carry):
        first(t).start()
        return carry

    lax.fori_loop(0, count, begin, 0)
    for j in range(npair):
        second(j).start()
    tot[...] = jnp.zeros_like(tot)
    def gather(t, carry):
        first(t).wait()
        k = firsts[1, t]
        tot[k] = tot[k] + p1[t].astype(F32)
        return carry

    lax.fori_loop(0, count, gather, 0)
    for j in range(npair):
        second(j).wait()

    def contract(left, right):
        return lax.dot_general(left, right, NT_DIMS, preferred_element_type=F32)

    b = p2[...].reshape(npair * rows, wide)
    e = contract(b, whi[...]) + contract(b, wlo[...])
    e = e + e
    for k in range(nk):
        prod[k] = e[:, k * nt : (k + 1) * nt]
    for j in range(npair):
        r = pl.ds(j * rows, rows)
        flat[r, :] = prod[own[0, j], r, :]

    w = tot[...].reshape(nk * rows, wide) * cw[...]
    hi = w.astype(BF16)
    lo = (w - hi.astype(F32)).astype(BF16)
    m = contract(jnp.concatenate([hi, lo], axis=0), full[: nk * nt])
    m = m[: nk * rows] + m[nk * rows :]
    m = m + m
    for k in range(nk):
        flat[pl.ds((npair + k) * rows, rows), :] = m[
            k * rows : (k + 1) * rows, k * nt : (k + 1) * nt
        ]
    z = flat_tiles(flat, (npair + nk) * rows)
    for j in range(npair + nk):
        out[j] = z[8 * j : 8 * j + 8]


def collect_kernel(own, got, out, here, sem):
    copy = pltpu.make_async_copy(got, here, sem)
    copy.start()
    copy.wait()
    nk = got.shape[1] - CAP
    npair = own.shape[1]
    for j in range(npair):
        out[j] = here[own[2, j], own[3, j]]
    for k in range(nk):
        out[npair + k] = jnp.sum(here[:, CAP + k], axis=0)


def bring(place, refs, whole, sem):
    copies = [
        pltpu.make_async_copy(r, whole.at[place[i]], sem.at[i]) for i, r in enumerate(refs)
    ]
    for c in copies:
        c.start()
    for c in copies:
        c.wait()


def arrange_kernel(place, r0, r1, r2, r3, dmat, whole, sem):
    bring(place, (r0, r1, r2, r3), whole, sem)
    half = dmat.shape[1] // 2
    for j in range(dmat.shape[0]):
        for a in range(2):
            left, right = whole[2 * a, j], whole[2 * a + 1, j]
            for g in range(4):
                cut = slice(half * g, half * (g + 1))
                dmat[j, pl.ds(half * a + 8 * g, 8), :] = jnp.concatenate(
                    [left[:, cut], right[:, cut]], axis=1
                )


def finish_kernel(place, dmat, r0, r1, r2, r3, blocks, mirrored, whole, emat, bmat, rows, sem):
    bring(place, (r0, r1, r2, r3), whole, sem)
    npair, nk = blocks.shape[0], mirrored.shape[0]
    nt = dmat.shape[1]
    half = nt // 2
    n = npair + nk
    for j in range(n):
        for a in range(4):
            tile = whole[a, j]
            emat[j, pl.ds(16 * a, 8, stride=2), :] = tile[:, :nt]
            emat[j, pl.ds(16 * a + 1, 8, stride=2), :] = tile[:, nt:]
    for j in range(n):
        if j < npair:
            bmat[j] = emat[j].T - dmat[j]
        else:
            bmat[j] = (emat[j] - dmat[j]).T
        even = bmat[j, pl.ds(0, half, stride=2), :]
        odd = bmat[j, pl.ds(1, half, stride=2), :]
        rows[pl.ds(j * half, half), :] = jnp.concatenate([even, odd], axis=1)
    for r in range(half):
        lanes = pl.ds(2 * nt * r, 2 * nt)
        blocks[:, lanes] = rows[pl.ds(r, npair, stride=half), :]
        mirrored[:, lanes] = rows[pl.ds(npair * half + r, nk, stride=half), :]


def in_vmem(count):
    return [pl.BlockSpec(memory_space=pltpu.VMEM)] * count


SMEM = pl.BlockSpec(memory_space=pltpu.SMEM)
ANY = pl.BlockSpec(memory_space=pl.ANY)


def per_device(x, y, p, coulomb, w, pairs, q_slot):
    n_ka = lax.axis_size("ka")
    me = lax.axis_index("ka")
    a = lax.axis_index("ga")
    nk, nt, gl = x.shape
    qs = w.shape[0]
    npair = pairs.shape[0]
    nslot = n_ka * CAP

    half, rows = nt // 2, nt // 4

    def shift(r):
        return [(i, (i + r) % 4) for i in range(4)]

    with jax.named_scope("pack"):
        y_far = lax.ppermute(y, "ga", [(i, 3 - i) for i in range(4)])
        cut = [jnp.where((a + r) % 4 < 2, x[:, :half], x[:, half:]) for r in range(4)]
        cut = cut[:1] + [lax.ppermute(cut[r], "ga", shift(r)) for r in range(1, 4)]

        def side(left, right):
            return jnp.concatenate([widen(left), widen(right)], axis=2)

        y_both = side(jnp.where(a < 2, y, y_far), jnp.where(a < 2, y_far, y))
        payload = jnp.concatenate([side(cut[0], cut[1]), side(cut[2], cut[3]), y_both], axis=1)
    with jax.named_scope("spread"):
        big = lax.all_gather(payload, "ka", axis=0, tiled=True)

    with jax.named_scope("weights"):
        cols = [
            jnp.pad(w[:, :, i * gl : (i + 1) * gl], ((0, 0), (0, QW - gl), (0, QW - gl)))
            for i in range(4)
        ]
        outer = jnp.concatenate([cols[0], cols[3]], axis=2)
        inner = jnp.concatenate([cols[1], cols[2]], axis=2)
        wk = []
        for r in range(4):
            to = (a + r) % 4
            v = jnp.where((to == 0) | (to == 3), outer, inner)
            wk.append(lax.ppermute(v, "ga", shift(r)) if r else v)
        wk = jnp.concatenate(wk, axis=1)

    with jax.named_scope("exchange_pack"):
        c1 = lax.reduce_precision(coulomb, 8, 7)
        c2 = lax.reduce_precision(coulomb - c1, 8, 7)
        c3 = coulomb - c1 - c2
        pieces = jnp.pad(jnp.stack([c1, c2, c3]).astype(BF16), ((0, 13), (0, 0)))
        held = jnp.concatenate([p.reshape(nk * nt, gl), pieces], axis=0)
        full = lax.all_gather(widen(held), "ga", axis=1, tiled=True)
        p_rows = full[: nk * nt].reshape(nk, nt, 4 * QW)
        p_rows = lax.dynamic_slice_in_dim(p_rows, a * rows, rows, axis=1)
        p_big = lax.all_gather(p_rows, "ka", axis=0, tiled=True)
        c_full = jnp.sum(full[nk * nt : nk * nt + 3].astype(F32), axis=0, keepdims=True)
        weighted = full[: nk * nt].astype(F32) * c_full
        w_hi = lax.reduce_precision(weighted, 8, 7)
        w_lo = (weighted - w_hi).astype(BF16)
        w_hi = w_hi.astype(BF16)

    with jax.named_scope("tables"):
        every = lax.all_gather(pairs, "ka", axis=0, tiled=True).reshape(n_ka, npair, 3)

        def routes(rows):
            slot = jnp.sum(
                jnp.where(
                    rows[..., 2, None] == jnp.arange(q_slot.shape[0]), q_slot, 0
                ),
                axis=-1,
            )
            q_owner = slot // qs
            k_owner = rows[..., 1] // nk
            return slot % qs, q_owner, rank_in_group(q_owner), k_owner, rank_in_group(k_owner)

        local, q_owner, q_rank, k_owner, k_rank = routes(every)
        ranks = jnp.arange(CAP)
        hot_q = (q_owner == me)[..., None] & (q_rank[..., None] == ranks)
        hot_k = (k_owner == me)[..., None] & (k_rank[..., None] == ranks)

        def pick(hot, v):
            return jnp.sum(jnp.where(hot, v[..., None], 0), axis=1).reshape(nslot)

        ones = jnp.ones_like(local)
        tab = jnp.stack(
            [
                pick(hot_q, ones),
                pick(hot_q, every[..., 0]),
                pick(hot_q, every[..., 1]),
                pick(hot_q, local),
                pick(hot_k, ones),
                pick(hot_k, every[..., 1] - me * nk),
                pick(hot_k, every[..., 0]),
            ]
        )
        _, o1, r1, _, _ = routes(pairs)
        own = jnp.stack([pairs[:, 0] - me * nk, pairs[:, 1], o1, r1])

    with jax.named_scope("plan"):
        npos = nslot + qs * CH
        used, slot = tab[0], tab[3]
        same = (slot[:, None] == slot[None, :]) & (used[None, :] == 1)
        order = jnp.arange(nslot)
        rank = jnp.sum((same & (order[:, None] > order[None, :])).astype(jnp.int32), axis=1)
        first = jnp.sum(used * (slot == 0))
        second = jnp.sum(used * (slot == 1))
        chunks_first = (first + CH - 1) // CH
        chunks = chunks_first + (second + CH - 1) // CH
        pos = jnp.where(slot == 0, rank, chunks_first * CH + rank)
        hot = (pos[None, :] == jnp.arange(npos)[:, None]) & (used == 1)[None, :]

        def at_pos(v, hot):
            return jnp.sum(jnp.where(hot, v[None, :], 0), axis=1)

        heads = jnp.pad(jnp.stack([chunks_first, chunks, a % 2]), (0, npos - 3))
        plan = jnp.stack(
            [at_pos(order - nslot, hot) + nslot, at_pos(tab[1], hot), at_pos(tab[2], hot), heads]
        )
        named = tab[4]
        rank = jnp.sum(jnp.where(order[:, None] > order[None, :], named[None, :], 0), axis=1)
        hot = (rank[None, :] == order[:, None]) & (named == 1)[None, :]
        total = jnp.broadcast_to(jnp.sum(named), (nslot,))
        firsts = jnp.stack([at_pos(tab[6], hot), at_pos(tab[5], hot), total])
    keep, away = pl.pallas_call(
        direct_kernel,
        out_shape=(jax.ShapeDtypeStruct((nslot, 8, 128), F32),) * 2,
        in_specs=[SMEM, ANY, *in_vmem(1)],
        out_specs=tuple(in_vmem(2)),
        scratch_shapes=[
            pltpu.VMEM((2, CH, nt, 2 * QW), BF16),
            pltpu.VMEM((3, CH, nt, 2 * QW), BF16),
            pltpu.VMEM((2, CH * half, 2 * QW), BF16),
            pltpu.VMEM((CH * half, 128), F32),
            pltpu.VMEM((nslot + 1, 8, 128), F32),
            pltpu.VMEM((nslot + 1, 8, 128), F32),
            pltpu.SemaphoreType.DMA((2, CH)),
            pltpu.SemaphoreType.DMA((3, CH)),
        ],
        compiler_params=pltpu.CompilerParams(vmem_limit_bytes=32 * 1024 * 1024),
        name="direct",
    )(plan, big, wk)
    with jax.named_scope("to_neighbour"):
        came = lax.ppermute(away, "ga", [(0, 1), (1, 0), (2, 3), (3, 2)])
    send = pl.pallas_call(
        route_kernel,
        out_shape=jax.ShapeDtypeStruct((n_ka, CAP + nk, 8, 128), F32),
        in_specs=[SMEM, ANY, ANY],
        out_specs=pl.BlockSpec(memory_space=pltpu.VMEM),
        scratch_shapes=[
            pltpu.VMEM((nslot, 8, 128), F32),
            pltpu.VMEM((nslot, 8, 128), F32),
            pltpu.SemaphoreType.DMA((2,)),
        ],
        compiler_params=pltpu.CompilerParams(vmem_limit_bytes=8 * 1024 * 1024),
        name="route",
    )(tab, keep, came)
    with jax.named_scope("to_holders"):
        got = lax.all_to_all(send, "ka", 0, 0, tiled=True)
    n = npair + nk
    mine = pl.pallas_call(
        collect_kernel,
        out_shape=jax.ShapeDtypeStruct((n, 8, 128), F32),
        in_specs=[SMEM, ANY],
        out_specs=pl.BlockSpec(memory_space=pltpu.VMEM),
        scratch_shapes=[pltpu.VMEM(send.shape, F32), pltpu.SemaphoreType.DMA],
        compiler_params=pltpu.CompilerParams(vmem_limit_bytes=8 * 1024 * 1024),
        name="collect",
    )(own, got)
    with jax.named_scope("direct_copies"):
        others = [lax.ppermute(mine, "ga", shift(r)) for r in range(1, 4)]
        place = jnp.stack([(a - r) % 4 for r in range(4)])
    dmat = pl.pallas_call(
        arrange_kernel,
        out_shape=jax.ShapeDtypeStruct((n, nt, nt), F32),
        in_specs=[SMEM, ANY, ANY, ANY, ANY],
        out_specs=pl.BlockSpec(memory_space=pltpu.VMEM),
        scratch_shapes=[pltpu.VMEM((4, n, 8, 128), F32), pltpu.SemaphoreType.DMA((4,))],
        compiler_params=pltpu.CompilerParams(vmem_limit_bytes=8 * 1024 * 1024),
        name="arrange",
    )(place, mine, *others)
    exch = pl.pallas_call(
        exchange_kernel,
        out_shape=jax.ShapeDtypeStruct((n, 8, 128), F32),
        in_specs=[SMEM, SMEM, ANY, ANY, *in_vmem(4)],
        out_specs=pl.BlockSpec(memory_space=pltpu.VMEM),
        scratch_shapes=[
            pltpu.VMEM((nslot, rows, 4 * QW), BF16),
            pltpu.VMEM((npair, rows, 4 * QW), BF16),
            pltpu.VMEM((nk, rows, 4 * QW), F32),
            pltpu.VMEM((nk, npair * rows, nt), F32),
            pltpu.VMEM((n * rows, nt), F32),
            pltpu.SemaphoreType.DMA((nslot,)),
            pltpu.SemaphoreType.DMA((npair,)),
        ],
        compiler_params=pltpu.CompilerParams(vmem_limit_bytes=50 * 1024 * 1024),
        name="exchange",
    )(firsts, own, p_big, others[2], full, w_hi, w_lo, c_full)
    with jax.named_scope("exchange_copies"):
        exch_others = [lax.ppermute(exch, "ga", shift(r)) for r in range(1, 4)]
    return pl.pallas_call(
        finish_kernel,
        out_shape=(
            jax.ShapeDtypeStruct((npair, nt * nt), F32),
            jax.ShapeDtypeStruct((nk, nt * nt), F32),
        ),
        in_specs=[SMEM, *in_vmem(2), ANY, ANY, ANY],
        out_specs=tuple(in_vmem(2)),
        scratch_shapes=[
            pltpu.VMEM((4, n, 8, 128), F32),
            pltpu.VMEM((n, nt, nt), F32),
            pltpu.VMEM((n, nt, nt), F32),
            pltpu.VMEM((n * half, 2 * nt), F32),
            pltpu.SemaphoreType.DMA((4,)),
        ],
        compiler_params=pltpu.CompilerParams(vmem_limit_bytes=16 * 1024 * 1024),
        name="finish",
    )(place, dmat, exch, *exch_others)


def solution(mesh):
    in_specs = (
        P("ka", None, "ga"),
        P("ka", None, "ga"),
        P("ka", None, "ga"),
        P("ga"),
        P("ka", "ga", None),
        P("ka", None),
        P(),
    )
    out_specs = (P("ka", None), P("ka", None))
    return jax.shard_map(
        per_device, mesh=mesh, in_specs=in_specs, out_specs=out_specs, check_vma=False
    )
```

```python
import jax
import jax.numpy as jnp
from jax import lax
from jax.experimental import pallas as pl
from jax.experimental.pallas import tpu as pltpu
from jax.sharding import PartitionSpec as P

CAP = 2
QW = 384
CH = 8
F32 = jnp.float32
BF16 = jnp.bfloat16
NT_DIMS = (((1,), (1,)), ((), ()))


def rank_in_group(owners):
    n = owners.shape[-1]
    same = owners[..., :, None] == owners[..., None, :]
    before = jnp.arange(n)[:, None] > jnp.arange(n)[None, :]
    return jnp.sum(jnp.logical_and(same, before).astype(jnp.int32), axis=-1)


def widen(v):
    return jnp.pad(v, ((0, 0),) * (v.ndim - 1) + ((0, QW - v.shape[-1]),))


def flat_tiles(tmp, rows):
    even = tmp[pl.ds(0, rows // 2, stride=2), :]
    odd = tmp[pl.ds(1, rows // 2, stride=2), :]
    return jnp.concatenate([even, odd], axis=1)


def direct_kernel(plan, big, w, keep, away, xs, ys, us, prod, kept, sent, sx, sy):
    half = prod.shape[0] // CH
    nt = 2 * half
    deep = xs.shape[3]
    nslot = keep.shape[0]
    chunks_first, chunks, parity = plan[3, 0], plan[3, 1], plan[3, 2]

    def x_copy(pos, buf, i):
        return pltpu.make_async_copy(big.at[plan[1, pos], pl.ds(0, nt)], xs.at[buf, i], sx.at[buf, i])

    def y_copy(pos, buf, i):
        return pltpu.make_async_copy(big.at[plan[2, pos], pl.ds(nt, nt)], ys.at[buf, i], sy.at[buf, i])

    def begin(c):
        for i in range(CH):
            x_copy(c * CH + i, lax.rem(c, 2), i).start()
            y_copy(c * CH + i, lax.rem(c, 3), i).start()

    def products(c):
        u = us[lax.rem(c + 2, 2)]
        y = ys[lax.rem(c + 3, 3)].reshape(CH * nt, deep)
        for i in range(0, CH, 4):
            d = lax.dot_general(
                u[half * i : half * (i + 4)],
                y[nt * i : nt * (i + 4)],
                NT_DIMS,
                preferred_element_type=F32,
            )
            for j in range(2):
                prod[half * i + nt * j : half * i + nt * j + nt] = d[
                    nt * j : nt * j + nt, 128 * j : 128 * j + 128
                ]
        lane = lax.broadcasted_iota(jnp.int32, (8, 128), 1)
        for i in range(CH):
            t = jnp.where(c < 0, nslot, plan[0, jnp.maximum(c, 0) * CH + i])
            rows = [prod[half * i + 8 * g : half * i + 8 * g + 8] for g in range(4)]
            tiles = []
            for h in range(2):
                start = nt * (i % 2) + half * h
                moved = [pltpu.roll(v, (half * g - start) % 128, 1) for g, v in enumerate(rows)]
                low = jnp.where(lane < half, moved[0], moved[1])
                high = jnp.where(lane < 3 * half, moved[2], moved[3])
                tiles.append(jnp.where(lane < nt, low, high))
            kept[t] = jnp.where(parity == 0, tiles[0], tiles[1])
            sent[t] = jnp.where(parity == 0, tiles[1], tiles[0])

    @pl.when(chunks > 0)
    def _():
        begin(0)

    def chunk(c, carry):
        @pl.when(c + 1 < chunks)
        def _():
            begin(c + 1)

        bx, by = lax.rem(c, 2), lax.rem(c, 3)
        for i in range(CH):
            x_copy(c * CH + i, bx, i).wait()
            y_copy(c * CH + i, by, i).wait()
        products(c - 1)
        slot = jnp.where(c < chunks_first, 0, 1)
        u = jnp.dot(
            xs[bx, :, :half].reshape(CH * half, deep), w[slot, :deep], preferred_element_type=F32
        )
        u = u + jnp.dot(
            xs[bx, :, half:].reshape(CH * half, deep), w[slot, deep:], preferred_element_type=F32
        )
        us[bx] = u.astype(BF16)
        return carry

    lax.fori_loop(0, chunks, chunk, 0)

    @pl.when(chunks > 0)
    def _():
        products(chunks - 1)

    keep[...] = kept[:nslot]
    away[...] = sent[:nslot]


def route_kernel(tab, keep, came, send, mine, theirs, sem):
    copies = [
        pltpu.make_async_copy(keep, mine, sem.at[0]),
        pltpu.make_async_copy(came, theirs, sem.at[1]),
    ]
    for c in copies:
        c.start()
    nk = send.shape[1] - CAP
    send[:, CAP:] = jnp.zeros((send.shape[0], nk, *send.shape[2:]), F32)
    for c in copies:
        c.wait()
    for t in range(tab.shape[1]):
        v = mine[t] + theirs[t]
        send[t // CAP, t % CAP] = v

        @pl.when(tab[0, t] == 1)
        def _():
            owner = tab[2, t] // nk
            row = CAP + tab[2, t] % nk
            send[owner, row] = send[owner, row] + v


def exchange_kernel(
    firsts, own, big, early, full, whi, wlo, cw, out, p1, p2, tot, prod, flat, s1, s2
):
    count = firsts[2, 0]
    npair = own.shape[1]
    nk, rows, wide = tot.shape
    nt = whi.shape[0] // nk

    def second(j):
        return pltpu.make_async_copy(big.at[own[1, j]], p2.at[j], s2.at[j])

    def first(t):
        return pltpu.make_async_copy(big.at[firsts[0, t]], p1.at[t], s1.at[t])

    for j in range(npair):
        second(j).start()

    def begin(t, carry):
        first(t).start()
        return carry

    lax.fori_loop(0, count, begin, 0)
    tot[...] = jnp.zeros_like(tot)
    def gather(t, carry):
        first(t).wait()
        k = firsts[1, t]
        tot[k] = tot[k] + p1[t].astype(F32)
        return carry

    lax.fori_loop(0, count, gather, 0)
    for j in range(npair):
        second(j).wait()

    def contract(left, right):
        return lax.dot_general(left, right, NT_DIMS, preferred_element_type=F32)

    b = p2[...].reshape(npair * rows, wide)
    e = contract(b, whi[...]) + contract(b, wlo[...])
    e = e + e
    for k in range(nk):
        prod[k] = e[:, k * nt : (k + 1) * nt]
    for j in range(npair):
        r = pl.ds(j * rows, rows)
        flat[r, :] = prod[own[0, j], r, :]

    w = tot[...].reshape(nk * rows, wide) * cw[...]
    hi = w.astype(BF16)
    lo = (w - hi.astype(F32)).astype(BF16)
    m = contract(jnp.concatenate([hi, lo], axis=0), full[: nk * nt])
    m = m[: nk * rows] + m[nk * rows :]
    m = m + m
    for k in range(nk):
        flat[pl.ds((npair + k) * rows, rows), :] = m[
            k * rows : (k + 1) * rows, k * nt : (k + 1) * nt
        ]
    z = flat_tiles(flat, (npair + nk) * rows)
    for j in range(npair + nk):
        out[j] = z[8 * j : 8 * j + 8]


def collect_kernel(own, got, out, here, sem):
    copy = pltpu.make_async_copy(got, here, sem)
    copy.start()
    copy.wait()
    nk = got.shape[1] - CAP
    npair = own.shape[1]
    for j in range(npair):
        out[j] = here[own[2, j], own[3, j]]
    for k in range(nk):
        out[npair + k] = jnp.sum(here[:, CAP + k], axis=0)


def bring(place, refs, whole, sem):
    copies = [
        pltpu.make_async_copy(r, whole.at[place[i]], sem.at[i]) for i, r in enumerate(refs)
    ]
    for c in copies:
        c.start()
    for c in copies:
        c.wait()


def arrange_kernel(place, r0, r1, r2, r3, dmat, whole, sem):
    bring(place, (r0, r1, r2, r3), whole, sem)
    half = dmat.shape[1] // 2
    for j in range(dmat.shape[0]):
        for a in range(2):
            left, right = whole[2 * a, j], whole[2 * a + 1, j]
            for g in range(4):
                cut = slice(half * g, half * (g + 1))
                dmat[j, pl.ds(half * a + 8 * g, 8), :] = jnp.concatenate(
                    [left[:, cut], right[:, cut]], axis=1
                )


def finish_kernel(place, dmat, r0, r1, r2, r3, blocks, mirrored, whole, emat, bmat, rows, sem):
    bring(place, (r0, r1, r2, r3), whole, sem)
    npair, nk = blocks.shape[0], mirrored.shape[0]
    nt = dmat.shape[1]
    half = nt // 2
    n = npair + nk
    for j in range(n):
        for a in range(4):
            tile = whole[a, j]
            emat[j, pl.ds(16 * a, 8, stride=2), :] = tile[:, :nt]
            emat[j, pl.ds(16 * a + 1, 8, stride=2), :] = tile[:, nt:]
    for j in range(n):
        if j < npair:
            bmat[j] = emat[j].T - dmat[j]
        else:
            bmat[j] = (emat[j] - dmat[j]).T
        even = bmat[j, pl.ds(0, half, stride=2), :]
        odd = bmat[j, pl.ds(1, half, stride=2), :]
        rows[pl.ds(j * half, half), :] = jnp.concatenate([even, odd], axis=1)
    for r in range(half):
        lanes = pl.ds(2 * nt * r, 2 * nt)
        blocks[:, lanes] = rows[pl.ds(r, npair, stride=half), :]
        mirrored[:, lanes] = rows[pl.ds(npair * half + r, nk, stride=half), :]


def in_vmem(count):
    return [pl.BlockSpec(memory_space=pltpu.VMEM)] * count


SMEM = pl.BlockSpec(memory_space=pltpu.SMEM)
ANY = pl.BlockSpec(memory_space=pl.ANY)


def per_device(x, y, p, coulomb, w, pairs, q_slot):
    n_ka = lax.axis_size("ka")
    me = lax.axis_index("ka")
    a = lax.axis_index("ga")
    nk, nt, gl = x.shape
    qs = w.shape[0]
    npair = pairs.shape[0]
    nslot = n_ka * CAP

    half, rows = nt // 2, nt // 4

    def shift(r):
        return [(i, (i + r) % 4) for i in range(4)]

    with jax.named_scope("pack"):
        y_far = lax.ppermute(y, "ga", [(i, 3 - i) for i in range(4)])
        cut = [jnp.where((a + r) % 4 < 2, x[:, :half], x[:, half:]) for r in range(4)]
        cut = cut[:1] + [lax.ppermute(cut[r], "ga", shift(r)) for r in range(1, 4)]

        def side(left, right):
            return jnp.concatenate([widen(left), widen(right)], axis=2)

        y_both = side(jnp.where(a < 2, y, y_far), jnp.where(a < 2, y_far, y))
        payload = jnp.concatenate([side(cut[0], cut[1]), side(cut[2], cut[3]), y_both], axis=1)
    with jax.named_scope("spread"):
        big = lax.all_gather(payload, "ka", axis=0, tiled=True)

    with jax.named_scope("weights"):
        cols = [
            jnp.pad(w[:, :, i * gl : (i + 1) * gl], ((0, 0), (0, QW - gl), (0, QW - gl)))
            for i in range(4)
        ]
        outer = jnp.concatenate([cols[0], cols[3]], axis=2)
        inner = jnp.concatenate([cols[1], cols[2]], axis=2)
        wk = []
        for r in range(4):
            to = (a + r) % 4
            v = jnp.where((to == 0) | (to == 3), outer, inner)
            wk.append(lax.ppermute(v, "ga", shift(r)) if r else v)
        wk = jnp.concatenate(wk, axis=1)

    with jax.named_scope("exchange_pack"):
        c1 = lax.reduce_precision(coulomb, 8, 7)
        c2 = lax.reduce_precision(coulomb - c1, 8, 7)
        c3 = coulomb - c1 - c2
        pieces = jnp.pad(jnp.stack([c1, c2, c3]).astype(BF16), ((0, 13), (0, 0)))
        held = jnp.concatenate([p.reshape(nk * nt, gl), pieces], axis=0)
        full = lax.all_gather(widen(held), "ga", axis=1, tiled=True)
        p_rows = full[: nk * nt].reshape(nk, nt, 4 * QW)
        p_rows = lax.dynamic_slice_in_dim(p_rows, a * rows, rows, axis=1)
        p_big = lax.all_gather(p_rows, "ka", axis=0, tiled=True)
        c_full = jnp.sum(full[nk * nt : nk * nt + 3].astype(F32), axis=0, keepdims=True)
        weighted = full[: nk * nt].astype(F32) * c_full
        w_hi = lax.reduce_precision(weighted, 8, 7)
        w_lo = (weighted - w_hi).astype(BF16)
        w_hi = w_hi.astype(BF16)

    with jax.named_scope("tables"):
        every = lax.all_gather(pairs, "ka", axis=0, tiled=True).reshape(n_ka, npair, 3)

        def routes(rows):
            slot = jnp.sum(
                jnp.where(
                    rows[..., 2, None] == jnp.arange(q_slot.shape[0]), q_slot, 0
                ),
                axis=-1,
            )
            q_owner = slot // qs
            k_owner = rows[..., 1] // nk
            return slot % qs, q_owner, rank_in_group(q_owner), k_owner, rank_in_group(k_owner)

        local, q_owner, q_rank, k_owner, k_rank = routes(every)
        ranks = jnp.arange(CAP)
        hot_q = (q_owner == me)[..., None] & (q_rank[..., None] == ranks)
        hot_k = (k_owner == me)[..., None] & (k_rank[..., None] == ranks)

        def pick(hot, v):
            return jnp.sum(jnp.where(hot, v[..., None], 0), axis=1).reshape(nslot)

        ones = jnp.ones_like(local)
        tab = jnp.stack(
            [
                pick(hot_q, ones),
                pick(hot_q, every[..., 0]),
                pick(hot_q, every[..., 1]),
                pick(hot_q, local),
                pick(hot_k, ones),
                pick(hot_k, every[..., 1] - me * nk),
                pick(hot_k, every[..., 0]),
            ]
        )
        _, o1, r1, _, _ = routes(pairs)
        own = jnp.stack([pairs[:, 0] - me * nk, pairs[:, 1], o1, r1])

    with jax.named_scope("plan"):
        npos = nslot + qs * CH
        used, slot = tab[0], tab[3]
        same = (slot[:, None] == slot[None, :]) & (used[None, :] == 1)
        order = jnp.arange(nslot)
        rank = jnp.sum((same & (order[:, None] > order[None, :])).astype(jnp.int32), axis=1)
        first = jnp.sum(used * (slot == 0))
        second = jnp.sum(used * (slot == 1))
        chunks_first = (first + CH - 1) // CH
        chunks = chunks_first + (second + CH - 1) // CH
        pos = jnp.where(slot == 0, rank, chunks_first * CH + rank)
        hot = (pos[None, :] == jnp.arange(npos)[:, None]) & (used == 1)[None, :]

        def at_pos(v, hot):
            return jnp.sum(jnp.where(hot, v[None, :], 0), axis=1)

        heads = jnp.pad(jnp.stack([chunks_first, chunks, a % 2]), (0, npos - 3))
        plan = jnp.stack(
            [at_pos(order - nslot, hot) + nslot, at_pos(tab[1], hot), at_pos(tab[2], hot), heads]
        )
        named = tab[4]
        rank = jnp.sum(jnp.where(order[:, None] > order[None, :], named[None, :], 0), axis=1)
        hot = (rank[None, :] == order[:, None]) & (named == 1)[None, :]
        total = jnp.broadcast_to(jnp.sum(named), (nslot,))
        firsts = jnp.stack([at_pos(tab[6], hot), at_pos(tab[5], hot), total])
    keep, away = pl.pallas_call(
        direct_kernel,
        out_shape=(jax.ShapeDtypeStruct((nslot, 8, 128), F32),) * 2,
        in_specs=[SMEM, ANY, *in_vmem(1)],
        out_specs=tuple(in_vmem(2)),
        scratch_shapes=[
            pltpu.VMEM((2, CH, nt, 2 * QW), BF16),
            pltpu.VMEM((3, CH, nt, 2 * QW), BF16),
            pltpu.VMEM((2, CH * half, 2 * QW), BF16),
            pltpu.VMEM((CH * half, 128), F32),
            pltpu.VMEM((nslot + 1, 8, 128), F32),
            pltpu.VMEM((nslot + 1, 8, 128), F32),
            pltpu.SemaphoreType.DMA((2, CH)),
            pltpu.SemaphoreType.DMA((3, CH)),
        ],
        compiler_params=pltpu.CompilerParams(vmem_limit_bytes=32 * 1024 * 1024),
        name="direct",
    )(plan, big, wk)
    with jax.named_scope("to_neighbour"):
        came = lax.ppermute(away, "ga", [(0, 1), (1, 0), (2, 3), (3, 2)])
    send = pl.pallas_call(
        route_kernel,
        out_shape=jax.ShapeDtypeStruct((n_ka, CAP + nk, 8, 128), F32),
        in_specs=[SMEM, ANY, ANY],
        out_specs=pl.BlockSpec(memory_space=pltpu.VMEM),
        scratch_shapes=[
            pltpu.VMEM((nslot, 8, 128), F32),
            pltpu.VMEM((nslot, 8, 128), F32),
            pltpu.SemaphoreType.DMA((2,)),
        ],
        compiler_params=pltpu.CompilerParams(vmem_limit_bytes=8 * 1024 * 1024),
        name="route",
    )(tab, keep, came)
    with jax.named_scope("to_holders"):
        got = lax.all_to_all(send, "ka", 0, 0, tiled=True)
    n = npair + nk
    mine = pl.pallas_call(
        collect_kernel,
        out_shape=jax.ShapeDtypeStruct((n, 8, 128), F32),
        in_specs=[SMEM, ANY],
        out_specs=pl.BlockSpec(memory_space=pltpu.VMEM),
        scratch_shapes=[pltpu.VMEM(send.shape, F32), pltpu.SemaphoreType.DMA],
        compiler_params=pltpu.CompilerParams(vmem_limit_bytes=8 * 1024 * 1024),
        name="collect",
    )(own, got)
    with jax.named_scope("direct_copies"):
        others = [lax.ppermute(mine, "ga", shift(r)) for r in range(1, 4)]
        place = jnp.stack([(a - r) % 4 for r in range(4)])
    dmat = pl.pallas_call(
        arrange_kernel,
        out_shape=jax.ShapeDtypeStruct((n, nt, nt), F32),
        in_specs=[SMEM, ANY, ANY, ANY, ANY],
        out_specs=pl.BlockSpec(memory_space=pltpu.VMEM),
        scratch_shapes=[pltpu.VMEM((4, n, 8, 128), F32), pltpu.SemaphoreType.DMA((4,))],
        compiler_params=pltpu.CompilerParams(vmem_limit_bytes=8 * 1024 * 1024),
        name="arrange",
    )(place, mine, *others)
    exch = pl.pallas_call(
        exchange_kernel,
        out_shape=jax.ShapeDtypeStruct((n, 8, 128), F32),
        in_specs=[SMEM, SMEM, ANY, ANY, *in_vmem(4)],
        out_specs=pl.BlockSpec(memory_space=pltpu.VMEM),
        scratch_shapes=[
            pltpu.VMEM((nslot, rows, 4 * QW), BF16),
            pltpu.VMEM((npair, rows, 4 * QW), BF16),
            pltpu.VMEM((nk, rows, 4 * QW), F32),
            pltpu.VMEM((nk, npair * rows, nt), F32),
            pltpu.VMEM((n * rows, nt), F32),
            pltpu.SemaphoreType.DMA((nslot,)),
            pltpu.SemaphoreType.DMA((npair,)),
        ],
        compiler_params=pltpu.CompilerParams(vmem_limit_bytes=50 * 1024 * 1024),
        name="exchange",
    )(firsts, own, p_big, others[2], full, w_hi, w_lo, c_full)
    with jax.named_scope("exchange_copies"):
        exch_others = [lax.ppermute(exch, "ga", shift(r)) for r in range(1, 4)]
    return pl.pallas_call(
        finish_kernel,
        out_shape=(
            jax.ShapeDtypeStruct((npair, nt * nt), F32),
            jax.ShapeDtypeStruct((nk, nt * nt), F32),
        ),
        in_specs=[SMEM, *in_vmem(2), ANY, ANY, ANY],
        out_specs=tuple(in_vmem(2)),
        scratch_shapes=[
            pltpu.VMEM((4, n, 8, 128), F32),
            pltpu.VMEM((n, nt, nt), F32),
            pltpu.VMEM((n, nt, nt), F32),
            pltpu.VMEM((n * half, 2 * nt), F32),
            pltpu.SemaphoreType.DMA((4,)),
        ],
        compiler_params=pltpu.CompilerParams(vmem_limit_bytes=16 * 1024 * 1024),
        name="finish",
    )(place, dmat, exch, *exch_others)


def solution(mesh):
    in_specs = (
        P("ka", None, "ga"),
        P("ka", None, "ga"),
        P("ka", None, "ga"),
        P("ga"),
        P("ka", "ga", None),
        P("ka", None),
        P(),
    )
    out_specs = (P("ka", None), P("ka", None))
    return jax.shard_map(
        per_device, mesh=mesh, in_specs=in_specs, out_specs=out_specs, check_vma=False
    )
```

```python
import jax
import jax.numpy as jnp
from jax import lax
from jax.experimental import pallas as pl
from jax.experimental.pallas import tpu as pltpu
from jax.sharding import PartitionSpec as P

CAP = 2
QW = 384
CH = 8
F32 = jnp.float32
BF16 = jnp.bfloat16
NT_DIMS = (((1,), (1,)), ((), ()))


def rank_in_group(owners):
    n = owners.shape[-1]
    same = owners[..., :, None] == owners[..., None, :]
    before = jnp.arange(n)[:, None] > jnp.arange(n)[None, :]
    return jnp.sum(jnp.logical_and(same, before).astype(jnp.int32), axis=-1)


def widen(v):
    return jnp.pad(v, ((0, 0),) * (v.ndim - 1) + ((0, QW - v.shape[-1]),))


def flat_tiles(tmp, rows):
    even = tmp[pl.ds(0, rows // 2, stride=2), :]
    odd = tmp[pl.ds(1, rows // 2, stride=2), :]
    return jnp.concatenate([even, odd], axis=1)


def direct_kernel(plan, big, w, keep, away, xs, ys, us, prod, kept, sent, sx, sy):
    half = prod.shape[0] // CH
    nt = 2 * half
    deep = xs.shape[3]
    nslot = keep.shape[0]
    chunks_first, chunks, parity = plan[3, 0], plan[3, 1], plan[3, 2]

    def x_copy(pos, buf, i):
        return pltpu.make_async_copy(big.at[plan[1, pos], pl.ds(0, nt)], xs.at[buf, i], sx.at[buf, i])

    def y_copy(pos, buf, i):
        return pltpu.make_async_copy(big.at[plan[2, pos], pl.ds(nt, nt)], ys.at[buf, i], sy.at[buf, i])

    def begin(c):
        for i in range(CH):
            x_copy(c * CH + i, lax.rem(c, 2), i).start()
            y_copy(c * CH + i, lax.rem(c, 3), i).start()

    def products(c):
        u = us[lax.rem(c + 2, 2)]
        y = ys[lax.rem(c + 3, 3)].reshape(CH * nt, deep)
        for i in range(0, CH, 4):
            d = lax.dot_general(
                u[half * i : half * (i + 4)],
                y[nt * i : nt * (i + 4)],
                NT_DIMS,
                preferred_element_type=F32,
            )
            for j in range(2):
                prod[half * i + nt * j : half * i + nt * j + nt] = d[
                    nt * j : nt * j + nt, 128 * j : 128 * j + 128
                ]
        lane = lax.broadcasted_iota(jnp.int32, (8, 128), 1)
        for i in range(CH):
            t = jnp.where(c < 0, nslot, plan[0, jnp.maximum(c, 0) * CH + i])
            rows = [prod[half * i + 8 * g : half * i + 8 * g + 8] for g in range(4)]
            tiles = []
            for h in range(2):
                start = nt * (i % 2) + half * h
                moved = [pltpu.roll(v, (half * g - start) % 128, 1) for g, v in enumerate(rows)]
                low = jnp.where(lane < half, moved[0], moved[1])
                high = jnp.where(lane < 3 * half, moved[2], moved[3])
                tiles.append(jnp.where(lane < nt, low, high))
            kept[t] = jnp.where(parity == 0, tiles[0], tiles[1])
            sent[t] = jnp.where(parity == 0, tiles[1], tiles[0])

    @pl.when(chunks > 0)
    def _():
        begin(0)

    def chunk(c, carry):
        @pl.when(c + 1 < chunks)
        def _():
            begin(c + 1)

        bx, by = lax.rem(c, 2), lax.rem(c, 3)
        for i in range(CH):
            x_copy(c * CH + i, bx, i).wait()
            y_copy(c * CH + i, by, i).wait()
        products(c - 1)
        slot = jnp.where(c < chunks_first, 0, 1)
        u = jnp.dot(
            xs[bx, :, :half].reshape(CH * half, deep), w[slot, :deep], preferred_element_type=F32
        )
        u = u + jnp.dot(
            xs[bx, :, half:].reshape(CH * half, deep), w[slot, deep:], preferred_element_type=F32
        )
        us[bx] = u.astype(BF16)
        return carry

    lax.fori_loop(0, chunks, chunk, 0)

    @pl.when(chunks > 0)
    def _():
        products(chunks - 1)

    keep[...] = kept[:nslot]
    away[...] = sent[:nslot]


def route_kernel(tab, keep, came, send, mine, theirs, sem):
    copies = [
        pltpu.make_async_copy(keep, mine, sem.at[0]),
        pltpu.make_async_copy(came, theirs, sem.at[1]),
    ]
    for c in copies:
        c.start()
    nk = send.shape[1] - CAP
    send[:, CAP:] = jnp.zeros((send.shape[0], nk, *send.shape[2:]), F32)
    for c in copies:
        c.wait()
    for t in range(tab.shape[1]):
        v = mine[t] + theirs[t]
        send[t // CAP, t % CAP] = v

        @pl.when(tab[0, t] == 1)
        def _():
            owner = tab[2, t] // nk
            row = CAP + tab[2, t] % nk
            send[owner, row] = send[owner, row] + v


def exchange_kernel(
    firsts, own, big, early, full, whi, wlo, cw, out, p1, p2, tot, prod, flat, s1, s2
):
    count = firsts[2, 0]
    npair = own.shape[1]
    nk, rows, wide = tot.shape
    nt = whi.shape[0] // nk

    def second(j):
        return pltpu.make_async_copy(big.at[own[1, j]], p2.at[j], s2.at[j])

    def first(t):
        return pltpu.make_async_copy(big.at[firsts[0, t]], p1.at[t], s1.at[t])

    for j in range(npair):
        second(j).start()

    def begin(t, carry):
        first(t).start()
        return carry

    lax.fori_loop(0, count, begin, 0)
    tot[...] = jnp.zeros_like(tot)
    def gather(t, carry):
        first(t).wait()
        k = firsts[1, t]
        tot[k] = tot[k] + p1[t].astype(F32)
        return carry

    lax.fori_loop(0, count, gather, 0)
    for j in range(npair):
        second(j).wait()

    def contract(left, right):
        return lax.dot_general(left, right, NT_DIMS, preferred_element_type=F32)

    b = p2[...].reshape(npair * rows, wide)
    e = contract(b, whi[...]) + contract(b, wlo[...])
    e = e + e
    for k in range(nk):
        prod[k] = e[:, k * nt : (k + 1) * nt]
    for j in range(npair):
        r = pl.ds(j * rows, rows)
        flat[r, :] = prod[own[0, j], r, :]

    w = tot[...].reshape(nk * rows, wide) * cw[...]
    hi = w.astype(BF16)
    lo = (w - hi.astype(F32)).astype(BF16)
    m = contract(jnp.concatenate([hi, lo], axis=0), full[: nk * nt])
    m = m[: nk * rows] + m[nk * rows :]
    m = m + m
    for k in range(nk):
        flat[pl.ds((npair + k) * rows, rows), :] = m[
            k * rows : (k + 1) * rows, k * nt : (k + 1) * nt
        ]
    z = flat_tiles(flat, (npair + nk) * rows)
    for j in range(npair + nk):
        out[j] = z[8 * j : 8 * j + 8]


def collect_kernel(own, got, out, here, sem):
    copy = pltpu.make_async_copy(got, here, sem)
    copy.start()
    copy.wait()
    nk = got.shape[1] - CAP
    npair = own.shape[1]
    for j in range(npair):
        out[j] = here[own[2, j], own[3, j]]
    for k in range(nk):
        out[npair + k] = jnp.sum(here[:, CAP + k], axis=0)


def bring(place, refs, whole, sem):
    copies = [
        pltpu.make_async_copy(r, whole.at[place[i]], sem.at[i]) for i, r in enumerate(refs)
    ]
    for c in copies:
        c.start()
    for c in copies:
        c.wait()


def arrange_kernel(place, r0, r1, r2, r3, dmat, whole, sem):
    bring(place, (r0, r1, r2, r3), whole, sem)
    half = dmat.shape[1] // 2
    for j in range(dmat.shape[0]):
        for a in range(2):
            left, right = whole[2 * a, j], whole[2 * a + 1, j]
            for g in range(4):
                cut = slice(half * g, half * (g + 1))
                dmat[j, pl.ds(half * a + 8 * g, 8), :] = jnp.concatenate(
                    [left[:, cut], right[:, cut]], axis=1
                )


def finish_kernel(place, dmat, r0, r1, r2, r3, blocks, mirrored, emat, bmat, rows):
    npair, nk = blocks.shape[0], mirrored.shape[0]
    nt = dmat.shape[1]
    half = nt // 2
    n = npair + nk
    for i, r in enumerate((r0, r1, r2, r3)):
        top = pl.multiple_of(16 * place[i], 16)
        for j in range(n):
            tile = r[j]
            emat[j, pl.ds(top, 8, stride=2), :] = tile[:, :nt]
            emat[j, pl.ds(top + 1, 8, stride=2), :] = tile[:, nt:]
    for j in range(n):
        if j < npair:
            bmat[j] = emat[j].T - dmat[j]
        else:
            bmat[j] = (emat[j] - dmat[j]).T
        even = bmat[j, pl.ds(0, half, stride=2), :]
        odd = bmat[j, pl.ds(1, half, stride=2), :]
        rows[pl.ds(j * half, half), :] = jnp.concatenate([even, odd], axis=1)
    for r in range(half):
        lanes = pl.ds(2 * nt * r, 2 * nt)
        blocks[:, lanes] = rows[pl.ds(r, npair, stride=half), :]
        mirrored[:, lanes] = rows[pl.ds(npair * half + r, nk, stride=half), :]


def in_vmem(count):
    return [pl.BlockSpec(memory_space=pltpu.VMEM)] * count


SMEM = pl.BlockSpec(memory_space=pltpu.SMEM)
ANY = pl.BlockSpec(memory_space=pl.ANY)


def per_device(x, y, p, coulomb, w, pairs, q_slot):
    n_ka = lax.axis_size("ka")
    me = lax.axis_index("ka")
    a = lax.axis_index("ga")
    nk, nt, gl = x.shape
    qs = w.shape[0]
    npair = pairs.shape[0]
    nslot = n_ka * CAP

    half, rows = nt // 2, nt // 4

    def shift(r):
        return [(i, (i + r) % 4) for i in range(4)]

    with jax.named_scope("pack"):
        y_far = lax.ppermute(y, "ga", [(i, 3 - i) for i in range(4)])
        cut = [jnp.where((a + r) % 4 < 2, x[:, :half], x[:, half:]) for r in range(4)]
        cut = cut[:1] + [lax.ppermute(cut[r], "ga", shift(r)) for r in range(1, 4)]

        def side(left, right):
            return jnp.concatenate([widen(left), widen(right)], axis=2)

        y_both = side(jnp.where(a < 2, y, y_far), jnp.where(a < 2, y_far, y))
        payload = jnp.concatenate([side(cut[0], cut[1]), side(cut[2], cut[3]), y_both], axis=1)
    with jax.named_scope("spread"):
        big = lax.all_gather(payload, "ka", axis=0, tiled=True)

    with jax.named_scope("weights"):
        cols = [
            jnp.pad(w[:, :, i * gl : (i + 1) * gl], ((0, 0), (0, QW - gl), (0, QW - gl)))
            for i in range(4)
        ]
        outer = jnp.concatenate([cols[0], cols[3]], axis=2)
        inner = jnp.concatenate([cols[1], cols[2]], axis=2)
        wk = []
        for r in range(4):
            to = (a + r) % 4
            v = jnp.where((to == 0) | (to == 3), outer, inner)
            wk.append(lax.ppermute(v, "ga", shift(r)) if r else v)
        wk = jnp.concatenate(wk, axis=1)

    with jax.named_scope("exchange_pack"):
        c1 = lax.reduce_precision(coulomb, 8, 7)
        c2 = lax.reduce_precision(coulomb - c1, 8, 7)
        c3 = coulomb - c1 - c2
        pieces = jnp.pad(jnp.stack([c1, c2, c3]).astype(BF16), ((0, 13), (0, 0)))
        held = jnp.concatenate([p.reshape(nk * nt, gl), pieces], axis=0)
        full = lax.all_gather(widen(held), "ga", axis=1, tiled=True)
        p_rows = full[: nk * nt].reshape(nk, nt, 4 * QW)
        p_rows = lax.dynamic_slice_in_dim(p_rows, a * rows, rows, axis=1)
        p_big = lax.all_gather(p_rows, "ka", axis=0, tiled=True)
        c_full = jnp.sum(full[nk * nt : nk * nt + 3].astype(F32), axis=0, keepdims=True)
        weighted = full[: nk * nt].astype(F32) * c_full
        w_hi = lax.reduce_precision(weighted, 8, 7)
        w_lo = (weighted - w_hi).astype(BF16)
        w_hi = w_hi.astype(BF16)

    with jax.named_scope("tables"):
        every = lax.all_gather(pairs, "ka", axis=0, tiled=True).reshape(n_ka, npair, 3)

        def routes(rows):
            slot = jnp.sum(
                jnp.where(
                    rows[..., 2, None] == jnp.arange(q_slot.shape[0]), q_slot, 0
                ),
                axis=-1,
            )
            q_owner = slot // qs
            k_owner = rows[..., 1] // nk
            return slot % qs, q_owner, rank_in_group(q_owner), k_owner, rank_in_group(k_owner)

        local, q_owner, q_rank, k_owner, k_rank = routes(every)
        ranks = jnp.arange(CAP)
        hot_q = (q_owner == me)[..., None] & (q_rank[..., None] == ranks)
        hot_k = (k_owner == me)[..., None] & (k_rank[..., None] == ranks)

        def pick(hot, v):
            return jnp.sum(jnp.where(hot, v[..., None], 0), axis=1).reshape(nslot)

        ones = jnp.ones_like(local)
        tab = jnp.stack(
            [
                pick(hot_q, ones),
                pick(hot_q, every[..., 0]),
                pick(hot_q, every[..., 1]),
                pick(hot_q, local),
                pick(hot_k, ones),
                pick(hot_k, every[..., 1] - me * nk),
                pick(hot_k, every[..., 0]),
            ]
        )
        _, o1, r1, _, _ = routes(pairs)
        own = jnp.stack([pairs[:, 0] - me * nk, pairs[:, 1], o1, r1])

    with jax.named_scope("plan"):
        npos = nslot + qs * CH
        used, slot = tab[0], tab[3]
        same = (slot[:, None] == slot[None, :]) & (used[None, :] == 1)
        order = jnp.arange(nslot)
        rank = jnp.sum((same & (order[:, None] > order[None, :])).astype(jnp.int32), axis=1)
        first = jnp.sum(used * (slot == 0))
        second = jnp.sum(used * (slot == 1))
        chunks_first = (first + CH - 1) // CH
        chunks = chunks_first + (second + CH - 1) // CH
        pos = jnp.where(slot == 0, rank, chunks_first * CH + rank)
        hot = (pos[None, :] == jnp.arange(npos)[:, None]) & (used == 1)[None, :]

        def at_pos(v, hot):
            return jnp.sum(jnp.where(hot, v[None, :], 0), axis=1)

        heads = jnp.pad(jnp.stack([chunks_first, chunks, a % 2]), (0, npos - 3))
        plan = jnp.stack(
            [at_pos(order - nslot, hot) + nslot, at_pos(tab[1], hot), at_pos(tab[2], hot), heads]
        )
        named = tab[4]
        rank = jnp.sum(jnp.where(order[:, None] > order[None, :], named[None, :], 0), axis=1)
        hot = (rank[None, :] == order[:, None]) & (named == 1)[None, :]
        total = jnp.broadcast_to(jnp.sum(named), (nslot,))
        firsts = jnp.stack([at_pos(tab[6], hot), at_pos(tab[5], hot), total])
    keep, away = pl.pallas_call(
        direct_kernel,
        out_shape=(jax.ShapeDtypeStruct((nslot, 8, 128), F32),) * 2,
        in_specs=[SMEM, ANY, *in_vmem(1)],
        out_specs=tuple(in_vmem(2)),
        scratch_shapes=[
            pltpu.VMEM((2, CH, nt, 2 * QW), BF16),
            pltpu.VMEM((3, CH, nt, 2 * QW), BF16),
            pltpu.VMEM((2, CH * half, 2 * QW), BF16),
            pltpu.VMEM((CH * half, 128), F32),
            pltpu.VMEM((nslot + 1, 8, 128), F32),
            pltpu.VMEM((nslot + 1, 8, 128), F32),
            pltpu.SemaphoreType.DMA((2, CH)),
            pltpu.SemaphoreType.DMA((3, CH)),
        ],
        compiler_params=pltpu.CompilerParams(vmem_limit_bytes=32 * 1024 * 1024),
        name="direct",
    )(plan, big, wk)
    with jax.named_scope("to_neighbour"):
        came = lax.ppermute(away, "ga", [(0, 1), (1, 0), (2, 3), (3, 2)])
    send = pl.pallas_call(
        route_kernel,
        out_shape=jax.ShapeDtypeStruct((n_ka, CAP + nk, 8, 128), F32),
        in_specs=[SMEM, ANY, ANY],
        out_specs=pl.BlockSpec(memory_space=pltpu.VMEM),
        scratch_shapes=[
            pltpu.VMEM((nslot, 8, 128), F32),
            pltpu.VMEM((nslot, 8, 128), F32),
            pltpu.SemaphoreType.DMA((2,)),
        ],
        compiler_params=pltpu.CompilerParams(vmem_limit_bytes=8 * 1024 * 1024),
        name="route",
    )(tab, keep, came)
    with jax.named_scope("to_holders"):
        got = lax.all_to_all(send, "ka", 0, 0, tiled=True)
    n = npair + nk
    mine = pl.pallas_call(
        collect_kernel,
        out_shape=jax.ShapeDtypeStruct((n, 8, 128), F32),
        in_specs=[SMEM, ANY],
        out_specs=pl.BlockSpec(memory_space=pltpu.VMEM),
        scratch_shapes=[pltpu.VMEM(send.shape, F32), pltpu.SemaphoreType.DMA],
        compiler_params=pltpu.CompilerParams(vmem_limit_bytes=8 * 1024 * 1024),
        name="collect",
    )(own, got)
    with jax.named_scope("direct_copies"):
        others = [lax.ppermute(mine, "ga", shift(r)) for r in range(1, 4)]
        place = jnp.stack([(a - r) % 4 for r in range(4)])
    dmat = pl.pallas_call(
        arrange_kernel,
        out_shape=jax.ShapeDtypeStruct((n, nt, nt), F32),
        in_specs=[SMEM, ANY, ANY, ANY, ANY],
        out_specs=pl.BlockSpec(memory_space=pltpu.VMEM),
        scratch_shapes=[pltpu.VMEM((4, n, 8, 128), F32), pltpu.SemaphoreType.DMA((4,))],
        compiler_params=pltpu.CompilerParams(vmem_limit_bytes=8 * 1024 * 1024),
        name="arrange",
    )(place, mine, *others)
    exch = pl.pallas_call(
        exchange_kernel,
        out_shape=jax.ShapeDtypeStruct((n, 8, 128), F32),
        in_specs=[SMEM, SMEM, ANY, ANY, *in_vmem(4)],
        out_specs=pl.BlockSpec(memory_space=pltpu.VMEM),
        scratch_shapes=[
            pltpu.VMEM((nslot, rows, 4 * QW), BF16),
            pltpu.VMEM((npair, rows, 4 * QW), BF16),
            pltpu.VMEM((nk, rows, 4 * QW), F32),
            pltpu.VMEM((nk, npair * rows, nt), F32),
            pltpu.VMEM((n * rows, nt), F32),
            pltpu.SemaphoreType.DMA((nslot,)),
            pltpu.SemaphoreType.DMA((npair,)),
        ],
        compiler_params=pltpu.CompilerParams(vmem_limit_bytes=50 * 1024 * 1024),
        name="exchange",
    )(firsts, own, p_big, others[2], full, w_hi, w_lo, c_full)
    with jax.named_scope("exchange_copies"):
        exch_others = [lax.ppermute(exch, "ga", shift(r)) for r in range(1, 4)]
    return pl.pallas_call(
        finish_kernel,
        out_shape=(
            jax.ShapeDtypeStruct((npair, nt * nt), F32),
            jax.ShapeDtypeStruct((nk, nt * nt), F32),
        ),
        in_specs=[SMEM, *in_vmem(5)],
        out_specs=tuple(in_vmem(2)),
        scratch_shapes=[
            pltpu.VMEM((n, nt, nt), F32),
            pltpu.VMEM((n, nt, nt), F32),
            pltpu.VMEM((n * half, 2 * nt), F32),
        ],
        compiler_params=pltpu.CompilerParams(vmem_limit_bytes=16 * 1024 * 1024),
        name="finish",
    )(place, dmat, exch, *exch_others)


def solution(mesh):
    in_specs = (
        P("ka", None, "ga"),
        P("ka", None, "ga"),
        P("ka", None, "ga"),
        P("ga"),
        P("ka", "ga", None),
        P("ka", None),
        P(),
    )
    out_specs = (P("ka", None), P("ka", None))
    return jax.shard_map(
        per_device, mesh=mesh, in_specs=in_specs, out_specs=out_specs, check_vma=False
    )
```
